32 devices in a mesh: frame: 4 (over x, core), within: 8 (over z, y).
Axes of the slice: x: 2, y: 2, z: 4, core: 2. Of those that a mesh axis runs over, the one named last changes fastest.
Arguments:
- queries: bfloat16 [4, 576, 1024], P('frame', 'within'), may hold values from -6 to 6
- keys_in: bfloat16 [4, 576, 1024], P('frame', 'within'), may hold values from -6 to 6
- values_in: bfloat16 [4, 576, 1024], P('frame', 'within'), may hold values from -6 to 6
- grad_out: bfloat16 [4, 576, 1024], P('frame', 'within'), may hold values from -6 to 6
- partners: int32 [4, 2], replicated, may hold values from 0 to 3
- registers: int32 [4], replicated, may hold values from 1 to 144
Outputs:
- grad_queries: bfloat16 [4, 576, 1024], P('frame', 'within')
- grad_keys: bfloat16 [4, 576, 1024], P('frame', 'within')
- grad_values: bfloat16 [4, 576, 1024], P('frame', 'within')
The draws below stay inside these ranges and needn't reach their ends.
Inputs may be any that keep to these rules, and one draw needn't show every extreme that they name: `partners`: A row may list a group more than once, and may list its own group.
All inputs are finite; a program needn't handle non-finite values.
Results may differ from the reference program's by a relative error of at most 0.012.
Values may be sent and summed in bfloat16 or wider, within the bound.
A program may use at most 128 MiB of HBM per device.

```python
import math
import jax
import jax.numpy as jnp
import numpy as np
from jax import lax

HEADS = 16
DH = 64
D = 1024
PART = 2
G = 4
S = 576


def draw_queries(key, part):
    base = jnp.clip(jax.random.normal(jax.random.fold_in(key, 1), (G, S, D), jnp.float32), -6.0, 6.0)
    return base.astype(jnp.bfloat16)


def draw_keys_in(key, part):
    base = jnp.clip(jax.random.normal(jax.random.fold_in(key, 2), (G, S, D), jnp.float32), -6.0, 6.0)
    return base.astype(jnp.bfloat16)


def set_ends(entries, own_key, least, top_value):
    shape = entries.shape
    place = [jax.random.randint(jax.random.fold_in(own_key, axis), (), 0, shape[axis]) for axis in range(len(shape))]
    entries = entries.at[tuple(place)].set(least)
    longest = shape.index(max(shape))
    place[longest] = (place[longest] + 1) % shape[longest]
    return entries.at[tuple(place)].set(top_value)


def block_scale(own_key, shape, pieces, low, high):
    def one(position, shards_of):
        steps = jax.random.uniform(jax.random.fold_in(jax.random.fold_in(own_key, 6), position), (shards_of,), jnp.float32, low / len(pieces), high / len(pieces))
        return jnp.repeat(jnp.exp(steps), shape[position] // shards_of).reshape((-1,) + (1,) * (len(shape) - position - 1))

    factor_of = one(*pieces[0])
    for cut in pieces[1:]:
        factor_of = factor_of * one(*cut)
    return factor_of


def cumulative_ranks(amount, slope):
    portions = [(1 << 20) // math.isqrt(rank ** slope) + 1 for rank in range(1, amount + 1)]
    scale = 1 + sum(portions) // (1 << 30)
    return np.cumsum(np.array([max(1, weight // scale) for weight in portions]))


def ranked_ids(stream_key, shape, count, skew):
    table = cumulative_ranks(count, skew)
    pick = jax.random.randint(jax.random.fold_in(stream_key, 1), shape, 0, int(table[count - 1]))
    rank = jnp.searchsorted(jnp.asarray(table, jnp.int32), pick, side="right")
    return jax.random.permutation(jax.random.fold_in(stream_key, 2), count)[rank].astype(jnp.int32)


def normal_values(stream_key, dims, spread, bound, pieces=(), held_as=jnp.bfloat16):
    gain = block_scale(stream_key, dims, pieces, -0.22, 0.18) if pieces else 1.0
    drawn = jax.random.normal(stream_key, dims, jnp.float32) * spread * gain
    return jnp.minimum(jnp.maximum(drawn, -bound), bound).astype(held_as)


def setup_inputs(seed: int = 0) -> dict:
    arg_keys = jax.random.split(jax.random.key(seed), 7)
    queries = draw_queries(jax.random.fold_in(arg_keys[6], 71), 0)
    keys_in = draw_keys_in(jax.random.fold_in(arg_keys[6], 71), 0)
    values_in = normal_values(arg_keys[2], (G, S, D), 1.0, 6.0, ((0, 4), (1, 8)))
    grad_out = normal_values(arg_keys[3], (G, S, D), 1.0, 6.0, ((0, 4), (1, 8)))
    partners = set_ends(ranked_ids(arg_keys[4], (G, PART), G, 2), jax.random.fold_in(arg_keys[4], 3), 0, G - 1).astype(jnp.int32)
    registers = set_ends(jax.random.randint(arg_keys[5], (G,), 1, S // 4 + 1), jax.random.fold_in(arg_keys[5], 1), 1, (S // 4 + 1) - 1).astype(jnp.int32)
    return dict(queries=queries, keys_in=keys_in, values_in=values_in, grad_out=grad_out, partners=partners, registers=registers)


def reference(queries, keys_in, values_in, grad_out, partners, registers):
    groups, seq, width = queries.shape
    scale = DH ** -0.5
    positions = jnp.arange(seq).astype(jnp.int32)

    def head_split(block):
        return block.reshape(block.shape[0], HEADS, DH).transpose(1, 0, 2)

    def one_head(operands):
        qh, kh, vh, dh, visible = operands
        raw = jnp.dot(qh, kh.T, preferred_element_type=jnp.float32) * scale
        raw = jnp.where(visible[None, :], raw, -1e30)
        top = jnp.max(raw, axis=1, keepdims=True)
        expo = jnp.exp(raw - top)
        prob = expo / jnp.sum(expo, axis=1, keepdims=True)
        dprod = jnp.dot(dh, vh.T, preferred_element_type=jnp.float32)
        delta = jnp.sum(prob * dprod, axis=1, keepdims=True)
        dscore = prob * (dprod - delta)
        prob_low = prob.astype(jnp.bfloat16)
        dscore_low = dscore.astype(jnp.bfloat16)
        dq = jnp.dot(dscore_low, kh, preferred_element_type=jnp.float32) * scale
        dk = jnp.dot(dscore_low.T, qh, preferred_element_type=jnp.float32) * scale
        dv = jnp.dot(prob_low.T, dh, preferred_element_type=jnp.float32)
        return dq, dk, dv

    def one_group(carry, index):
        dk_all, dv_all = carry
        listed = jnp.concatenate([index[None].astype(jnp.int32), partners[index].astype(jnp.int32)])
        keys_list = keys_in[listed].reshape(-1, width)
        values_list = values_in[listed].reshape(-1, width)
        hidden_regs = positions[None, :] >= registers[partners[index]][:, None]
        visible = jnp.concatenate([jnp.ones((seq,), dtype=bool), hidden_regs.reshape(-1)])
        visible_all = jnp.broadcast_to(visible[None, :], (HEADS, visible.shape[0]))
        dq, dk, dv = lax.map(one_head, (head_split(queries[index]), head_split(keys_list),
                                        head_split(values_list), head_split(grad_out[index]), visible_all))
        dq = dq.transpose(1, 0, 2).reshape(seq, width)
        dk = dk.transpose(1, 0, 2).reshape(PART + 1, seq, width)
        dv = dv.transpose(1, 0, 2).reshape(PART + 1, seq, width)
        dk_all = dk_all.at[listed].add(dk)
        dv_all = dv_all.at[listed].add(dv)
        return (dk_all, dv_all), dq.astype(jnp.bfloat16)

    start = (jnp.zeros((groups, seq, width), jnp.float32), jnp.zeros((groups, seq, width), jnp.float32))
    (dk_all, dv_all), grad_queries = lax.scan(one_group, start, jnp.arange(groups).astype(jnp.int32))
    return grad_queries, dk_all.astype(jnp.bfloat16), dv_all.astype(jnp.bfloat16)
```

```python
import functools
import math

import jax
import jax.numpy as jnp
import numpy as np
from jax import lax
from jax.experimental import pallas as pl
from jax.experimental.pallas import tpu as pltpu
from jax.sharding import PartitionSpec as P

DH = 64
PAIR = 2 * DH
SPLITS = 3
UNIT = 640
HIDDEN = -1e30
BF = jnp.bfloat16
F32 = jnp.float32
MESH = pl.DeviceIdType.MESH


def pieces_of(value):
    left, out = float(value), []
    for _ in range(SPLITS):
        part = float(np.asarray(left, dtype=jnp.bfloat16))
        out.append(part)
        left = left - part if abs(value) < 1e20 else 0.0
    return out


def rdot(a, b):
    return lax.dot_general(a, b, (((1,), (1,)), ((), ())), preferred_element_type=F32)


def dot(a, b):
    return jnp.dot(a, b, preferred_element_type=F32)


def each(lo, hi, do):
    def step(t, carry):
        do(t)
        return carry
    lax.fori_loop(lo, hi, step, 0)


def kernel(F, W, R, QC, inline, part_ref, reg_ref, q_ref, k_ref, v_ref, d_ref, dq_in, fin_in,
           kv_send, qd_send, kv_in, qd_in, kaug, vz, kt, qaug, xraw, qdz, sbuf, dpbuf, acc, dqacc, dqs,
           tops, top_ref, total_ref, dsum_ref,
           red_send, red_in, fin_send, dq_send, own_sem,
           kv_ss, fw_ss, kv_rs, qd_ss, qd_rs, red_ss, red_rs, fin_ss, fin_rs, dq_ss, dq_rs):
    fs = F // R
    hf = F // 2
    rows = q_ref.shape[1]
    width = q_ref.shape[2]
    seq = rows * W
    n_slots = part_ref.shape[0]
    scale = DH ** -0.5
    half = dq_send.shape[2]
    nq = R * seq
    n_chunks = nq // QC
    n_units, per = acc.shape[0], acc.shape[1]
    unit = per * F * rows
    f = lax.axis_index("frame")
    w = lax.axis_index("within")
    c = lax.rem(f, fs)
    a0 = lax.div(f, fs)
    sib = f + 1 - 2 * lax.rem(f, 2)
    head = w * R + a0

    barrier = pltpu.get_barrier_semaphore()

    def ahead(dw):
        return lax.rem(w + W - dw, W)

    def behind(dw):
        return lax.rem(w + dw, W)

    def greet(t):
        pl.semaphore_signal(barrier, inc=1, device_id=(lax.rem(f + 2 * lax.rem(t, hf), F), ahead(lax.div(t, hf))),
                            device_id_type=MESH)

    each(1, hf * W, greet)
    for dc in range(1, fs, 2):
        pl.semaphore_signal(barrier, inc=1, device_id=(a0 * fs + lax.rem(c + dc, fs), w), device_id_type=MESH)

    for first, second, out in ((q_ref, d_ref, qd_send), (k_ref, v_ref, kv_send)):
        for j in range(width // PAIR):
            cols = slice(j * PAIR, (j + 1) * PAIR)
            one = first[0, :, cols]
            two = second[0, :, cols]
            out[2 * j] = jnp.concatenate([one[:, :DH], two[:, :DH]], axis=1)
            out[2 * j + 1] = jnp.concatenate([one[:, DH:], two[:, DH:]], axis=1)
    kv_in[f, w] = kv_send[head]
    qd_in[a0, w] = qd_send[head]

    pl.semaphore_wait(barrier, hf * W - 1 + fs // 2)

    def kv_copy(t):
        ff = lax.rem(f + 2 * lax.rem(t, hf), F)
        ww = ahead(lax.div(t, hf))
        return pltpu.make_async_remote_copy(
            src_ref=kv_send.at[ww * R + lax.div(ff, fs)], dst_ref=kv_in.at[f, w],
            send_sem=kv_ss.at[t], recv_sem=kv_rs.at[f * W + w],
            device_id=(ff, ww), device_id_type=MESH)

    def pass_on(origin, t):
        ff = lax.rem(origin + F - 2 * lax.rem(t, hf), F)
        ww = behind(lax.div(t, hf))
        return pltpu.make_async_remote_copy(
            src_ref=kv_in.at[ff, ww], dst_ref=kv_in.at[ff, ww],
            send_sem=fw_ss.at[t], recv_sem=kv_rs.at[ff * W + ww],
            device_id=(sib, w), device_id_type=MESH)

    def qd_copy(t):
        aa, ww = lax.rem(a0 + lax.rem(t, R), R), ahead(lax.div(t, R))
        return pltpu.make_async_remote_copy(
            src_ref=qd_send.at[ww * R + aa], dst_ref=qd_in.at[a0, w],
            send_sem=qd_ss.at[t], recv_sem=qd_rs.at[a0 * W + w],
            device_id=(aa * fs + c, ww), device_id_type=MESH)

    def arrival(t, buffer, send, recv, index, source):
        return pltpu.make_async_remote_copy(
            src_ref=buffer.at[index], dst_ref=buffer.at[index], send_sem=send.at[t], recv_sem=recv,
            device_id=source, device_id_type=MESH)

    def qd_arrival(t):
        aa, ww = lax.rem(a0 + R - lax.rem(t, R), R), behind(lax.div(t, R))
        return arrival(t, qd_in, qd_ss, qd_rs.at[aa * W + ww], (aa, ww), (aa * fs + c, ww))

    def head_arrival(t, buffer, send, recv):
        aa, ww = lax.rem(a0 + R - lax.rem(t, R), R), ahead(lax.div(t, R))
        return arrival(t, buffer, send, recv.at[ww * R + aa], (ww * R + aa,), (aa * fs + c, ww))

    each(1, R * W, lambda t: qd_copy(t).start())
    pass_on(f, 0).start()
    each(1, hf * W, lambda t: kv_copy(t).start())

    acc[...] = jnp.zeros_like(acc)
    dqacc[...] = jnp.zeros_like(dqacc)

    def relay(t):
        move = pass_on(f, t)
        move.wait_recv()
        move.start()

    lane1 = lax.broadcasted_iota(jnp.int32, (1, PAIR), 1)
    table = [pieces_of(HIDDEN)] + [pieces_of(math.log(n)) for n in range(1, n_slots + 2)]
    marks = []
    for p in range(F):
        seen = jnp.zeros((1, PAIR), F32)
        unseen = jnp.zeros((1, PAIR), F32)
        for gi in range(R):
            g = c + fs * gi
            own = jnp.where(p == g, 1, 0)
            count = own
            for slot in range(n_slots):
                count = count + jnp.where(part_ref[slot, g] == p, 1, 0)
            for e in range(SPLITS):
                here = lane1 == DH + SPLITS * gi + e
                for n in range(n_slots + 2):
                    if n < 2:
                        unseen = jnp.where(here & (own == n), table[n][e], unseen)
                    seen = jnp.where(here & (count == n), table[n][e], seen)
        marks.append((seen, unseen))

    lane = lax.broadcasted_iota(jnp.int32, (rows, PAIR), 1)
    row = lax.broadcasted_iota(jnp.int32, (rows, PAIR), 0)

    def prepare(u):
        aug, raw = [], []
        for d in range(per):
            ww = behind(u * per + d)
            for p in range(F):
                both = kv_in[p, ww].astype(F32)
                extra = jnp.where(row + ww * rows >= reg_ref[p], marks[p][0], marks[p][1])
                raw.append(both)
                aug.append(jnp.where(lane < DH, both, extra))
        raw = jnp.concatenate(raw, axis=0)
        keep = lax.broadcasted_iota(jnp.int32, (unit, PAIR), 1) >= DH
        kaug[u] = jnp.concatenate(aug, axis=0).astype(BF)
        vz[u] = jnp.where(keep, raw, 0.0).astype(BF)
        kt[u] = (raw * scale).T[:DH].astype(BF)

    def direct(u):
        each(max(u * per * hf, 1), (u + 1) * per * hf, relay)

    def settle(u):
        each(u * per * hf, (u + 1) * per * hf, lambda t: pass_on(sib, t).wait_recv())
        prepare(u)

    def rows_of(i):
        return pl.ds(pl.multiple_of(i * QC, QC), QC)

    def begin(b):
        top_ref[b] = jnp.full_like(top_ref[b], -3e38)
        total_ref[b] = jnp.zeros_like(total_ref[b])
        dsum_ref[b] = jnp.zeros_like(dsum_ref[b])

    def forth(u, i, b):
        at = rows_of(i)
        raw = rdot(kaug[u], qaug[at])
        old = top_ref[b]
        top = jnp.maximum(old, jnp.max(raw, axis=0, keepdims=True))
        keep = jnp.exp(old - top)
        expo = jnp.exp(raw - top)
        dprod = rdot(vz[u], xraw[at])
        sbuf[u, b] = expo
        dpbuf[u, b] = dprod
        tops[u, b] = top
        top_ref[b] = top
        total_ref[b] = total_ref[b] * keep + jnp.sum(expo, axis=0, keepdims=True)
        dsum_ref[b] = dsum_ref[b] * keep + jnp.sum(expo * dprod, axis=0, keepdims=True)

    def back(u, i, b):
        inv = 1.0 / total_ref[b]
        factor = jnp.exp(tops[u, b] - top_ref[b]) * inv
        prob = sbuf[u, b] * factor
        dscore = (prob * (dpbuf[u, b] - dsum_ref[b] * inv)).astype(BF)
        added = dot(jnp.concatenate([dscore, prob.astype(BF)], axis=1), qdz[i])
        acc[u] += added.reshape(per, F, rows, PAIR)
        dqacc[i] += dot(kt[u], dscore)

    def own_copy(block, buffer, n):
        return pltpu.make_async_copy(block, buffer.at[head], own_sem.at[n])

    def red_copy(u, dc):
        return pltpu.make_async_remote_copy(
            src_ref=red_send.at[u, dc - 1], dst_ref=red_in.at[u, dc - 1],
            send_sem=red_ss.at[u * (fs - 1) + dc - 1], recv_sem=red_rs.at[u * (fs - 1) + dc - 1],
            device_id=(a0 * fs + lax.rem(c + dc, fs), w), device_id_type=MESH)

    def ship_part(u):
        for dc in range(1, fs):
            for gi in range(R):
                red_send[u, dc - 1, gi] = acc[u, :, lax.rem(c + dc, fs) + fs * gi].astype(BF)
            red_copy(u, dc).start()

    def fin_copy(t):
        dw = lax.div(t, R)
        aa, ww = lax.rem(a0 + lax.rem(t, R), R), behind(dw)
        return pltpu.make_async_remote_copy(
            src_ref=fin_send.at[lax.div(dw, per), aa, lax.rem(dw, per)], dst_ref=fin_in.at[head],
            send_sem=fin_ss.at[t], recv_sem=fin_rs.at[head],
            device_id=(aa * fs + c, ww), device_id_type=MESH)

    def ship_home(u):
        for dc in range(1, fs):
            red_copy(u, dc).wait_recv()
        for gi in range(R):
            whole = acc[u, :, c + fs * gi]
            for dc in range(1, fs):
                whole = whole + red_in[u, dc - 1, gi].astype(F32)
            fin_send[u, gi] = whole.astype(BF)
        if u == 0:
            own_copy(fin_send.at[0, a0, 0], fin_in, 0).start()
        each(max(u * per * R, 1), (u + 1) * per * R, lambda t: fin_copy(t).start())

    def take_queries():
        each(1, R * W, lambda t: qd_arrival(t).wait_recv())
        wide = lax.broadcasted_iota(jnp.int32, (nq, PAIR), 1)
        tall = lax.broadcasted_iota(jnp.int32, (nq, PAIR), 0)
        both = qd_in[...].astype(F32).reshape(nq, PAIR)
        mark = jnp.zeros((nq, PAIR), F32)
        for gi in range(R):
            mine = (tall >= gi * seq) & (tall < (gi + 1) * seq)
            mark = jnp.where(mine & (wide >= DH + SPLITS * gi) & (wide < DH + SPLITS * (gi + 1)), 1.0, mark)
        scaled = both * scale
        qaug[...] = jnp.where(wide < DH, scaled, mark).astype(BF)
        xraw[...] = both.astype(BF)
        qdz[:, :QC] = jnp.where(wide < DH, scaled, 0.0).astype(BF).reshape(n_chunks, QC, PAIR)
        qdz[:, QC:] = jnp.where(wide >= DH, both, 0.0).astype(BF).reshape(n_chunks, QC, PAIR)

    take_queries()
    if inline:
        each(0, n_chunks, begin)
        direct(0)
        for u in range(n_units):
            settle(u)
            forth(u, 0, 0)
            if u + 1 < n_units:
                direct(u + 1)
            each(1, n_chunks, lambda i: forth(u, i, i))
        for u in range(n_units):
            back(u, 0, 0)
            if u:
                ship_home(u - 1)
            each(1, n_chunks, lambda i: back(u, i, i))
            ship_part(u)
    else:
        for u in range(n_units):
            direct(u)
        for u in range(n_units):
            settle(u)

        def block(i):
            begin(0)
            each(0, n_units, lambda u: forth(u, i, 0))
            each(0, n_units, lambda u: back(u, i, 0))

        each(0, n_chunks, block)
        for u in range(n_units):
            ship_part(u)
        for u in range(n_units - 1):
            ship_home(u)

    def dq_copy(t):
        aa, ww = lax.rem(a0 + lax.rem(t, R), R), behind(lax.div(t, R))
        return pltpu.make_async_remote_copy(
            src_ref=dq_send.at[aa, ww], dst_ref=dq_in.at[head],
            send_sem=dq_ss.at[t], recv_sem=dq_rs.at[head],
            device_id=(aa * fs + c, ww), device_id_type=MESH)

    for i in range(n_chunks):
        dqs[i * QC:(i + 1) * QC] = jnp.concatenate([dqacc[i], jnp.zeros((DH, QC), F32)], axis=0).T
    for gi in range(R):
        for ww in range(W):
            base = gi * seq + ww * rows
            dq_send[gi, ww] = jnp.concatenate(
                [dqs[base:base + half, :DH], dqs[base + rows - half:base + rows, :DH]], axis=1).astype(BF)
    own_copy(dq_send.at[a0, w], dq_in, 1).start()
    each(1, R * W, lambda t: dq_copy(t).start())
    ship_home(n_units - 1)

    each(1, R * W, lambda t: head_arrival(t, dq_in, dq_ss, dq_rs).wait_recv())
    each(1, R * W, lambda t: head_arrival(t, fin_in, fin_ss, fin_rs).wait_recv())
    each(1, hf * W, lambda t: kv_copy(t).wait_send())
    each(0, hf * W, lambda t: pass_on(f, t).wait_send())
    each(1, R * W, lambda t: qd_copy(t).wait_send())
    own_copy(fin_send.at[0, a0, 0], fin_in, 0).wait()
    own_copy(dq_send.at[a0, w], dq_in, 1).wait()
    each(1, R * W, lambda t: dq_copy(t).wait_send())
    each(1, R * W, lambda t: fin_copy(t).wait_send())
    for u in range(n_units):
        for dc in range(1, fs):
            red_copy(u, dc).wait_send()


def tokens_again(dq_in, fin_in, dq_out, dk_out, dv_out):
    half, rows, width = dq_in.shape[1], dq_out.shape[1], dq_out.shape[2]
    for j in range(width // PAIR):
        cols = slice(j * PAIR, (j + 1) * PAIR)
        sides = []
        for h in (2 * j, 2 * j + 1):
            got = dq_in[h].astype(F32)
            sides.append(jnp.concatenate([got[:, :DH], got[2 * half - rows:, DH:]], axis=0))
        dq_out[0, :, cols] = jnp.concatenate(sides, axis=1).astype(BF)

    for j in range(width // PAIR):
        cols = slice(j * PAIR, (j + 1) * PAIR)
        one, two = fin_in[2 * j], fin_in[2 * j + 1]
        dk_out[0, :, cols] = jnp.concatenate([one[:, :DH], two[:, :DH]], axis=1)
        dv_out[0, :, cols] = jnp.concatenate([one[:, DH:], two[:, DH:]], axis=1)


def local(F, W, queries, keys_in, values_in, grad_out, partners, registers):
    _, rows, width = queries.shape
    heads = width // DH
    R = heads // W
    fs = F // R
    seq = rows * W
    nq = R * seq
    half = ((rows + 1) // 2 + 7) // 8 * 8
    inline = F * seq * nq * 8 <= 24 * 2 ** 20
    QC = next(b for b in ((576, 384, 128) if inline else (128,)) if nq % b == 0)
    held = nq // QC if inline else 1
    per = next(n for n in range(W, 0, -1) if W % n == 0 and (n == 1 or n * F * rows <= UNIT))
    units = W // per
    unit = per * F * rows
    vm = lambda *shape: pltpu.VMEM(shape, BF)
    vf = lambda *shape: pltpu.VMEM(shape, F32)
    dma = lambda n: pltpu.SemaphoreType.DMA((n,))
    out = jax.ShapeDtypeStruct((1, rows, width), BF)
    dq_heads, kv_heads = pl.pallas_call(
        functools.partial(kernel, F, W, R, QC, inline),
        out_shape=(jax.ShapeDtypeStruct((heads, half, PAIR), BF), jax.ShapeDtypeStruct((heads, rows, PAIR), BF)),
        in_specs=[pl.BlockSpec(memory_space=pltpu.SMEM)] * 2 + [pl.BlockSpec(memory_space=pltpu.VMEM)] * 4,
        out_specs=(pl.BlockSpec(memory_space=pl.ANY),) * 2,
        scratch_shapes=[
            vm(heads, rows, PAIR), vm(heads, rows, PAIR),
            vm(F, W, rows, PAIR), vm(R, W, rows, PAIR),
            vm(units, unit, PAIR), vm(units, unit, PAIR), vm(units, DH, unit),
            vm(nq, PAIR), vm(nq, PAIR), vm(nq // QC, 2 * QC, PAIR),
            vf(units, held, unit, QC), vf(units, held, unit, QC), vf(units, per, F, rows, PAIR),
            vf(nq // QC, DH, QC), vf(nq, PAIR),
            vf(units, held, 1, QC), vf(held, 1, QC), vf(held, 1, QC), vf(held, 1, QC),
            vm(units, fs - 1, R, per, rows, PAIR), vm(units, fs - 1, R, per, rows, PAIR),
            vm(units, R, per, rows, PAIR), vm(R, W, half, PAIR), dma(2),
            dma(F // 2 * W), dma(F // 2 * W), dma(F * W), dma(R * W), dma(R * W),
            dma(units * (fs - 1)), dma(units * (fs - 1)), dma(R * W), dma(heads), dma(R * W), dma(heads),
        ],
        compiler_params=pltpu.CompilerParams(
            collective_id=0, has_side_effects=True, vmem_limit_bytes=60 * 2 ** 20),
    )(partners.T, registers, queries, keys_in, values_in, grad_out)
    return pl.pallas_call(
        tokens_again,
        out_shape=(out, out, out),
        in_specs=[pl.BlockSpec(memory_space=pltpu.VMEM)] * 2,
        out_specs=(pl.BlockSpec(memory_space=pltpu.VMEM),) * 3,
    )(dq_heads, kv_heads)


def halves(F, W, part_ref, reg_ref, q_ref, k_ref, v_ref, d_ref, dq_in, fin_in,
           kv_send, qd_send, kv_in, qd_in, kaug, vz, kt, qaug, xraw, qdz, sbuf, dpbuf, acc, dqacc, dqs,
           tops, top_ref, total_ref, dsum_ref, st_send, st_in, fin_send, dq_send, own_sem,
           kv_ss, kv_rs, qd_ss, qd_rs, st_ss, st_rs, dq_ss, dq_rs, fin_ss, fin_rs):
    rows, width = q_ref.shape[1], q_ref.shape[2]
    n_slots = part_ref.shape[0]
    U, per = acc.shape[0], acc.shape[1]
    L = U * per
    heads = F * L
    group = per * F
    unit = group * rows
    QC = unit
    scale = DH ** -0.5
    half = dq_send.shape[3]
    f = lax.axis_index("frame")
    w = lax.axis_index("within")
    part = lax.div(w, L)
    other = 1 - part
    l = lax.rem(w, L)
    u0 = lax.div(l, per)
    d0 = lax.rem(l, per)
    head = f * L + l

    barrier = pltpu.get_barrier_semaphore()

    def greet(t):
        pl.semaphore_signal(barrier, inc=1, device_id=(lax.rem(f + lax.rem(t, F), F), lax.rem(w + lax.div(t, F), W)),
                            device_id_type=MESH)

    each(1, F * W, greet)

    for first, second, out in ((k_ref, v_ref, kv_send), (q_ref, d_ref, qd_send)):
        for j in range(width // PAIR):
            cols = slice(j * PAIR, (j + 1) * PAIR)
            one = first[0, :, cols]
            two = second[0, :, cols]
            out[2 * j] = jnp.concatenate([one[:, :DH], two[:, :DH]], axis=1)
            out[2 * j + 1] = jnp.concatenate([one[:, DH:], two[:, DH:]], axis=1)
    kv_in[l, f] = kv_send[head]
    qd_in[w, f] = qd_send[head]

    pl.semaphore_wait(barrier, F * W - 1)

    def around(t):
        return lax.rem(d0 + lax.div(lax.rem(t, group), F), per), lax.rem(f + lax.rem(t, F), F)

    def near(t):
        d, ff = around(t)
        return ff, lax.rem(u0 + lax.div(t, group), U) * per + d

    def far(t):
        d, ff = around(lax.div(t, U))
        return ff, lax.rem(u0 + lax.rem(t, U), U) * per + d

    def remote(src, dst, ss, rs, device):
        return pltpu.make_async_remote_copy(src_ref=src, dst_ref=dst, send_sem=ss, recv_sem=rs,
                                            device_id=device, device_id_type=MESH)

    def kv_copy(t):
        ff, ll = near(t)
        return remote(kv_send.at[ff * L + ll], kv_in.at[l, f], kv_ss.at[t], kv_rs.at[l * F + f], (ff, part * L + ll))

    def kv_arrival(t):
        ff, ll = near(t)
        here = kv_in.at[ll, ff]
        return remote(here, here, kv_ss.at[t], kv_rs.at[ll * F + ff], (ff, part * L + ll))

    def qd_copy(t):
        ff, ll = near(t)
        return remote(qd_send.at[ff * L + ll], qd_in.at[w, f], qd_ss.at[t], qd_rs.at[w * F + f], (ff, part * L + ll))

    def qd_cross(t):
        ff, ll = far(t)
        return remote(qd_send.at[ff * L + ll], qd_in.at[w, f], qd_ss.at[heads + t], qd_rs.at[w * F + f],
                      (ff, other * L + ll))

    def block_of(slot):
        if slot < U:
            return part * U + lax.rem(u0 + slot, U)
        return other * U + (slot - U) + part * (U - 1 - 2 * (slot - U))

    def qd_arrival(block, t):
        d, ff = around(t)
        ww = block * per + d
        here = qd_in.at[ww, ff]
        return remote(here, here, qd_ss.at[t], qd_rs.at[ww * F + ff], (ff, ww))

    def send_near(t):
        kv_copy(t).start()
        qd_copy(t).start()

    each(1, heads, send_near)
    each(0, heads, lambda t: qd_cross(t).start())

    acc[...] = jnp.zeros_like(acc)
    st_send[...] = jnp.zeros_like(st_send)

    lane1 = lax.broadcasted_iota(jnp.int32, (1, PAIR), 1)
    table = [pieces_of(HIDDEN)] + [pieces_of(math.log(n)) for n in range(1, n_slots + 2)]
    marks = []
    for p in range(F):
        seen = jnp.zeros((1, PAIR), F32)
        unseen = jnp.zeros((1, PAIR), F32)
        for g in range(F):
            own = 1 if p == g else 0
            count = own
            for slot in range(n_slots):
                count = count + jnp.where(part_ref[slot, g] == p, 1, 0)
            for e in range(SPLITS):
                here = lane1 == DH + SPLITS * g + e
                unseen = jnp.where(here, table[own][e], unseen)
                for n in range(own, n_slots + 2):
                    seen = jnp.where(here & (count == n), table[n][e], seen)
        marks.append((seen, unseen))

    lane = lax.broadcasted_iota(jnp.int32, (rows, PAIR), 1)
    row = lax.broadcasted_iota(jnp.int32, (rows, PAIR), 0)
    tall = lax.broadcasted_iota(jnp.int32, (unit, PAIR), 1)

    def prepare(j):
        u = lax.rem(u0 + j, U)
        aug, raw = [], []
        for d in range(per):
            ll = u * per + d
            for p in range(F):
                both = kv_in[ll, p].astype(F32)
                extra = jnp.where(row + (part * L + ll) * rows >= reg_ref[p], marks[p][0], marks[p][1])
                raw.append(both)
                aug.append(jnp.where(lane < DH, both, extra))
        raw = jnp.concatenate(raw, axis=0)
        kaug[j] = jnp.concatenate(aug, axis=0).astype(BF)
        vz[j] = jnp.where(tall >= DH, raw, 0.0).astype(BF)
        kt[j] = (raw * scale).T[:DH].astype(BF)

    def take_keys(j):
        each(max(j * group, 1), (j + 1) * group, lambda t: kv_arrival(t).wait_recv())
        prepare(j)

    hot = [jnp.where((lane >= DH + SPLITS * g) & (lane < DH + SPLITS * (g + 1)), 1.0, 0.0) for g in range(F)]

    def take_queries(i):
        block = block_of(i)
        each(0 if i else 1, group, lambda t: qd_arrival(block, t).wait_recv())
        raw, aug = [], []
        for d in range(per):
            for g in range(F):
                both = qd_in[block * per + d, g].astype(F32)
                raw.append(both)
                aug.append(jnp.where(lane < DH, both * scale, hot[g]))
        raw = jnp.concatenate(raw, axis=0)
        qaug[i] = jnp.concatenate(aug, axis=0).astype(BF)
        xraw[i] = raw.astype(BF)
        qdz[i, :QC] = jnp.where(tall < DH, raw * scale, 0.0).astype(BF)
        qdz[i, QC:] = jnp.where(tall >= DH, raw, 0.0).astype(BF)

    def forth(j, i):
        raw = rdot(kaug[j], qaug[i])
        top = jnp.max(raw, axis=0, keepdims=True)
        if j:
            old = top_ref[i]
            top = jnp.maximum(old, top)
        expo = jnp.exp(raw - top)
        dprod = rdot(vz[j], xraw[i])
        sbuf[j, i] = expo
        dpbuf[j, i] = dprod
        tops[j, i] = top
        top_ref[i] = top
        total = jnp.sum(expo, axis=0, keepdims=True)
        dsum = jnp.sum(expo * dprod, axis=0, keepdims=True)
        if j:
            keep = jnp.exp(old - top)
            total = total_ref[i] * keep + total
            dsum = dsum_ref[i] * keep + dsum
        total_ref[i] = total
        dsum_ref[i] = dsum

    spans = [(c, min(c + PAIR, QC)) for c in range(0, QC, PAIR)]

    def st_copy(i):
        return remote(st_send.at[i], st_in.at[block_of(i)], st_ss.at[i], st_rs.at[block_of(i)], (f, other * L + l))

    def give(i):
        for s, ref in enumerate((top_ref, total_ref, dsum_ref)):
            value = ref[i]
            for n, (lo, hi) in enumerate(spans):
                at = s * len(spans) + n
                st_send[i, at:at + 1, :hi - lo] = value[:, lo:hi]
        st_copy(i).start()

    def meet(i, block):
        here = st_in.at[block]
        remote(here, here, st_ss.at[0], st_rs.at[block], (f, other * L + l)).wait_recv()
        got = []
        for s in range(3):
            got.append(jnp.concatenate(
                [st_in[block, s * len(spans) + n:s * len(spans) + n + 1, :hi - lo] for n, (lo, hi) in enumerate(spans)],
                axis=1))
        mine = top_ref[i]
        top = jnp.maximum(mine, got[0])
        a, b = jnp.exp(mine - top), jnp.exp(got[0] - top)
        inv = 1.0 / (total_ref[i] * a + got[1] * b)
        top_ref[i] = top
        dsum_ref[i] = (dsum_ref[i] * a + got[2] * b) * inv
        total_ref[i] = inv

    def back(j, i):
        factor = jnp.exp(tops[j, i] - top_ref[i]) * total_ref[i]
        prob = sbuf[j, i] * factor
        dscore = (prob * (dpbuf[j, i] - dsum_ref[i])).astype(BF)
        added = dot(jnp.concatenate([dscore, prob.astype(BF)], axis=1), qdz[i])
        acc[j] += added.reshape(per, F, rows, PAIR)
        more = dot(kt[j], dscore)
        if j:
            more = dqacc[...] + more
        dqacc[...] = more

    def dq_copy(i, block, t):
        d, ff = around(t)
        return remote(dq_send.at[i, d, ff], dq_in.at[part, head], dq_ss.at[i * group + t],
                      dq_rs.at[part * heads + head], (ff, block * per + d))

    def dq_own(i):
        return pltpu.make_async_copy(dq_send.at[i, d0, f], dq_in.at[part, head], own_sem.at[0])

    def ship_queries(i, block, slot):
        dqs[...] = jnp.concatenate([dqacc[...], jnp.zeros((DH, QC), F32)], axis=0).T
        for d in range(per):
            for g in range(F):
                base = (d * F + g) * rows
                dq_send[i, d, g] = jnp.concatenate(
                    [dqs[base:base + half, :DH], dqs[base + rows - half:base + rows, :DH]], axis=1).astype(BF)
        if slot >= U:
            dq_copy(i, block, 0).start()
        else:
            @pl.when(i == 0)
            def _():
                dq_own(i).start()

            @pl.when(i != 0)
            def _():
                dq_copy(i, block, 0).start()
        each(1, group, lambda t: dq_copy(i, block, t).start())

    def fin_copy(t):
        ff, ll = near(t)
        return remote(fin_send.at[lax.div(t, group), lax.rem(ll, per), ff], fin_in.at[head], fin_ss.at[t],
                      fin_rs.at[head], (ff, part * L + ll))

    def fin_own():
        return pltpu.make_async_copy(fin_send.at[0, d0, f], fin_in.at[head], own_sem.at[1])

    def ship_keys(j):
        fin_send[j] = acc[j].astype(BF)
        if j == 0:
            fin_own().start()
        each(max(j * group, 1), (j + 1) * group, lambda t: fin_copy(t).start())

    for i in range(U):
        for j in range(U):
            if i == 0:
                take_keys(j)
            if j == 0:
                take_queries(i)
            forth(j, i)
        give(i)
    for i in range(U, 2 * U):
        take_queries(i)
        for j in range(U):
            forth(j, i)
        give(i)
        meet(i, block_of(i))
        for j in range(U):
            back(j, i)
        ship_queries(i, block_of(i), i)
    for n in range(U):
        u = n + (1 - part) * (U - 1 - 2 * n)
        i = lax.rem(u + U - u0, U)
        meet(i, part * U + u)
        for j in range(U):
            back(j, i)
            if n == U - 1:
                if j == U - 1:
                    ship_queries(i, part * U + u, n)
                ship_keys(j)
        if n < U - 1:
            ship_queries(i, part * U + u, n)

    def dq_arrival(t):
        ff, ww = lax.rem(f + lax.rem(t, F), F), lax.rem(w + lax.div(t, F), W)
        pp, hh = lax.div(ww, L), ff * L + lax.rem(ww, L)
        here = dq_in.at[pp, hh]
        return remote(here, here, dq_ss.at[0], dq_rs.at[pp * heads + hh], (ff, ww))

    def fin_arrival(t):
        ff, ll = near(t)
        here = fin_in.at[ff * L + ll]
        return remote(here, here, fin_ss.at[t], fin_rs.at[ff * L + ll], (ff, part * L + ll))

    each(1, F * W, lambda t: dq_arrival(t).wait_recv())
    each(1, heads, lambda t: fin_arrival(t).wait_recv())
    dq_own(0).wait()
    fin_own().wait()

    def sent(t):
        kv_copy(t).wait_send()
        qd_copy(t).wait_send()
        fin_copy(t).wait_send()

    each(1, heads, sent)
    each(0, heads, lambda t: qd_cross(t).wait_send())
    for i in range(2 * U):
        st_copy(i).wait_send()
        each(0 if i else 1, group, lambda t: dq_copy(i, block_of(i), t).wait_send())


def both_halves(dq_in, fin_in, dq_out, dk_out, dv_out):
    half, rows, width = dq_in.shape[2], dq_out.shape[1], dq_out.shape[2]
    for j in range(width // PAIR):
        cols = slice(j * PAIR, (j + 1) * PAIR)
        sides = []
        for h in (2 * j, 2 * j + 1):
            got = dq_in[0, h].astype(F32) + dq_in[1, h].astype(F32)
            sides.append(jnp.concatenate([got[:, :DH], got[2 * half - rows:, DH:]], axis=0))
        dq_out[0, :, cols] = jnp.concatenate(sides, axis=1).astype(BF)
        one, two = fin_in[2 * j], fin_in[2 * j + 1]
        dk_out[0, :, cols] = jnp.concatenate([one[:, :DH], two[:, :DH]], axis=1)
        dv_out[0, :, cols] = jnp.concatenate([one[:, DH:], two[:, DH:]], axis=1)


def local_halves(F, W, queries, keys_in, values_in, grad_out, partners, registers):
    _, rows, width = queries.shape
    heads = width // DH
    L = W // 2
    half = ((rows + 1) // 2 + 7) // 8 * 8
    per = next(n for n in range(L, 0, -1) if L % n == 0 and (n == 1 or n * F * rows <= UNIT))
    U = L // per
    unit = per * F * rows
    C = 2 * U
    stats = (3 * ((unit + PAIR - 1) // PAIR) + 7) // 8 * 8
    vm = lambda *shape: pltpu.VMEM(shape, BF)
    vf = lambda *shape: pltpu.VMEM(shape, F32)
    dma = lambda n: pltpu.SemaphoreType.DMA((n,))
    out = jax.ShapeDtypeStruct((1, rows, width), BF)
    dq_heads, kv_heads = pl.pallas_call(
        functools.partial(halves, F, W),
        out_shape=(jax.ShapeDtypeStruct((2, heads, half, PAIR), BF), jax.ShapeDtypeStruct((heads, rows, PAIR), BF)),
        in_specs=[pl.BlockSpec(memory_space=pltpu.SMEM)] * 2 + [pl.BlockSpec(memory_space=pltpu.VMEM)] * 4,
        out_specs=(pl.BlockSpec(memory_space=pl.ANY),) * 2,
        scratch_shapes=[
            vm(heads, rows, PAIR), vm(heads, rows, PAIR), vm(L, F, rows, PAIR), vm(W, F, rows, PAIR),
            vm(U, unit, PAIR), vm(U, unit, PAIR), vm(U, DH, unit),
            vm(C, unit, PAIR), vm(C, unit, PAIR), vm(C, 2 * unit, PAIR),
            vf(U, C, unit, unit), vf(U, C, unit, unit), vf(U, per, F, rows, PAIR),
            vf(DH, unit), vf(unit, PAIR),
            vf(U, C, 1, unit), vf(C, 1, unit), vf(C, 1, unit), vf(C, 1, unit),
            vf(C, stats, PAIR), vf(C, stats, PAIR),
            vm(U, per, F, rows, PAIR), vm(C, per, F, half, PAIR), dma(2),
            dma(heads), dma(heads), dma(2 * heads), dma(2 * heads), dma(C), dma(C),
            dma(2 * heads), dma(2 * heads), dma(heads), dma(heads),
        ],
        compiler_params=pltpu.CompilerParams(
            collective_id=0, has_side_effects=True, vmem_limit_bytes=60 * 2 ** 20),
    )(partners.T, registers, queries, keys_in, values_in, grad_out)
    return pl.pallas_call(
        both_halves,
        out_shape=(out, out, out),
        in_specs=[pl.BlockSpec(memory_space=pltpu.VMEM)] * 2,
        out_specs=(pl.BlockSpec(memory_space=pltpu.VMEM),) * 3,
    )(dq_heads, kv_heads)


def choose(F, W, queries, *others):
    _, rows, width = queries.shape
    heads = width // DH
    held = 2 * F * W // 2 * rows * F * W * rows * 4
    if W % 2 == 0 and F * W == 2 * heads and SPLITS * F <= DH and held <= 24 * 2 ** 20:
        return local_halves(F, W, queries, *others)
    return local(F, W, queries, *others)


def solution(mesh):
    spec = P("frame", "within", None)
    return jax.shard_map(
        functools.partial(choose, mesh.shape["frame"], mesh.shape["within"]),
        mesh=mesh,
        in_specs=(spec, spec, spec, spec, P(), P()),
        out_specs=(spec, spec, spec),
        check_vma=False,
    )
```

```python
import functools
import math

import jax
import jax.numpy as jnp
import numpy as np
from jax import lax
from jax.experimental import pallas as pl
from jax.experimental.pallas import tpu as pltpu
from jax.sharding import PartitionSpec as P

DH = 64
PAIR = 2 * DH
SPLITS = 3
UNIT = 640
HIDDEN = -1e30
BF = jnp.bfloat16
F32 = jnp.float32
MESH = pl.DeviceIdType.MESH


def pieces_of(value):
    left, out = float(value), []
    for _ in range(SPLITS):
        part = float(np.asarray(left, dtype=jnp.bfloat16))
        out.append(part)
        left = left - part if abs(value) < 1e20 else 0.0
    return out


def rdot(a, b):
    return lax.dot_general(a, b, (((1,), (1,)), ((), ())), preferred_element_type=F32)


def dot(a, b):
    return jnp.dot(a, b, preferred_element_type=F32)


def each(lo, hi, do):
    def step(t, carry):
        do(t)
        return carry
    lax.fori_loop(lo, hi, step, 0)


def kernel(F, W, R, QC, inline, part_ref, reg_ref, q_ref, k_ref, v_ref, d_ref, dq_in, fin_in,
           kv_send, qd_send, kv_in, qd_in, kaug, vz, kt, qaug, xraw, qdz, sbuf, dpbuf, acc, dqacc, dqs,
           tops, top_ref, total_ref, dsum_ref,
           red_send, red_in, fin_send, dq_send, own_sem,
           kv_ss, fw_ss, kv_rs, qd_ss, qd_rs, red_ss, red_rs, fin_ss, fin_rs, dq_ss, dq_rs):
    fs = F // R
    hf = F // 2
    rows = q_ref.shape[1]
    width = q_ref.shape[2]
    seq = rows * W
    n_slots = part_ref.shape[0]
    scale = DH ** -0.5
    half = dq_send.shape[2]
    nq = R * seq
    n_chunks = nq // QC
    n_units, per = acc.shape[0], acc.shape[1]
    unit = per * F * rows
    f = lax.axis_index("frame")
    w = lax.axis_index("within")
    c = lax.rem(f, fs)
    a0 = lax.div(f, fs)
    sib = f + 1 - 2 * lax.rem(f, 2)
    head = w * R + a0

    barrier = pltpu.get_barrier_semaphore()

    def ahead(dw):
        return lax.rem(w + W - dw, W)

    def behind(dw):
        return lax.rem(w + dw, W)

    def greet(t):
        pl.semaphore_signal(barrier, inc=1, device_id=(lax.rem(f + 2 * lax.rem(t, hf), F), ahead(lax.div(t, hf))),
                            device_id_type=MESH)

    each(1, hf * W, greet)
    for dc in range(1, fs, 2):
        pl.semaphore_signal(barrier, inc=1, device_id=(a0 * fs + lax.rem(c + dc, fs), w), device_id_type=MESH)

    for first, second, out in ((q_ref, d_ref, qd_send), (k_ref, v_ref, kv_send)):
        for j in range(width // PAIR):
            cols = slice(j * PAIR, (j + 1) * PAIR)
            one = first[0, :, cols]
            two = second[0, :, cols]
            out[2 * j] = jnp.concatenate([one[:, :DH], two[:, :DH]], axis=1)
            out[2 * j + 1] = jnp.concatenate([one[:, DH:], two[:, DH:]], axis=1)
    kv_in[f, w] = kv_send[head]
    qd_in[a0, w] = qd_send[head]

    pl.semaphore_wait(barrier, hf * W - 1 + fs // 2)

    def kv_copy(t):
        ff = lax.rem(f + 2 * lax.rem(t, hf), F)
        ww = ahead(lax.div(t, hf))
        return pltpu.make_async_remote_copy(
            src_ref=kv_send.at[ww * R + lax.div(ff, fs)], dst_ref=kv_in.at[f, w],
            send_sem=kv_ss.at[t], recv_sem=kv_rs.at[f * W + w],
            device_id=(ff, ww), device_id_type=MESH)

    def pass_on(origin, t):
        ff = lax.rem(origin + F - 2 * lax.rem(t, hf), F)
        ww = behind(lax.div(t, hf))
        return pltpu.make_async_remote_copy(
            src_ref=kv_in.at[ff, ww], dst_ref=kv_in.at[ff, ww],
            send_sem=fw_ss.at[t], recv_sem=kv_rs.at[ff * W + ww],
            device_id=(sib, w), device_id_type=MESH)

    def qd_copy(t):
        aa, ww = lax.rem(a0 + lax.rem(t, R), R), ahead(lax.div(t, R))
        return pltpu.make_async_remote_copy(
            src_ref=qd_send.at[ww * R + aa], dst_ref=qd_in.at[a0, w],
            send_sem=qd_ss.at[t], recv_sem=qd_rs.at[a0 * W + w],
            device_id=(aa * fs + c, ww), device_id_type=MESH)

    def arrival(t, buffer, send, recv, index, source):
        return pltpu.make_async_remote_copy(
            src_ref=buffer.at[index], dst_ref=buffer.at[index], send_sem=send.at[t], recv_sem=recv,
            device_id=source, device_id_type=MESH)

    def qd_arrival(t):
        aa, ww = lax.rem(a0 + R - lax.rem(t, R), R), behind(lax.div(t, R))
        return arrival(t, qd_in, qd_ss, qd_rs.at[aa * W + ww], (aa, ww), (aa * fs + c, ww))

    def head_arrival(t, buffer, send, recv):
        aa, ww = lax.rem(a0 + R - lax.rem(t, R), R), ahead(lax.div(t, R))
        return arrival(t, buffer, send, recv.at[ww * R + aa], (ww * R + aa,), (aa * fs + c, ww))

    each(1, R * W, lambda t: qd_copy(t).start())
    pass_on(f, 0).start()
    each(1, hf * W, lambda t: kv_copy(t).start())

    acc[...] = jnp.zeros_like(acc)
    dqacc[...] = jnp.zeros_like(dqacc)

    def relay(t):
        move = pass_on(f, t)
        move.wait_recv()
        move.start()

    lane1 = lax.broadcasted_iota(jnp.int32, (1, PAIR), 1)
    table = [pieces_of(HIDDEN)] + [pieces_of(math.log(n)) for n in range(1, n_slots + 2)]
    marks = []
    for p in range(F):
        seen = jnp.zeros((1, PAIR), F32)
        unseen = jnp.zeros((1, PAIR), F32)
        for gi in range(R):
            g = c + fs * gi
            own = jnp.where(p == g, 1, 0)
            count = own
            for slot in range(n_slots):
                count = count + jnp.where(part_ref[slot, g] == p, 1, 0)
            for e in range(SPLITS):
                here = lane1 == DH + SPLITS * gi + e
                for n in range(n_slots + 2):
                    if n < 2:
                        unseen = jnp.where(here & (own == n), table[n][e], unseen)
                    seen = jnp.where(here & (count == n), table[n][e], seen)
        marks.append((seen, unseen))

    lane = lax.broadcasted_iota(jnp.int32, (rows, PAIR), 1)
    row = lax.broadcasted_iota(jnp.int32, (rows, PAIR), 0)

    def prepare(u):
        aug, raw = [], []
        for d in range(per):
            ww = behind(u * per + d)
            for p in range(F):
                both = kv_in[p, ww].astype(F32)
                extra = jnp.where(row + ww * rows >= reg_ref[p], marks[p][0], marks[p][1])
                raw.append(both)
                aug.append(jnp.where(lane < DH, both, extra))
        raw = jnp.concatenate(raw, axis=0)
        keep = lax.broadcasted_iota(jnp.int32, (unit, PAIR), 1) >= DH
        kaug[u] = jnp.concatenate(aug, axis=0).astype(BF)
        vz[u] = jnp.where(keep, raw, 0.0).astype(BF)
        kt[u] = (raw * scale).T[:DH].astype(BF)

    def direct(u):
        each(max(u * per * hf, 1), (u + 1) * per * hf, relay)

    def settle(u):
        each(u * per * hf, (u + 1) * per * hf, lambda t: pass_on(sib, t).wait_recv())
        prepare(u)

    def rows_of(i):
        return pl.ds(pl.multiple_of(i * QC, QC), QC)

    def begin(b):
        top_ref[b] = jnp.full_like(top_ref[b], -3e38)
        total_ref[b] = jnp.zeros_like(total_ref[b])
        dsum_ref[b] = jnp.zeros_like(dsum_ref[b])

    def forth(u, i, b):
        at = rows_of(i)
        raw = rdot(kaug[u], qaug[at])
        old = top_ref[b]
        top = jnp.maximum(old, jnp.max(raw, axis=0, keepdims=True))
        keep = jnp.exp(old - top)
        expo = jnp.exp(raw - top)
        dprod = rdot(vz[u], xraw[at])
        sbuf[u, b] = expo
        dpbuf[u, b] = dprod
        tops[u, b] = top
        top_ref[b] = top
        total_ref[b] = total_ref[b] * keep + jnp.sum(expo, axis=0, keepdims=True)
        dsum_ref[b] = dsum_ref[b] * keep + jnp.sum(expo * dprod, axis=0, keepdims=True)

    def back(u, i, b):
        inv = 1.0 / total_ref[b]
        factor = jnp.exp(tops[u, b] - top_ref[b]) * inv
        prob = sbuf[u, b] * factor
        dscore = (prob * (dpbuf[u, b] - dsum_ref[b] * inv)).astype(BF)
        added = dot(jnp.concatenate([dscore, prob.astype(BF)], axis=1), qdz[i])
        acc[u] += added.reshape(per, F, rows, PAIR)
        dqacc[i] += dot(kt[u], dscore)

    def own_copy(block, buffer, n):
        return pltpu.make_async_copy(block, buffer.at[head], own_sem.at[n])

    def red_copy(u, dc):
        return pltpu.make_async_remote_copy(
            src_ref=red_send.at[u, dc - 1], dst_ref=red_in.at[u, dc - 1],
            send_sem=red_ss.at[u * (fs - 1) + dc - 1], recv_sem=red_rs.at[u * (fs - 1) + dc - 1],
            device_id=(a0 * fs + lax.rem(c + dc, fs), w), device_id_type=MESH)

    def ship_part(u):
        for dc in range(1, fs):
            for gi in range(R):
                red_send[u, dc - 1, gi] = acc[u, :, lax.rem(c + dc, fs) + fs * gi].astype(BF)
            red_copy(u, dc).start()

    def fin_copy(t):
        dw = lax.div(t, R)
        aa, ww = lax.rem(a0 + lax.rem(t, R), R), behind(dw)
        return pltpu.make_async_remote_copy(
            src_ref=fin_send.at[lax.div(dw, per), aa, lax.rem(dw, per)], dst_ref=fin_in.at[head],
            send_sem=fin_ss.at[t], recv_sem=fin_rs.at[head],
            device_id=(aa * fs + c, ww), device_id_type=MESH)

    def ship_home(u):
        for dc in range(1, fs):
            red_copy(u, dc).wait_recv()
        for gi in range(R):
            whole = acc[u, :, c + fs * gi]
            for dc in range(1, fs):
                whole = whole + red_in[u, dc - 1, gi].astype(F32)
            fin_send[u, gi] = whole.astype(BF)
        if u == 0:
            own_copy(fin_send.at[0, a0, 0], fin_in, 0).start()
        each(max(u * per * R, 1), (u + 1) * per * R, lambda t: fin_copy(t).start())

    def take_queries():
        each(1, R * W, lambda t: qd_arrival(t).wait_recv())
        wide = lax.broadcasted_iota(jnp.int32, (nq, PAIR), 1)
        tall = lax.broadcasted_iota(jnp.int32, (nq, PAIR), 0)
        both = qd_in[...].astype(F32).reshape(nq, PAIR)
        mark = jnp.zeros((nq, PAIR), F32)
        for gi in range(R):
            mine = (tall >= gi * seq) & (tall < (gi + 1) * seq)
            mark = jnp.where(mine & (wide >= DH + SPLITS * gi) & (wide < DH + SPLITS * (gi + 1)), 1.0, mark)
        scaled = both * scale
        qaug[...] = jnp.where(wide < DH, scaled, mark).astype(BF)
        xraw[...] = both.astype(BF)
        qdz[:, :QC] = jnp.where(wide < DH, scaled, 0.0).astype(BF).reshape(n_chunks, QC, PAIR)
        qdz[:, QC:] = jnp.where(wide >= DH, both, 0.0).astype(BF).reshape(n_chunks, QC, PAIR)

    take_queries()
    if inline:
        each(0, n_chunks, begin)
        direct(0)
        for u in range(n_units):
            settle(u)
            forth(u, 0, 0)
            if u + 1 < n_units:
                direct(u + 1)
            each(1, n_chunks, lambda i: forth(u, i, i))
        for u in range(n_units):
            back(u, 0, 0)
            if u:
                ship_home(u - 1)
            each(1, n_chunks, lambda i: back(u, i, i))
            ship_part(u)
    else:
        for u in range(n_units):
            direct(u)
        for u in range(n_units):
            settle(u)

        def block(i):
            begin(0)
            each(0, n_units, lambda u: forth(u, i, 0))
            each(0, n_units, lambda u: back(u, i, 0))

        each(0, n_chunks, block)
        for u in range(n_units):
            ship_part(u)
        for u in range(n_units - 1):
            ship_home(u)

    def dq_copy(t):
        aa, ww = lax.rem(a0 + lax.rem(t, R), R), behind(lax.div(t, R))
        return pltpu.make_async_remote_copy(
            src_ref=dq_send.at[aa, ww], dst_ref=dq_in.at[head],
            send_sem=dq_ss.at[t], recv_sem=dq_rs.at[head],
            device_id=(aa * fs + c, ww), device_id_type=MESH)

    for i in range(n_chunks):
        dqs[i * QC:(i + 1) * QC] = jnp.concatenate([dqacc[i], jnp.zeros((DH, QC), F32)], axis=0).T
    for gi in range(R):
        for ww in range(W):
            base = gi * seq + ww * rows
            dq_send[gi, ww] = jnp.concatenate(
                [dqs[base:base + half, :DH], dqs[base + rows - half:base + rows, :DH]], axis=1).astype(BF)
    own_copy(dq_send.at[a0, w], dq_in, 1).start()
    each(1, R * W, lambda t: dq_copy(t).start())
    ship_home(n_units - 1)

    each(1, R * W, lambda t: head_arrival(t, dq_in, dq_ss, dq_rs).wait_recv())
    each(1, R * W, lambda t: head_arrival(t, fin_in, fin_ss, fin_rs).wait_recv())
    each(1, hf * W, lambda t: kv_copy(t).wait_send())
    each(0, hf * W, lambda t: pass_on(f, t).wait_send())
    each(1, R * W, lambda t: qd_copy(t).wait_send())
    own_copy(fin_send.at[0, a0, 0], fin_in, 0).wait()
    own_copy(dq_send.at[a0, w], dq_in, 1).wait()
    each(1, R * W, lambda t: dq_copy(t).wait_send())
    each(1, R * W, lambda t: fin_copy(t).wait_send())
    for u in range(n_units):
        for dc in range(1, fs):
            red_copy(u, dc).wait_send()


def tokens_again(dq_in, fin_in, dq_out, dk_out, dv_out):
    half, rows, width = dq_in.shape[1], dq_out.shape[1], dq_out.shape[2]
    for j in range(width // PAIR):
        cols = slice(j * PAIR, (j + 1) * PAIR)
        sides = []
        for h in (2 * j, 2 * j + 1):
            got = dq_in[h].astype(F32)
            sides.append(jnp.concatenate([got[:, :DH], got[2 * half - rows:, DH:]], axis=0))
        dq_out[0, :, cols] = jnp.concatenate(sides, axis=1).astype(BF)

    for j in range(width // PAIR):
        cols = slice(j * PAIR, (j + 1) * PAIR)
        one, two = fin_in[2 * j], fin_in[2 * j + 1]
        dk_out[0, :, cols] = jnp.concatenate([one[:, :DH], two[:, :DH]], axis=1)
        dv_out[0, :, cols] = jnp.concatenate([one[:, DH:], two[:, DH:]], axis=1)


def local(F, W, queries, keys_in, values_in, grad_out, partners, registers):
    _, rows, width = queries.shape
    heads = width // DH
    R = heads // W
    fs = F // R
    seq = rows * W
    nq = R * seq
    half = ((rows + 1) // 2 + 7) // 8 * 8
    inline = F * seq * nq * 8 <= 24 * 2 ** 20
    QC = next(b for b in ((576, 384, 128) if inline else (128,)) if nq % b == 0)
    held = nq // QC if inline else 1
    per = next(n for n in range(W, 0, -1) if W % n == 0 and (n == 1 or n * F * rows <= UNIT))
    units = W // per
    unit = per * F * rows
    vm = lambda *shape: pltpu.VMEM(shape, BF)
    vf = lambda *shape: pltpu.VMEM(shape, F32)
    dma = lambda n: pltpu.SemaphoreType.DMA((n,))
    out = jax.ShapeDtypeStruct((1, rows, width), BF)
    dq_heads, kv_heads = pl.pallas_call(
        functools.partial(kernel, F, W, R, QC, inline),
        out_shape=(jax.ShapeDtypeStruct((heads, half, PAIR), BF), jax.ShapeDtypeStruct((heads, rows, PAIR), BF)),
        in_specs=[pl.BlockSpec(memory_space=pltpu.SMEM)] * 2 + [pl.BlockSpec(memory_space=pltpu.VMEM)] * 4,
        out_specs=(pl.BlockSpec(memory_space=pl.ANY),) * 2,
        scratch_shapes=[
            vm(heads, rows, PAIR), vm(heads, rows, PAIR),
            vm(F, W, rows, PAIR), vm(R, W, rows, PAIR),
            vm(units, unit, PAIR), vm(units, unit, PAIR), vm(units, DH, unit),
            vm(nq, PAIR), vm(nq, PAIR), vm(nq // QC, 2 * QC, PAIR),
            vf(units, held, unit, QC), vf(units, held, unit, QC), vf(units, per, F, rows, PAIR),
            vf(nq // QC, DH, QC), vf(nq, PAIR),
            vf(units, held, 1, QC), vf(held, 1, QC), vf(held, 1, QC), vf(held, 1, QC),
            vm(units, fs - 1, R, per, rows, PAIR), vm(units, fs - 1, R, per, rows, PAIR),
            vm(units, R, per, rows, PAIR), vm(R, W, half, PAIR), dma(2),
            dma(F // 2 * W), dma(F // 2 * W), dma(F * W), dma(R * W), dma(R * W),
            dma(units * (fs - 1)), dma(units * (fs - 1)), dma(R * W), dma(heads), dma(R * W), dma(heads),
        ],
        compiler_params=pltpu.CompilerParams(
            collective_id=0, has_side_effects=True, vmem_limit_bytes=60 * 2 ** 20),
    )(partners.T, registers, queries, keys_in, values_in, grad_out)
    return pl.pallas_call(
        tokens_again,
        out_shape=(out, out, out),
        in_specs=[pl.BlockSpec(memory_space=pltpu.VMEM)] * 2,
        out_specs=(pl.BlockSpec(memory_space=pltpu.VMEM),) * 3,
    )(dq_heads, kv_heads)


def halves(F, W, part_hbm, reg_hbm, q_hbm, k_hbm, v_hbm, d_hbm, dq_in, fin_in,
           part_ref, reg_ref, q_ref, k_ref, v_ref, d_ref, kv_send, qd_send, kv_in, qd_in,
           kaug, vz, kt, qaug, xraw, qdz, sbuf, dpbuf, acc, dqacc, dqs,
           tops, top_ref, total_ref, dsum_ref, st_send, st_in, fin_send, dq_send,
           in_sem, kv_ss, kv_rs, qd_ss, qd_rs, st_ss, st_rs, dq_ss, dq_rs, fin_ss, fin_rs, below, above):
    rows, width = q_ref.shape[1], q_ref.shape[2]
    n_slots = part_ref.shape[0]
    U, per = kv_in.shape[0], kv_in.shape[1]
    L = U * per
    B = 2 * U
    heads = F * L
    group = per * F
    unit = group * rows
    QC = unit
    scale = DH ** -0.5
    half = dq_send.shape[1]
    f = lax.axis_index("frame")
    w = lax.axis_index("within")
    block0 = lax.div(w, per)
    d0 = lax.rem(w, per)
    part = lax.div(block0, U)
    other = 1 - part
    u0 = lax.rem(block0, U)
    l = u0 * per + d0
    head = f * L + l

    barrier = pltpu.get_barrier_semaphore()

    def around(t):
        return lax.rem(d0 + lax.div(t, F), per), lax.rem(f + lax.rem(t, F), F)

    def knock(sem, block, d, ff):
        pl.semaphore_signal(sem, inc=1, device_id=(ff, block * per + d), device_id_type=MESH)

    def greet(t):
        d, ff = around(group - t)
        knock(barrier, block0, d, ff)

    @pl.when(block0 > 0)
    def _():
        knock(barrier, block0 - 1, d0, f)

    @pl.when(block0 < B - 1)
    def _():
        knock(barrier, block0 + 1, d0, f)

    each(1, group, greet)
    loads = [pltpu.make_async_copy(src, dst, in_sem.at[n]) for n, (src, dst) in enumerate(
        ((k_hbm, k_ref), (v_hbm, v_ref), (q_hbm, q_ref), (d_hbm, d_ref), (part_hbm, part_ref), (reg_hbm, reg_ref)))]
    for load in loads:
        load.start()

    for first, second, out in ((k_ref, v_ref, kv_send), (q_ref, d_ref, qd_send)):
        for load in (loads.pop(0), loads.pop(0)):
            load.wait()
        for j in range(width // PAIR):
            cols = slice(j * PAIR, (j + 1) * PAIR)
            one = first[0, :, cols]
            two = second[0, :, cols]
            out[2 * j] = jnp.concatenate([one[:, :DH], two[:, :DH]], axis=1)
            out[2 * j + 1] = jnp.concatenate([one[:, DH:], two[:, DH:]], axis=1)

    def remote(src, dst, ss, rs, device):
        return pltpu.make_async_remote_copy(src_ref=src, dst_ref=dst, send_sem=ss, recv_sem=rs,
                                            device_id=device, device_id_type=MESH)

    def head_at(block, d, ff):
        return ff * L + lax.rem(block, U) * per + d

    def kv_copy(block, t):
        d, ff = around(t)
        return remote(kv_send.at[head_at(block, d, ff)], kv_in.at[u0, d0, f], kv_ss.at[0], kv_rs.at[u0],
                      (ff, block * per + d))

    def qd_copy(block, t):
        d, ff = around(t)
        return remote(qd_send.at[head_at(block, d, ff)], qd_in.at[block0, d0, f], qd_ss.at[0], qd_rs.at[block0],
                      (ff, block * per + d))

    def send_block(block, first):
        @pl.when(lax.div(block, U) == part)
        def _():
            each(first, group, lambda t: kv_copy(block, t).start())
        each(first, group, lambda t: qd_copy(block, t).start())

    pltpu.make_async_copy(kv_send.at[head], kv_in.at[u0, d0, f], kv_rs.at[u0]).start()
    pltpu.make_async_copy(qd_send.at[head], qd_in.at[block0, d0, f], qd_rs.at[block0]).start()
    pl.semaphore_wait(barrier, group - 1 + jnp.where(block0 > 0, 1, 0) + jnp.where(block0 < B - 1, 1, 0))

    @pl.when(block0 > 0)
    def _():
        knock(above, block0 - 1, d0, f)

    @pl.when(block0 < B - 1)
    def _():
        knock(below, block0 + 1, d0, f)

    send_block(block0, 1)
    for n in range(1, B):
        @pl.when(block0 >= n)
        def _():
            pl.semaphore_wait(below, 1)

            @pl.when(block0 < B - 1)
            def _():
                knock(below, block0 + 1, d0, f)
            send_block(block0 - n, 0)

        @pl.when(block0 + n < B)
        def _():
            pl.semaphore_wait(above, 1)

            @pl.when(block0 > 0)
            def _():
                knock(above, block0 - 1, d0, f)
            send_block(block0 + n, 0)

    acc[...] = jnp.zeros_like(acc)
    st_send[...] = jnp.zeros_like(st_send)
    for load in loads:
        load.wait()

    lane1 = lax.broadcasted_iota(jnp.int32, (1, PAIR), 1)
    table = [pieces_of(HIDDEN)] + [pieces_of(math.log(n)) for n in range(1, n_slots + 2)]
    marks = []
    for p in range(F):
        seen = jnp.zeros((1, PAIR), F32)
        unseen = jnp.zeros((1, PAIR), F32)
        for g in range(F):
            own = 1 if p == g else 0
            count = own
            for slot in range(n_slots):
                count = count + jnp.where(part_ref[slot, g] == p, 1, 0)
            for e in range(SPLITS):
                here = lane1 == DH + SPLITS * g + e
                unseen = jnp.where(here, table[own][e], unseen)
                for n in range(own, n_slots + 2):
                    seen = jnp.where(here & (count == n), table[n][e], seen)
        marks.append((seen, unseen))

    lane = lax.broadcasted_iota(jnp.int32, (rows, PAIR), 1)
    row = lax.broadcasted_iota(jnp.int32, (rows, PAIR), 0)
    tall = lax.broadcasted_iota(jnp.int32, (unit, PAIR), 1)
    hot = [jnp.where((lane >= DH + SPLITS * g) & (lane < DH + SPLITS * (g + 1)), 1.0, 0.0) for g in range(F)]

    def take_keys(j):
        u = lax.rem(u0 + j, U)
        here = kv_in.at[u]
        remote(here, here, kv_ss.at[0], kv_rs.at[u], (f, w)).wait_recv()
        aug, raw = [], []
        for d in range(per):
            first = ((part * U + u) * per + d) * rows
            for p in range(F):
                both = kv_in[u, d, p].astype(F32)
                extra = jnp.where(row + first >= reg_ref[p], marks[p][0], marks[p][1])
                raw.append(both)
                aug.append(jnp.where(lane < DH, both, extra))
        raw = jnp.concatenate(raw, axis=0)
        kaug[j] = jnp.concatenate(aug, axis=0).astype(BF)
        vz[j] = jnp.where(tall >= DH, raw, 0.0).astype(BF)
        kt[j] = (raw * scale).T[:DH].astype(BF)

    def take_queries(i):
        here = qd_in.at[i]
        remote(here, here, qd_ss.at[0], qd_rs.at[i], (f, w)).wait_recv()
        raw, aug = [], []
        for d in range(per):
            for g in range(F):
                both = qd_in[i, d, g].astype(F32)
                raw.append(both)
                aug.append(jnp.where(lane < DH, both * scale, hot[g]))
        raw = jnp.concatenate(raw, axis=0)
        qaug[i] = jnp.concatenate(aug, axis=0).astype(BF)
        xraw[i] = raw.astype(BF)
        qdz[i, :QC] = jnp.where(tall < DH, raw * scale, 0.0).astype(BF)
        qdz[i, QC:] = jnp.where(tall >= DH, raw, 0.0).astype(BF)

    def forth(j, i):
        raw = rdot(kaug[j], qaug[i])
        top = jnp.max(raw, axis=0, keepdims=True)
        if j:
            old = top_ref[i]
            top = jnp.maximum(old, top)
        expo = jnp.exp(raw - top)
        dprod = rdot(vz[j], xraw[i])
        sbuf[j, i] = expo
        dpbuf[j, i] = dprod
        tops[j, i] = top
        top_ref[i] = top
        total = jnp.sum(expo, axis=0, keepdims=True)
        dsum = jnp.sum(expo * dprod, axis=0, keepdims=True)
        if j:
            keep = jnp.exp(old - top)
            total = total_ref[i] * keep + total
            dsum = dsum_ref[i] * keep + dsum
        total_ref[i] = total
        dsum_ref[i] = dsum

    spans = [(c, min(c + PAIR, QC)) for c in range(0, QC, PAIR)]

    def give(i):
        for s, ref in enumerate((top_ref, total_ref, dsum_ref)):
            value = ref[i]
            for n, (lo, hi) in enumerate(spans):
                at = s * len(spans) + n
                st_send[i, at:at + 1, :hi - lo] = value[:, lo:hi]
        remote(st_send.at[i], st_in.at[i], st_ss.at[0], st_rs.at[i], (f, other * L + l)).start()

    def meet(i):
        here = st_in.at[i]
        remote(here, here, st_ss.at[0], st_rs.at[i], (f, other * L + l)).wait_recv()
        got = []
        for s in range(3):
            got.append(jnp.concatenate(
                [st_in[i, s * len(spans) + n:s * len(spans) + n + 1, :hi - lo] for n, (lo, hi) in enumerate(spans)],
                axis=1))
        mine = top_ref[i]
        top = jnp.maximum(mine, got[0])
        a, b = jnp.exp(mine - top), jnp.exp(got[0] - top)
        inv = 1.0 / (total_ref[i] * a + got[1] * b)
        top_ref[i] = top
        dsum_ref[i] = (dsum_ref[i] * a + got[2] * b) * inv
        total_ref[i] = inv

    def back(j, i):
        factor = jnp.exp(tops[j, i] - top_ref[i]) * total_ref[i]
        prob = sbuf[j, i] * factor
        dscore = (prob * (dpbuf[j, i] - dsum_ref[i])).astype(BF)
        added = dot(jnp.concatenate([dscore, prob.astype(BF)], axis=1), qdz[i])
        acc[j] += added.reshape(group, rows, PAIR)
        more = dot(kt[j], dscore)
        if j:
            more = dqacc[...] + more
        dqacc[...] = more

    def dq_copy(i, t):
        d, ff = around(t)
        return remote(dq_send.at[i * group + d * F + ff], dq_in.at[part, head], dq_ss.at[0], dq_rs.at[part], (ff, i * per + d))

    def ship_queries(i):
        dqs[...] = jnp.concatenate([dqacc[...], jnp.zeros((DH, QC), F32)], axis=0).T
        for d in range(per):
            for g in range(F):
                base = (d * F + g) * rows
                dq_send[i * group + d * F + g] = jnp.concatenate(
                    [dqs[base:base + half, :DH], dqs[base + rows - half:base + rows, :DH]], axis=1).astype(BF)

        @pl.when(i == block0)
        def _():
            pltpu.make_async_copy(dq_send.at[i * group + d0 * F + f], dq_in.at[part, head], dq_rs.at[part]).start()

        @pl.when(i != block0)
        def _():
            dq_copy(i, 0).start()
        each(1, group, lambda t: dq_copy(i, t).start())

    def fin_copy(j, t):
        d, ff = around(t)
        return remote(fin_send.at[j * group + d * F + ff], fin_in.at[head], fin_ss.at[0], fin_rs.at[0],
                      (ff, (part * U + lax.rem(u0 + j, U)) * per + d))

    def ship_keys(j):
        fin_send[j * group:(j + 1) * group] = acc[j].astype(BF)
        if j == 0:
            pltpu.make_async_copy(fin_send.at[d0 * F + f], fin_in.at[head], fin_rs.at[0]).start()
        each(0 if j else 1, group, lambda t: fin_copy(j, t).start())

    def local(n):
        return part * U + lax.rem(u0 + n, U)

    def remote_block(n):
        return other * U + n + part * (U - 1 - 2 * n)

    edge = jnp.where(part == 0, U - 1, 0) == u0
    order = [local(0)]
    for n in range(U - 1):
        order.append(jnp.where(edge, remote_block(n), local(n + 1)))
        order.append(jnp.where(edge, local(n + 1), remote_block(n)))
    order.append(remote_block(U - 1))

    for n, i in enumerate(order):
        if n == B - 1:
            for e in range(U - 1):
                meet(remote_block(e))
                for j in range(U):
                    back(j, remote_block(e))
                ship_queries(remote_block(e))
        if n:
            take_queries(i)
        for j in range(U):
            if n == 0:
                take_keys(j)
                if j == 0:
                    take_queries(i)
            forth(j, i)
        give(i)
    last = [remote_block(U - 1)] + [part * U + n + other * (U - 1 - 2 * n) for n in range(U)]
    for n, i in enumerate(last):
        meet(i)
        for j in range(U):
            back(j, i)
            if n == U and j == U - 1:
                ship_queries(i)
            if n == U:
                ship_keys(j)
        if n < U:
            ship_queries(i)

    def sent(ref, sem):
        remote(ref, ref, sem.at[0], sem.at[0], (f, w)).wait_send()

    sent(kv_send.at[pl.ds(0, heads - 1)], kv_ss)
    sent(qd_send, qd_ss)
    sent(qd_send.at[pl.ds(0, heads - 1)], qd_ss)
    sent(st_send, st_ss)
    for side in (other, part):
        here = dq_in.at[side]
        remote(here, here, dq_ss.at[0], dq_rs.at[side], (f, w)).wait_recv()
    remote(fin_in, fin_in, fin_ss.at[0], fin_rs.at[0], (f, w)).wait_recv()
    sent(dq_send.at[pl.ds(0, B * group - 1)], dq_ss)
    sent(fin_send.at[pl.ds(0, U * group - 1)], fin_ss)


def both_halves(dq_in, fin_in, dq_out, dk_out, dv_out):
    half, rows, width = dq_in.shape[2], dq_out.shape[1], dq_out.shape[2]
    for j in range(width // PAIR):
        cols = slice(j * PAIR, (j + 1) * PAIR)
        sides = []
        for h in (2 * j, 2 * j + 1):
            got = dq_in[0, h].astype(F32) + dq_in[1, h].astype(F32)
            sides.append(jnp.concatenate([got[:, :DH], got[2 * half - rows:, DH:]], axis=0))
        dq_out[0, :, cols] = jnp.concatenate(sides, axis=1).astype(BF)
        one, two = fin_in[2 * j], fin_in[2 * j + 1]
        dk_out[0, :, cols] = jnp.concatenate([one[:, :DH], two[:, :DH]], axis=1)
        dv_out[0, :, cols] = jnp.concatenate([one[:, DH:], two[:, DH:]], axis=1)


def local_halves(F, W, queries, keys_in, values_in, grad_out, partners, registers):
    _, rows, width = queries.shape
    heads = width // DH
    L = W // 2
    half = ((rows + 1) // 2 + 7) // 8 * 8
    per = next(n for n in range(L, 0, -1) if L % n == 0 and (n == 1 or n * F * rows <= UNIT))
    U = L // per
    unit = per * F * rows
    C = 2 * U
    stats = (3 * ((unit + PAIR - 1) // PAIR) + 7) // 8 * 8
    vm = lambda *shape: pltpu.VMEM(shape, BF)
    vf = lambda *shape: pltpu.VMEM(shape, F32)
    dma = lambda n: pltpu.SemaphoreType.DMA((n,))
    out = jax.ShapeDtypeStruct((1, rows, width), BF)
    dq_heads, kv_heads = pl.pallas_call(
        functools.partial(halves, F, W),
        out_shape=(jax.ShapeDtypeStruct((2, heads, half, PAIR), BF), jax.ShapeDtypeStruct((heads, rows, PAIR), BF)),
        in_specs=[pl.BlockSpec(memory_space=pl.ANY)] * 6,
        out_specs=(pl.BlockSpec(memory_space=pl.ANY),) * 2,
        scratch_shapes=[
            pltpu.SMEM(partners.T.shape, jnp.int32), pltpu.SMEM(registers.shape, jnp.int32),
            vm(1, rows, width), vm(1, rows, width), vm(1, rows, width), vm(1, rows, width),
            vm(heads, rows, PAIR), vm(heads, rows, PAIR), vm(U, per, F, rows, PAIR), vm(C, per, F, rows, PAIR),
            vm(U, unit, PAIR), vm(U, unit, PAIR), vm(U, DH, unit),
            vm(C, unit, PAIR), vm(C, unit, PAIR), vm(C, 2 * unit, PAIR),
            vf(U, C, unit, unit), vf(U, C, unit, unit), vf(U, per * F, rows, PAIR),
            vf(DH, unit), vf(unit, PAIR),
            vf(U, C, 1, unit), vf(C, 1, unit), vf(C, 1, unit), vf(C, 1, unit),
            vf(C, stats, PAIR), vf(C, stats, PAIR),
            vm(heads, rows, PAIR), vm(C * per * F, half, PAIR),
            dma(6), dma(1), dma(U), dma(1), dma(C), dma(1), dma(C), dma(1), dma(2), dma(1), dma(1),
            pltpu.SemaphoreType.REGULAR, pltpu.SemaphoreType.REGULAR,
        ],
        compiler_params=pltpu.CompilerParams(
            collective_id=0, has_side_effects=True, vmem_limit_bytes=60 * 2 ** 20),
    )(partners.T, registers, queries, keys_in, values_in, grad_out)
    return pl.pallas_call(
        both_halves,
        out_shape=(out, out, out),
        in_specs=[pl.BlockSpec(memory_space=pltpu.VMEM)] * 2,
        out_specs=(pl.BlockSpec(memory_space=pltpu.VMEM),) * 3,
    )(dq_heads, kv_heads)


def choose(F, W, queries, *others):
    _, rows, width = queries.shape
    heads = width // DH
    held = 2 * F * W // 2 * rows * F * W * rows * 4
    if W % 2 == 0 and F * W == 2 * heads and SPLITS * F <= DH and held <= 24 * 2 ** 20:
        return local_halves(F, W, queries, *others)
    return local(F, W, queries, *others)


def solution(mesh):
    spec = P("frame", "within", None)
    return jax.shard_map(
        functools.partial(choose, mesh.shape["frame"], mesh.shape["within"]),
        mesh=mesh,
        in_specs=(spec, spec, spec, spec, P(), P()),
        out_specs=(spec, spec, spec),
        check_vma=False,
    )
```

```python
import functools
import math

import jax
import jax.numpy as jnp
import numpy as np
from jax import lax
from jax.experimental import pallas as pl
from jax.experimental.pallas import tpu as pltpu
from jax.sharding import PartitionSpec as P

DH = 64
PAIR = 2 * DH
SPLITS = 3
UNIT = 640
TILE = 256
SUB = 96
HIDDEN = -1e30
BF = jnp.bfloat16
F32 = jnp.float32
MESH = pl.DeviceIdType.MESH


def pieces_of(value):
    left, out = float(value), []
    for _ in range(SPLITS):
        part = float(np.asarray(left, dtype=jnp.bfloat16))
        out.append(part)
        left = left - part if abs(value) < 1e20 else 0.0
    return out


def rdot(a, b):
    return lax.dot_general(a, b, (((1,), (1,)), ((), ())), preferred_element_type=F32)


def dot(a, b):
    return jnp.dot(a, b, preferred_element_type=F32)


def each(lo, hi, do):
    def step(t, carry):
        do(t)
        return carry
    lax.fori_loop(lo, hi, step, 0)


def kernel(F, W, R, QC, inline, part_ref, reg_ref, q_ref, k_ref, v_ref, d_ref, dq_in, fin_in,
           kv_send, qd_send, kv_in, qd_in, kaug, vz, kt, qaug, xraw, qdz, sbuf, dpbuf, acc, dqacc, dqs,
           tops, top_ref, total_ref, dsum_ref,
           red_send, red_in, fin_send, dq_send, own_sem,
           kv_ss, fw_ss, kv_rs, qd_ss, qd_rs, red_ss, red_rs, fin_ss, fin_rs, dq_ss, dq_rs):
    fs = F // R
    hf = F // 2
    rows = q_ref.shape[1]
    width = q_ref.shape[2]
    seq = rows * W
    n_slots = part_ref.shape[0]
    scale = DH ** -0.5
    half = dq_send.shape[2]
    nq = R * seq
    n_chunks = nq // QC
    n_units, per = acc.shape[0], acc.shape[1]
    unit = per * F * rows
    f = lax.axis_index("frame")
    w = lax.axis_index("within")
    c = lax.rem(f, fs)
    a0 = lax.div(f, fs)
    sib = f + 1 - 2 * lax.rem(f, 2)
    head = w * R + a0

    barrier = pltpu.get_barrier_semaphore()

    def ahead(dw):
        return lax.rem(w + W - dw, W)

    def behind(dw):
        return lax.rem(w + dw, W)

    def greet(t):
        pl.semaphore_signal(barrier, inc=1, device_id=(lax.rem(f + 2 * lax.rem(t, hf), F), ahead(lax.div(t, hf))),
                            device_id_type=MESH)

    each(1, hf * W, greet)
    for dc in range(1, fs, 2):
        pl.semaphore_signal(barrier, inc=1, device_id=(a0 * fs + lax.rem(c + dc, fs), w), device_id_type=MESH)

    for first, second, out in ((q_ref, d_ref, qd_send), (k_ref, v_ref, kv_send)):
        for j in range(width // PAIR):
            cols = slice(j * PAIR, (j + 1) * PAIR)
            one = first[0, :, cols]
            two = second[0, :, cols]
            out[2 * j] = jnp.concatenate([one[:, :DH], two[:, :DH]], axis=1)
            out[2 * j + 1] = jnp.concatenate([one[:, DH:], two[:, DH:]], axis=1)
    kv_in[f, w] = kv_send[head]
    qd_in[a0, w] = qd_send[head]

    pl.semaphore_wait(barrier, hf * W - 1 + fs // 2)

    def kv_copy(t):
        ff = lax.rem(f + 2 * lax.rem(t, hf), F)
        ww = ahead(lax.div(t, hf))
        return pltpu.make_async_remote_copy(
            src_ref=kv_send.at[ww * R + lax.div(ff, fs)], dst_ref=kv_in.at[f, w],
            send_sem=kv_ss.at[t], recv_sem=kv_rs.at[f * W + w],
            device_id=(ff, ww), device_id_type=MESH)

    def pass_on(origin, t):
        ff = lax.rem(origin + F - 2 * lax.rem(t, hf), F)
        ww = behind(lax.div(t, hf))
        return pltpu.make_async_remote_copy(
            src_ref=kv_in.at[ff, ww], dst_ref=kv_in.at[ff, ww],
            send_sem=fw_ss.at[t], recv_sem=kv_rs.at[ff * W + ww],
            device_id=(sib, w), device_id_type=MESH)

    def qd_copy(t):
        aa, ww = lax.rem(a0 + lax.rem(t, R), R), ahead(lax.div(t, R))
        return pltpu.make_async_remote_copy(
            src_ref=qd_send.at[ww * R + aa], dst_ref=qd_in.at[a0, w],
            send_sem=qd_ss.at[t], recv_sem=qd_rs.at[a0 * W + w],
            device_id=(aa * fs + c, ww), device_id_type=MESH)

    def arrival(t, buffer, send, recv, index, source):
        return pltpu.make_async_remote_copy(
            src_ref=buffer.at[index], dst_ref=buffer.at[index], send_sem=send.at[t], recv_sem=recv,
            device_id=source, device_id_type=MESH)

    def qd_arrival(t):
        aa, ww = lax.rem(a0 + R - lax.rem(t, R), R), behind(lax.div(t, R))
        return arrival(t, qd_in, qd_ss, qd_rs.at[aa * W + ww], (aa, ww), (aa * fs + c, ww))

    def head_arrival(t, buffer, send, recv):
        aa, ww = lax.rem(a0 + R - lax.rem(t, R), R), ahead(lax.div(t, R))
        return arrival(t, buffer, send, recv.at[ww * R + aa], (ww * R + aa,), (aa * fs + c, ww))

    each(1, R * W, lambda t: qd_copy(t).start())
    pass_on(f, 0).start()
    each(1, hf * W, lambda t: kv_copy(t).start())

    acc[...] = jnp.zeros_like(acc)
    dqacc[...] = jnp.zeros_like(dqacc)

    def relay(t):
        move = pass_on(f, t)
        move.wait_recv()
        move.start()

    lane1 = lax.broadcasted_iota(jnp.int32, (1, PAIR), 1)
    table = [pieces_of(HIDDEN)] + [pieces_of(math.log(n)) for n in range(1, n_slots + 2)]
    marks = []
    for p in range(F):
        seen = jnp.zeros((1, PAIR), F32)
        unseen = jnp.zeros((1, PAIR), F32)
        for gi in range(R):
            g = c + fs * gi
            own = jnp.where(p == g, 1, 0)
            count = own
            for slot in range(n_slots):
                count = count + jnp.where(part_ref[slot, g] == p, 1, 0)
            for e in range(SPLITS):
                here = lane1 == DH + SPLITS * gi + e
                for n in range(n_slots + 2):
                    if n < 2:
                        unseen = jnp.where(here & (own == n), table[n][e], unseen)
                    seen = jnp.where(here & (count == n), table[n][e], seen)
        marks.append((seen, unseen))

    lane = lax.broadcasted_iota(jnp.int32, (rows, PAIR), 1)
    row = lax.broadcasted_iota(jnp.int32, (rows, PAIR), 0)

    def prepare(u):
        aug, raw = [], []
        for d in range(per):
            ww = behind(u * per + d)
            for p in range(F):
                both = kv_in[p, ww].astype(F32)
                extra = jnp.where(row + ww * rows >= reg_ref[p], marks[p][0], marks[p][1])
                raw.append(both)
                aug.append(jnp.where(lane < DH, both, extra))
        raw = jnp.concatenate(raw, axis=0)
        keep = lax.broadcasted_iota(jnp.int32, (unit, PAIR), 1) >= DH
        kaug[u] = jnp.concatenate(aug, axis=0).astype(BF)
        vz[u] = jnp.where(keep, raw, 0.0).astype(BF)
        kt[u] = (raw * scale).T[:DH].astype(BF)

    def direct(u):
        each(max(u * per * hf, 1), (u + 1) * per * hf, relay)

    def settle(u):
        each(u * per * hf, (u + 1) * per * hf, lambda t: pass_on(sib, t).wait_recv())
        prepare(u)

    def rows_of(i):
        return pl.ds(pl.multiple_of(i * QC, QC), QC)

    def begin(b):
        top_ref[b] = jnp.full_like(top_ref[b], -3e38)
        total_ref[b] = jnp.zeros_like(total_ref[b])
        dsum_ref[b] = jnp.zeros_like(dsum_ref[b])

    def forth(u, i, b):
        at = rows_of(i)
        raw = rdot(kaug[u], qaug[at])
        old = top_ref[b]
        top = jnp.maximum(old, jnp.max(raw, axis=0, keepdims=True))
        keep = jnp.exp(old - top)
        expo = jnp.exp(raw - top)
        dprod = rdot(vz[u], xraw[at])
        sbuf[u, b] = expo
        dpbuf[u, b] = dprod
        tops[u, b] = top
        top_ref[b] = top
        total_ref[b] = total_ref[b] * keep + jnp.sum(expo, axis=0, keepdims=True)
        dsum_ref[b] = dsum_ref[b] * keep + jnp.sum(expo * dprod, axis=0, keepdims=True)

    def back(u, i, b):
        inv = 1.0 / total_ref[b]
        factor = jnp.exp(tops[u, b] - top_ref[b]) * inv
        prob = sbuf[u, b] * factor
        dscore = (prob * (dpbuf[u, b] - dsum_ref[b] * inv)).astype(BF)
        added = dot(jnp.concatenate([dscore, prob.astype(BF)], axis=1), qdz[i])
        acc[u] += added.reshape(per, F, rows, PAIR)
        dqacc[i] += dot(kt[u], dscore)

    def own_copy(block, buffer, n):
        return pltpu.make_async_copy(block, buffer.at[head], own_sem.at[n])

    def red_copy(u, dc):
        return pltpu.make_async_remote_copy(
            src_ref=red_send.at[u, dc - 1], dst_ref=red_in.at[u, dc - 1],
            send_sem=red_ss.at[u * (fs - 1) + dc - 1], recv_sem=red_rs.at[u * (fs - 1) + dc - 1],
            device_id=(a0 * fs + lax.rem(c + dc, fs), w), device_id_type=MESH)

    def ship_part(u):
        for dc in range(1, fs):
            for gi in range(R):
                red_send[u, dc - 1, gi] = acc[u, :, lax.rem(c + dc, fs) + fs * gi].astype(BF)
            red_copy(u, dc).start()

    def fin_copy(t):
        dw = lax.div(t, R)
        aa, ww = lax.rem(a0 + lax.rem(t, R), R), behind(dw)
        return pltpu.make_async_remote_copy(
            src_ref=fin_send.at[lax.div(dw, per), aa, lax.rem(dw, per)], dst_ref=fin_in.at[head],
            send_sem=fin_ss.at[t], recv_sem=fin_rs.at[head],
            device_id=(aa * fs + c, ww), device_id_type=MESH)

    def ship_home(u):
        for dc in range(1, fs):
            red_copy(u, dc).wait_recv()
        for gi in range(R):
            whole = acc[u, :, c + fs * gi]
            for dc in range(1, fs):
                whole = whole + red_in[u, dc - 1, gi].astype(F32)
            fin_send[u, gi] = whole.astype(BF)
        if u == 0:
            own_copy(fin_send.at[0, a0, 0], fin_in, 0).start()
        each(max(u * per * R, 1), (u + 1) * per * R, lambda t: fin_copy(t).start())

    def take_queries():
        each(1, R * W, lambda t: qd_arrival(t).wait_recv())
        wide = lax.broadcasted_iota(jnp.int32, (nq, PAIR), 1)
        tall = lax.broadcasted_iota(jnp.int32, (nq, PAIR), 0)
        both = qd_in[...].astype(F32).reshape(nq, PAIR)
        mark = jnp.zeros((nq, PAIR), F32)
        for gi in range(R):
            mine = (tall >= gi * seq) & (tall < (gi + 1) * seq)
            mark = jnp.where(mine & (wide >= DH + SPLITS * gi) & (wide < DH + SPLITS * (gi + 1)), 1.0, mark)
        scaled = both * scale
        qaug[...] = jnp.where(wide < DH, scaled, mark).astype(BF)
        xraw[...] = both.astype(BF)
        qdz[:, :QC] = jnp.where(wide < DH, scaled, 0.0).astype(BF).reshape(n_chunks, QC, PAIR)
        qdz[:, QC:] = jnp.where(wide >= DH, both, 0.0).astype(BF).reshape(n_chunks, QC, PAIR)

    take_queries()
    if inline:
        each(0, n_chunks, begin)
        direct(0)
        for u in range(n_units):
            settle(u)
            forth(u, 0, 0)
            if u + 1 < n_units:
                direct(u + 1)
            each(1, n_chunks, lambda i: forth(u, i, i))
        for u in range(n_units):
            back(u, 0, 0)
            if u:
                ship_home(u - 1)
            each(1, n_chunks, lambda i: back(u, i, i))
            ship_part(u)
    else:
        for u in range(n_units):
            direct(u)
        for u in range(n_units):
            settle(u)

        def block(i):
            begin(0)
            each(0, n_units, lambda u: forth(u, i, 0))
            each(0, n_units, lambda u: back(u, i, 0))

        each(0, n_chunks, block)
        for u in range(n_units):
            ship_part(u)
        for u in range(n_units - 1):
            ship_home(u)

    def dq_copy(t):
        aa, ww = lax.rem(a0 + lax.rem(t, R), R), behind(lax.div(t, R))
        return pltpu.make_async_remote_copy(
            src_ref=dq_send.at[aa, ww], dst_ref=dq_in.at[head],
            send_sem=dq_ss.at[t], recv_sem=dq_rs.at[head],
            device_id=(aa * fs + c, ww), device_id_type=MESH)

    for i in range(n_chunks):
        dqs[i * QC:(i + 1) * QC] = jnp.concatenate([dqacc[i], jnp.zeros((DH, QC), F32)], axis=0).T
    for gi in range(R):
        for ww in range(W):
            base = gi * seq + ww * rows
            dq_send[gi, ww] = jnp.concatenate(
                [dqs[base:base + half, :DH], dqs[base + rows - half:base + rows, :DH]], axis=1).astype(BF)
    own_copy(dq_send.at[a0, w], dq_in, 1).start()
    each(1, R * W, lambda t: dq_copy(t).start())
    ship_home(n_units - 1)

    each(1, R * W, lambda t: head_arrival(t, dq_in, dq_ss, dq_rs).wait_recv())
    each(1, R * W, lambda t: head_arrival(t, fin_in, fin_ss, fin_rs).wait_recv())
    each(1, hf * W, lambda t: kv_copy(t).wait_send())
    each(0, hf * W, lambda t: pass_on(f, t).wait_send())
    each(1, R * W, lambda t: qd_copy(t).wait_send())
    own_copy(fin_send.at[0, a0, 0], fin_in, 0).wait()
    own_copy(dq_send.at[a0, w], dq_in, 1).wait()
    each(1, R * W, lambda t: dq_copy(t).wait_send())
    each(1, R * W, lambda t: fin_copy(t).wait_send())
    for u in range(n_units):
        for dc in range(1, fs):
            red_copy(u, dc).wait_send()


def tokens_again(dq_in, fin_in, dq_out, dk_out, dv_out):
    half, rows, width = dq_in.shape[1], dq_out.shape[1], dq_out.shape[2]
    for j in range(width // PAIR):
        cols = slice(j * PAIR, (j + 1) * PAIR)
        sides = []
        for h in (2 * j, 2 * j + 1):
            got = dq_in[h].astype(F32)
            sides.append(jnp.concatenate([got[:, :DH], got[2 * half - rows:, DH:]], axis=0))
        dq_out[0, :, cols] = jnp.concatenate(sides, axis=1).astype(BF)

    for j in range(width // PAIR):
        cols = slice(j * PAIR, (j + 1) * PAIR)
        one, two = fin_in[2 * j], fin_in[2 * j + 1]
        dk_out[0, :, cols] = jnp.concatenate([one[:, :DH], two[:, :DH]], axis=1)
        dv_out[0, :, cols] = jnp.concatenate([one[:, DH:], two[:, DH:]], axis=1)


def local(F, W, queries, keys_in, values_in, grad_out, partners, registers):
    _, rows, width = queries.shape
    heads = width // DH
    R = heads // W
    fs = F // R
    seq = rows * W
    nq = R * seq
    half = ((rows + 1) // 2 + 7) // 8 * 8
    inline = F * seq * nq * 8 <= 24 * 2 ** 20
    QC = next(b for b in ((576, 384, 128) if inline else (128,)) if nq % b == 0)
    held = nq // QC if inline else 1
    per = next(n for n in range(W, 0, -1) if W % n == 0 and (n == 1 or n * F * rows <= UNIT))
    units = W // per
    unit = per * F * rows
    vm = lambda *shape: pltpu.VMEM(shape, BF)
    vf = lambda *shape: pltpu.VMEM(shape, F32)
    dma = lambda n: pltpu.SemaphoreType.DMA((n,))
    out = jax.ShapeDtypeStruct((1, rows, width), BF)
    dq_heads, kv_heads = pl.pallas_call(
        functools.partial(kernel, F, W, R, QC, inline),
        out_shape=(jax.ShapeDtypeStruct((heads, half, PAIR), BF), jax.ShapeDtypeStruct((heads, rows, PAIR), BF)),
        in_specs=[pl.BlockSpec(memory_space=pltpu.SMEM)] * 2 + [pl.BlockSpec(memory_space=pltpu.VMEM)] * 4,
        out_specs=(pl.BlockSpec(memory_space=pl.ANY),) * 2,
        scratch_shapes=[
            vm(heads, rows, PAIR), vm(heads, rows, PAIR),
            vm(F, W, rows, PAIR), vm(R, W, rows, PAIR),
            vm(units, unit, PAIR), vm(units, unit, PAIR), vm(units, DH, unit),
            vm(nq, PAIR), vm(nq, PAIR), vm(nq // QC, 2 * QC, PAIR),
            vf(units, held, unit, QC), vf(units, held, unit, QC), vf(units, per, F, rows, PAIR),
            vf(nq // QC, DH, QC), vf(nq, PAIR),
            vf(units, held, 1, QC), vf(held, 1, QC), vf(held, 1, QC), vf(held, 1, QC),
            vm(units, fs - 1, R, per, rows, PAIR), vm(units, fs - 1, R, per, rows, PAIR),
            vm(units, R, per, rows, PAIR), vm(R, W, half, PAIR), dma(2),
            dma(F // 2 * W), dma(F // 2 * W), dma(F * W), dma(R * W), dma(R * W),
            dma(units * (fs - 1)), dma(units * (fs - 1)), dma(R * W), dma(heads), dma(R * W), dma(heads),
        ],
        compiler_params=pltpu.CompilerParams(
            collective_id=0, has_side_effects=True, vmem_limit_bytes=60 * 2 ** 20),
    )(partners.T, registers, queries, keys_in, values_in, grad_out)
    return pl.pallas_call(
        tokens_again,
        out_shape=(out, out, out),
        in_specs=[pl.BlockSpec(memory_space=pltpu.VMEM)] * 2,
        out_specs=(pl.BlockSpec(memory_space=pltpu.VMEM),) * 3,
    )(dq_heads, kv_heads)


def halves(F, W, part_hbm, reg_hbm, q_hbm, k_hbm, v_hbm, d_hbm, dq_in, fin_in,
           part_ref, reg_ref, q_ref, k_ref, v_ref, d_ref, kv_send, qd_send, kv_in, qd_in,
           kaug, vz, kt, qaug, xraw, qdz, sbuf, dpbuf, acc, dqacc, dqs,
           tops, top_ref, total_ref, dsum_ref, st_send, st_in, fin_send, dq_send,
           in_sem, kv_ss, kv_rs, qd_ss, qd_rs, st_ss, st_rs, dq_ss, dq_rs, fin_ss, fin_rs, below, above):
    rows, width = q_ref.shape[1], q_ref.shape[2]
    n_slots = part_ref.shape[0]
    U, per = kv_in.shape[0], kv_in.shape[1]
    L = U * per
    B = 2 * U
    heads = F * L
    group = per * F
    unit = group * rows
    QP = qaug.shape[1]
    tiles = [(c, min(c + TILE, QP)) for c in range(0, QP, TILE)]
    n_subs = tops.shape[2]
    sub = unit // n_subs
    scale = DH ** -0.5
    half = dq_send.shape[1]
    f = lax.axis_index("frame")
    w = lax.axis_index("within")
    block0 = lax.div(w, per)
    d0 = lax.rem(w, per)
    part = lax.div(block0, U)
    other = 1 - part
    u0 = lax.rem(block0, U)
    l = u0 * per + d0
    head = f * L + l

    barrier = pltpu.get_barrier_semaphore()

    def around(t):
        return lax.rem(d0 + lax.div(t, F), per), lax.rem(f + lax.rem(t, F), F)

    def knock(sem, block, d, ff):
        pl.semaphore_signal(sem, inc=1, device_id=(ff, block * per + d), device_id_type=MESH)

    def greet(t):
        d, ff = around(group - t)
        knock(barrier, block0, d, ff)

    @pl.when(block0 > 0)
    def _():
        knock(barrier, block0 - 1, d0, f)

    @pl.when(block0 < B - 1)
    def _():
        knock(barrier, block0 + 1, d0, f)

    each(1, group, greet)
    loads = [pltpu.make_async_copy(src, dst, in_sem.at[n]) for n, (src, dst) in enumerate(
        ((k_hbm, k_ref), (v_hbm, v_ref), (q_hbm, q_ref), (d_hbm, d_ref), (part_hbm, part_ref), (reg_hbm, reg_ref)))]
    for load in loads:
        load.start()

    for first, second, out in ((k_ref, v_ref, kv_send), (q_ref, d_ref, qd_send)):
        for load in (loads.pop(0), loads.pop(0)):
            load.wait()
        for j in range(width // PAIR):
            cols = slice(j * PAIR, (j + 1) * PAIR)
            one = first[0, :, cols]
            two = second[0, :, cols]
            out[2 * j] = jnp.concatenate([one[:, :DH], two[:, :DH]], axis=1)
            out[2 * j + 1] = jnp.concatenate([one[:, DH:], two[:, DH:]], axis=1)

    def remote(src, dst, ss, rs, device):
        return pltpu.make_async_remote_copy(src_ref=src, dst_ref=dst, send_sem=ss, recv_sem=rs,
                                            device_id=device, device_id_type=MESH)

    def head_at(block, d, ff):
        return ff * L + lax.rem(block, U) * per + d

    def kv_copy(block, t):
        d, ff = around(t)
        return remote(kv_send.at[head_at(block, d, ff)], kv_in.at[u0, d0, f], kv_ss.at[0], kv_rs.at[u0],
                      (ff, block * per + d))

    def qd_copy(block, t):
        d, ff = around(t)
        return remote(qd_send.at[head_at(block, d, ff)], qd_in.at[block0, d0, f], qd_ss.at[0], qd_rs.at[block0],
                      (ff, block * per + d))

    def send_block(block, first):
        @pl.when(lax.div(block, U) == part)
        def _():
            each(first, group, lambda t: kv_copy(block, t).start())
        each(first, group, lambda t: qd_copy(block, t).start())

    pltpu.make_async_copy(kv_send.at[head], kv_in.at[u0, d0, f], kv_rs.at[u0]).start()
    pltpu.make_async_copy(qd_send.at[head], qd_in.at[block0, d0, f], qd_rs.at[block0]).start()
    pl.semaphore_wait(barrier, group - 1 + jnp.where(block0 > 0, 1, 0) + jnp.where(block0 < B - 1, 1, 0))

    @pl.when(block0 > 0)
    def _():
        knock(above, block0 - 1, d0, f)

    @pl.when(block0 < B - 1)
    def _():
        knock(below, block0 + 1, d0, f)

    send_block(block0, 1)
    for n in range(1, B):
        @pl.when(block0 >= n)
        def _():
            pl.semaphore_wait(below, 1)

            @pl.when(block0 < B - 1)
            def _():
                knock(below, block0 + 1, d0, f)
            send_block(block0 - n, 0)

        @pl.when(block0 + n < B)
        def _():
            pl.semaphore_wait(above, 1)

            @pl.when(block0 > 0)
            def _():
                knock(above, block0 - 1, d0, f)
            send_block(block0 + n, 0)

    acc[...] = jnp.zeros_like(acc)
    st_send[...] = jnp.zeros_like(st_send)
    if QP > unit:
        for ref, first in ((qaug, unit), (xraw, unit), (qdz, unit), (qdz, QP + unit)):
            ref[:, first:first + QP - unit] = jnp.zeros((B, QP - unit, PAIR), BF)
    for load in loads:
        load.wait()

    lane1 = lax.broadcasted_iota(jnp.int32, (1, PAIR), 1)
    table = [pieces_of(HIDDEN)] + [pieces_of(math.log(n)) for n in range(1, n_slots + 2)]
    marks = []
    for p in range(F):
        seen = jnp.zeros((1, PAIR), F32)
        unseen = jnp.zeros((1, PAIR), F32)
        for g in range(F):
            own = 1 if p == g else 0
            count = own
            for slot in range(n_slots):
                count = count + jnp.where(part_ref[slot, g] == p, 1, 0)
            for e in range(SPLITS):
                here = lane1 == DH + SPLITS * g + e
                unseen = jnp.where(here, table[own][e], unseen)
                for n in range(own, n_slots + 2):
                    seen = jnp.where(here & (count == n), table[n][e], seen)
        marks.append((seen, unseen))

    lane = lax.broadcasted_iota(jnp.int32, (rows, PAIR), 1)
    row = lax.broadcasted_iota(jnp.int32, (rows, PAIR), 0)
    tall = lax.broadcasted_iota(jnp.int32, (unit, PAIR), 1)
    hot = [jnp.where((lane >= DH + SPLITS * g) & (lane < DH + SPLITS * (g + 1)), 1.0, 0.0) for g in range(F)]

    def take_keys(j):
        u = lax.rem(u0 + j, U)
        here = kv_in.at[u]
        remote(here, here, kv_ss.at[0], kv_rs.at[u], (f, w)).wait_recv()
        aug, raw = [], []
        for d in range(per):
            first = ((part * U + u) * per + d) * rows
            for p in range(F):
                both = kv_in[u, d, p].astype(F32)
                extra = jnp.where(row + first >= reg_ref[p], marks[p][0], marks[p][1])
                raw.append(both)
                aug.append(jnp.where(lane < DH, both, extra))
        raw = jnp.concatenate(raw, axis=0)
        kaug[j] = jnp.concatenate(aug, axis=0).astype(BF)
        vz[j] = jnp.where(tall >= DH, raw, 0.0).astype(BF)
        kt[j] = (raw * scale).T[:DH].astype(BF)

    def take_queries(i):
        here = qd_in.at[i]
        remote(here, here, qd_ss.at[0], qd_rs.at[i], (f, w)).wait_recv()
        raw, aug = [], []
        for d in range(per):
            for g in range(F):
                both = qd_in[i, d, g].astype(F32)
                raw.append(both)
                aug.append(jnp.where(lane < DH, both * scale, hot[g]))
        raw = jnp.concatenate(raw, axis=0)
        qaug[i, :unit] = jnp.concatenate(aug, axis=0).astype(BF)
        xraw[i, :unit] = raw.astype(BF)
        qdz[i, :unit] = jnp.where(tall < DH, raw * scale, 0.0).astype(BF)
        qdz[i, QP:QP + unit] = jnp.where(tall >= DH, raw, 0.0).astype(BF)

    def forth(j, i):
        for lo, hi in tiles:
            raw = rdot(kaug[j], qaug[i, lo:hi])
            dprod = rdot(vz[j], xraw[i, lo:hi])
            if j:
                top, total, dsum = top_ref[i, :, lo:hi], total_ref[i, :, lo:hi], dsum_ref[i, :, lo:hi]
            for s in range(n_subs):
                at = slice(s * sub, (s + 1) * sub)
                part_raw = raw[at].reshape(sub // 8, 8, hi - lo)
                part_dp = dprod[at].reshape(sub // 8, 8, hi - lo)
                peak = jnp.max(part_raw, axis=0)
                if j or s:
                    peak = jnp.maximum(top, peak)
                expo = jnp.exp(part_raw - peak[None])
                more, dmore = jnp.sum(expo, axis=0), jnp.sum(expo * part_dp, axis=0)
                if j or s:
                    keep = jnp.exp(top - peak)
                    more, dmore = total * keep + more, dsum * keep + dmore
                top, total, dsum = peak, more, dmore
                sbuf[j, i, at, lo:hi] = expo.reshape(sub, hi - lo)
                dpbuf[j, i, at, lo:hi] = part_dp.reshape(sub, hi - lo)
                tops[j, i, s, :, lo:hi] = peak
            top_ref[i, :, lo:hi] = top
            total_ref[i, :, lo:hi] = total
            dsum_ref[i, :, lo:hi] = dsum

    spans = [(c, c + PAIR) for c in range(0, QP, PAIR)]

    def give(i):
        peak = jnp.max(top_ref[i], axis=0, keepdims=True)
        keep = jnp.exp(top_ref[i] - peak)
        total = jnp.sum(total_ref[i] * keep, axis=0, keepdims=True)
        dsum = jnp.sum(dsum_ref[i] * keep, axis=0, keepdims=True)
        for s, value in enumerate((peak, total, dsum)):
            for n, (lo, hi) in enumerate(spans):
                at = s * len(spans) + n
                st_send[i, at:at + 1] = value[:, lo:hi]
        remote(st_send.at[i], st_in.at[i], st_ss.at[0], st_rs.at[i], (f, other * L + l)).start()

    def meet(i):
        here = st_in.at[i]
        remote(here, here, st_ss.at[0], st_rs.at[i], (f, other * L + l)).wait_recv()
        def row_of(ref, s):
            return jnp.concatenate(
                [ref[i, s * len(spans) + n:s * len(spans) + n + 1] for n in range(len(spans))], axis=1)

        mine, yours = [[row_of(ref, s) for s in range(3)] for ref in (st_send, st_in)]
        peak = jnp.maximum(mine[0], yours[0])
        a, b = jnp.exp(mine[0] - peak), jnp.exp(yours[0] - peak)
        inv = 1.0 / (mine[1] * a + yours[1] * b)
        whole = (8, QP)
        top_ref[i] = jnp.broadcast_to(peak, whole)
        total_ref[i] = jnp.broadcast_to(inv, whole)
        dsum_ref[i] = jnp.broadcast_to((mine[2] * a + yours[2] * b) * inv, whole)

    def back(j, i):
        probs, dscores = [], []
        for s in range(n_subs):
            at = slice(s * sub, (s + 1) * sub)
            factor = jnp.exp(tops[j, i, s] - top_ref[i]) * total_ref[i]
            prob = sbuf[j, i, at].reshape(sub // 8, 8, QP) * factor[None]
            dscore = prob * (dpbuf[j, i, at].reshape(sub // 8, 8, QP) - dsum_ref[i][None])
            probs.append(prob.reshape(sub, QP).astype(BF))
            dscores.append(dscore.reshape(sub, QP).astype(BF))
        dscore = jnp.concatenate(dscores, axis=0)
        added = dot(jnp.concatenate([dscore, jnp.concatenate(probs, axis=0)], axis=1), qdz[i])
        acc[j] += added.reshape(group, rows, PAIR)
        more = dot(kt[j], dscore)
        if j < U - 1:
            more = dqacc[...] + more
        dqacc[...] = more

    def dq_copy(i, t):
        d, ff = around(t)
        return remote(dq_send.at[i * group + d * F + ff], dq_in.at[part, head], dq_ss.at[0], dq_rs.at[part], (ff, i * per + d))

    def ship_queries(i):
        dqs[...] = jnp.concatenate([dqacc[...], jnp.zeros((DH, QP), F32)], axis=0).T
        for d in range(per):
            for g in range(F):
                base = (d * F + g) * rows
                dq_send[i * group + d * F + g] = jnp.concatenate(
                    [dqs[base:base + half, :DH], dqs[base + rows - half:base + rows, :DH]], axis=1).astype(BF)

        @pl.when(i == block0)
        def _():
            pltpu.make_async_copy(dq_send.at[i * group + d0 * F + f], dq_in.at[part, head], dq_rs.at[part]).start()

        @pl.when(i != block0)
        def _():
            dq_copy(i, 0).start()
        each(1, group, lambda t: dq_copy(i, t).start())

    def fin_copy(j, t):
        d, ff = around(t)
        return remote(fin_send.at[j * group + d * F + ff], fin_in.at[head], fin_ss.at[0], fin_rs.at[0],
                      (ff, (part * U + lax.rem(u0 + j, U)) * per + d))

    def ship_keys(j):
        fin_send[j * group:(j + 1) * group] = acc[j].astype(BF)
        if j == 0:
            pltpu.make_async_copy(fin_send.at[d0 * F + f], fin_in.at[head], fin_rs.at[0]).start()
        each(0 if j else 1, group, lambda t: fin_copy(j, t).start())

    def local(n):
        return part * U + lax.rem(u0 + n, U)

    def remote_block(n):
        return other * U + n + part * (U - 1 - 2 * n)

    edge = jnp.where(part == 0, U - 1, 0) == u0
    order = [local(0)]
    for n in range(U - 1):
        order.append(jnp.where(edge, remote_block(n), local(n + 1)))
        order.append(jnp.where(edge, local(n + 1), remote_block(n)))
    order.append(remote_block(U - 1))

    for n, i in enumerate(order):
        if n:
            take_queries(i)
        for j in range(U):
            if n == 0:
                take_keys(j)
                if j == 0:
                    take_queries(i)
            forth(j, i)
        give(i)
    last = [remote_block(n) for n in range(U)] + [local(n) for n in reversed(range(U))]
    for n, i in enumerate(last):
        meet(i)
        for j in reversed(range(U)):
            back(j, i)
            if n == B - 1 and j:
                ship_keys(j)
        ship_queries(i)
    ship_keys(0)

    def sent(ref, sem):
        remote(ref, ref, sem.at[0], sem.at[0], (f, w)).wait_send()

    sent(kv_send.at[pl.ds(0, heads - 1)], kv_ss)
    sent(qd_send, qd_ss)
    sent(qd_send.at[pl.ds(0, heads - 1)], qd_ss)
    sent(st_send, st_ss)
    for side in (other, part):
        here = dq_in.at[side]
        remote(here, here, dq_ss.at[0], dq_rs.at[side], (f, w)).wait_recv()
    remote(fin_in, fin_in, fin_ss.at[0], fin_rs.at[0], (f, w)).wait_recv()
    sent(dq_send.at[pl.ds(0, B * group - 1)], dq_ss)
    sent(fin_send.at[pl.ds(0, U * group - 1)], fin_ss)


def both_halves(dq_in, fin_in, dq_out, dk_out, dv_out):
    half, rows, width = dq_in.shape[2], dq_out.shape[1], dq_out.shape[2]
    for j in range(width // PAIR):
        cols = slice(j * PAIR, (j + 1) * PAIR)
        sides = []
        for h in (2 * j, 2 * j + 1):
            got = dq_in[0, h].astype(F32) + dq_in[1, h].astype(F32)
            sides.append(jnp.concatenate([got[:, :DH], got[2 * half - rows:, DH:]], axis=0))
        dq_out[0, :, cols] = jnp.concatenate(sides, axis=1).astype(BF)
        one, two = fin_in[2 * j], fin_in[2 * j + 1]
        dk_out[0, :, cols] = jnp.concatenate([one[:, :DH], two[:, :DH]], axis=1)
        dv_out[0, :, cols] = jnp.concatenate([one[:, DH:], two[:, DH:]], axis=1)


def local_halves(F, W, queries, keys_in, values_in, grad_out, partners, registers):
    _, rows, width = queries.shape
    heads = width // DH
    L = W // 2
    half = ((rows + 1) // 2 + 7) // 8 * 8
    per = next(n for n in range(L, 0, -1) if L % n == 0 and (n == 1 or n * F * rows <= UNIT))
    U = L // per
    unit = per * F * rows
    C = 2 * U
    QP = (unit + PAIR - 1) // PAIR * PAIR
    subs = unit // next(n for n in range(SUB, 0, -8) if unit % n == 0)
    stats = (3 * (QP // PAIR) + 7) // 8 * 8
    vm = lambda *shape: pltpu.VMEM(shape, BF)
    vf = lambda *shape: pltpu.VMEM(shape, F32)
    dma = lambda n: pltpu.SemaphoreType.DMA((n,))
    out = jax.ShapeDtypeStruct((1, rows, width), BF)
    dq_heads, kv_heads = pl.pallas_call(
        functools.partial(halves, F, W),
        out_shape=(jax.ShapeDtypeStruct((2, heads, half, PAIR), BF), jax.ShapeDtypeStruct((heads, rows, PAIR), BF)),
        in_specs=[pl.BlockSpec(memory_space=pl.ANY)] * 6,
        out_specs=(pl.BlockSpec(memory_space=pl.ANY),) * 2,
        scratch_shapes=[
            pltpu.SMEM(partners.T.shape, jnp.int32), pltpu.SMEM(registers.shape, jnp.int32),
            vm(1, rows, width), vm(1, rows, width), vm(1, rows, width), vm(1, rows, width),
            vm(heads, rows, PAIR), vm(heads, rows, PAIR), vm(U, per, F, rows, PAIR), vm(C, per, F, rows, PAIR),
            vm(U, unit, PAIR), vm(U, unit, PAIR), vm(U, DH, unit),
            vm(C, QP, PAIR), vm(C, QP, PAIR), vm(C, 2 * QP, PAIR),
            vf(U, C, unit, QP), vf(U, C, unit, QP), vf(U, per * F, rows, PAIR),
            vf(DH, QP), vf(QP, PAIR),
            vf(U, C, subs, 8, QP), vf(C, 8, QP), vf(C, 8, QP), vf(C, 8, QP),
            vf(C, stats, PAIR), vf(C, stats, PAIR),
            vm(heads, rows, PAIR), vm(C * per * F, half, PAIR),
            dma(6), dma(1), dma(U), dma(1), dma(C), dma(1), dma(C), dma(1), dma(2), dma(1), dma(1),
            pltpu.SemaphoreType.REGULAR, pltpu.SemaphoreType.REGULAR,
        ],
        compiler_params=pltpu.CompilerParams(
            collective_id=0, has_side_effects=True, vmem_limit_bytes=60 * 2 ** 20),
    )(partners.T, registers, queries, keys_in, values_in, grad_out)
    return pl.pallas_call(
        both_halves,
        out_shape=(out, out, out),
        in_specs=[pl.BlockSpec(memory_space=pltpu.VMEM)] * 2,
        out_specs=(pl.BlockSpec(memory_space=pltpu.VMEM),) * 3,
    )(dq_heads, kv_heads)


def choose(F, W, queries, *others):
    _, rows, width = queries.shape
    heads = width // DH
    held = 2 * F * W // 2 * rows * F * W * rows * 4
    if W % 2 == 0 and F * W == 2 * heads and SPLITS * F <= DH and held <= 24 * 2 ** 20:
        return local_halves(F, W, queries, *others)
    return local(F, W, queries, *others)


def solution(mesh):
    spec = P("frame", "within", None)
    return jax.shard_map(
        functools.partial(choose, mesh.shape["frame"], mesh.shape["within"]),
        mesh=mesh,
        in_specs=(spec, spec, spec, spec, P(), P()),
        out_specs=(spec, spec, spec),
        check_vma=False,
    )
```

```python
import functools
import math

import jax
import jax.numpy as jnp
import numpy as np
from jax import lax
from jax.experimental import pallas as pl
from jax.experimental.pallas import tpu as pltpu
from jax.sharding import PartitionSpec as P

DH = 64
PAIR = 2 * DH
SPLITS = 3
UNIT = 640
TILE = 256
SUB = 96
HIDDEN = -1e30
BF = jnp.bfloat16
F32 = jnp.float32
MESH = pl.DeviceIdType.MESH


def pieces_of(value):
    left, out = float(value), []
    for _ in range(SPLITS):
        part = float(np.asarray(left, dtype=jnp.bfloat16))
        out.append(part)
        left = left - part if abs(value) < 1e20 else 0.0
    return out


def rdot(a, b):
    return lax.dot_general(a, b, (((1,), (1,)), ((), ())), preferred_element_type=F32)


def dot(a, b):
    return jnp.dot(a, b, preferred_element_type=F32)


def each(lo, hi, do):
    def step(t, carry):
        do(t)
        return carry
    lax.fori_loop(lo, hi, step, 0)


def kernel(F, W, R, QC, inline, part_ref, reg_ref, q_ref, k_ref, v_ref, d_ref, dq_in, fin_in,
           kv_send, qd_send, kv_in, qd_in, kaug, vz, kt, qaug, xraw, qdz, sbuf, dpbuf, acc, dqacc, dqs,
           tops, top_ref, total_ref, dsum_ref,
           red_send, red_in, fin_send, dq_send, own_sem,
           kv_ss, fw_ss, kv_rs, qd_ss, qd_rs, red_ss, red_rs, fin_ss, fin_rs, dq_ss, dq_rs):
    fs = F // R
    hf = F // 2
    rows = q_ref.shape[1]
    width = q_ref.shape[2]
    seq = rows * W
    n_slots = part_ref.shape[0]
    scale = DH ** -0.5
    half = dq_send.shape[2]
    nq = R * seq
    n_chunks = nq // QC
    n_units, per = acc.shape[0], acc.shape[1]
    unit = per * F * rows
    f = lax.axis_index("frame")
    w = lax.axis_index("within")
    c = lax.rem(f, fs)
    a0 = lax.div(f, fs)
    sib = f + 1 - 2 * lax.rem(f, 2)
    head = w * R + a0

    barrier = pltpu.get_barrier_semaphore()

    def ahead(dw):
        return lax.rem(w + W - dw, W)

    def behind(dw):
        return lax.rem(w + dw, W)

    def greet(t):
        pl.semaphore_signal(barrier, inc=1, device_id=(lax.rem(f + 2 * lax.rem(t, hf), F), ahead(lax.div(t, hf))),
                            device_id_type=MESH)

    each(1, hf * W, greet)
    for dc in range(1, fs, 2):
        pl.semaphore_signal(barrier, inc=1, device_id=(a0 * fs + lax.rem(c + dc, fs), w), device_id_type=MESH)

    for first, second, out in ((q_ref, d_ref, qd_send), (k_ref, v_ref, kv_send)):
        for j in range(width // PAIR):
            cols = slice(j * PAIR, (j + 1) * PAIR)
            one = first[0, :, cols]
            two = second[0, :, cols]
            out[2 * j] = jnp.concatenate([one[:, :DH], two[:, :DH]], axis=1)
            out[2 * j + 1] = jnp.concatenate([one[:, DH:], two[:, DH:]], axis=1)
    kv_in[f, w] = kv_send[head]
    qd_in[a0, w] = qd_send[head]

    pl.semaphore_wait(barrier, hf * W - 1 + fs // 2)

    def kv_copy(t):
        ff = lax.rem(f + 2 * lax.rem(t, hf), F)
        ww = ahead(lax.div(t, hf))
        return pltpu.make_async_remote_copy(
            src_ref=kv_send.at[ww * R + lax.div(ff, fs)], dst_ref=kv_in.at[f, w],
            send_sem=kv_ss.at[t], recv_sem=kv_rs.at[f * W + w],
            device_id=(ff, ww), device_id_type=MESH)

    def pass_on(origin, t):
        ff = lax.rem(origin + F - 2 * lax.rem(t, hf), F)
        ww = behind(lax.div(t, hf))
        return pltpu.make_async_remote_copy(
            src_ref=kv_in.at[ff, ww], dst_ref=kv_in.at[ff, ww],
            send_sem=fw_ss.at[t], recv_sem=kv_rs.at[ff * W + ww],
            device_id=(sib, w), device_id_type=MESH)

    def qd_copy(t):
        aa, ww = lax.rem(a0 + lax.rem(t, R), R), ahead(lax.div(t, R))
        return pltpu.make_async_remote_copy(
            src_ref=qd_send.at[ww * R + aa], dst_ref=qd_in.at[a0, w],
            send_sem=qd_ss.at[t], recv_sem=qd_rs.at[a0 * W + w],
            device_id=(aa * fs + c, ww), device_id_type=MESH)

    def arrival(t, buffer, send, recv, index, source):
        return pltpu.make_async_remote_copy(
            src_ref=buffer.at[index], dst_ref=buffer.at[index], send_sem=send.at[t], recv_sem=recv,
            device_id=source, device_id_type=MESH)

    def qd_arrival(t):
        aa, ww = lax.rem(a0 + R - lax.rem(t, R), R), behind(lax.div(t, R))
        return arrival(t, qd_in, qd_ss, qd_rs.at[aa * W + ww], (aa, ww), (aa * fs + c, ww))

    def head_arrival(t, buffer, send, recv):
        aa, ww = lax.rem(a0 + R - lax.rem(t, R), R), ahead(lax.div(t, R))
        return arrival(t, buffer, send, recv.at[ww * R + aa], (ww * R + aa,), (aa * fs + c, ww))

    each(1, R * W, lambda t: qd_copy(t).start())
    pass_on(f, 0).start()
    each(1, hf * W, lambda t: kv_copy(t).start())

    acc[...] = jnp.zeros_like(acc)
    dqacc[...] = jnp.zeros_like(dqacc)

    def relay(t):
        move = pass_on(f, t)
        move.wait_recv()
        move.start()

    lane1 = lax.broadcasted_iota(jnp.int32, (1, PAIR), 1)
    table = [pieces_of(HIDDEN)] + [pieces_of(math.log(n)) for n in range(1, n_slots + 2)]
    marks = []
    for p in range(F):
        seen = jnp.zeros((1, PAIR), F32)
        unseen = jnp.zeros((1, PAIR), F32)
        for gi in range(R):
            g = c + fs * gi
            own = jnp.where(p == g, 1, 0)
            count = own
            for slot in range(n_slots):
                count = count + jnp.where(part_ref[slot, g] == p, 1, 0)
            for e in range(SPLITS):
                here = lane1 == DH + SPLITS * gi + e
                for n in range(n_slots + 2):
                    if n < 2:
                        unseen = jnp.where(here & (own == n), table[n][e], unseen)
                    seen = jnp.where(here & (count == n), table[n][e], seen)
        marks.append((seen, unseen))

    lane = lax.broadcasted_iota(jnp.int32, (rows, PAIR), 1)
    row = lax.broadcasted_iota(jnp.int32, (rows, PAIR), 0)

    def prepare(u):
        aug, raw = [], []
        for d in range(per):
            ww = behind(u * per + d)
            for p in range(F):
                both = kv_in[p, ww].astype(F32)
                extra = jnp.where(row + ww * rows >= reg_ref[p], marks[p][0], marks[p][1])
                raw.append(both)
                aug.append(jnp.where(lane < DH, both, extra))
        raw = jnp.concatenate(raw, axis=0)
        keep = lax.broadcasted_iota(jnp.int32, (unit, PAIR), 1) >= DH
        kaug[u] = jnp.concatenate(aug, axis=0).astype(BF)
        vz[u] = jnp.where(keep, raw, 0.0).astype(BF)
        kt[u] = (raw * scale).T[:DH].astype(BF)

    def direct(u):
        each(max(u * per * hf, 1), (u + 1) * per * hf, relay)

    def settle(u):
        each(u * per * hf, (u + 1) * per * hf, lambda t: pass_on(sib, t).wait_recv())
        prepare(u)

    def rows_of(i):
        return pl.ds(pl.multiple_of(i * QC, QC), QC)

    def begin(b):
        top_ref[b] = jnp.full_like(top_ref[b], -3e38)
        total_ref[b] = jnp.zeros_like(total_ref[b])
        dsum_ref[b] = jnp.zeros_like(dsum_ref[b])

    def forth(u, i, b):
        at = rows_of(i)
        raw = rdot(kaug[u], qaug[at])
        old = top_ref[b]
        top = jnp.maximum(old, jnp.max(raw, axis=0, keepdims=True))
        keep = jnp.exp(old - top)
        expo = jnp.exp(raw - top)
        dprod = rdot(vz[u], xraw[at])
        sbuf[u, b] = expo
        dpbuf[u, b] = dprod
        tops[u, b] = top
        top_ref[b] = top
        total_ref[b] = total_ref[b] * keep + jnp.sum(expo, axis=0, keepdims=True)
        dsum_ref[b] = dsum_ref[b] * keep + jnp.sum(expo * dprod, axis=0, keepdims=True)

    def back(u, i, b):
        inv = 1.0 / total_ref[b]
        factor = jnp.exp(tops[u, b] - top_ref[b]) * inv
        prob = sbuf[u, b] * factor
        dscore = (prob * (dpbuf[u, b] - dsum_ref[b] * inv)).astype(BF)
        added = dot(jnp.concatenate([dscore, prob.astype(BF)], axis=1), qdz[i])
        acc[u] += added.reshape(per, F, rows, PAIR)
        dqacc[i] += dot(kt[u], dscore)

    def own_copy(block, buffer, n):
        return pltpu.make_async_copy(block, buffer.at[head], own_sem.at[n])

    def red_copy(u, dc):
        return pltpu.make_async_remote_copy(
            src_ref=red_send.at[u, dc - 1], dst_ref=red_in.at[u, dc - 1],
            send_sem=red_ss.at[u * (fs - 1) + dc - 1], recv_sem=red_rs.at[u * (fs - 1) + dc - 1],
            device_id=(a0 * fs + lax.rem(c + dc, fs), w), device_id_type=MESH)

    def ship_part(u):
        for dc in range(1, fs):
            for gi in range(R):
                red_send[u, dc - 1, gi] = acc[u, :, lax.rem(c + dc, fs) + fs * gi].astype(BF)
            red_copy(u, dc).start()

    def fin_copy(t):
        dw = lax.div(t, R)
        aa, ww = lax.rem(a0 + lax.rem(t, R), R), behind(dw)
        return pltpu.make_async_remote_copy(
            src_ref=fin_send.at[lax.div(dw, per), aa, lax.rem(dw, per)], dst_ref=fin_in.at[head],
            send_sem=fin_ss.at[t], recv_sem=fin_rs.at[head],
            device_id=(aa * fs + c, ww), device_id_type=MESH)

    def ship_home(u):
        for dc in range(1, fs):
            red_copy(u, dc).wait_recv()
        for gi in range(R):
            whole = acc[u, :, c + fs * gi]
            for dc in range(1, fs):
                whole = whole + red_in[u, dc - 1, gi].astype(F32)
            fin_send[u, gi] = whole.astype(BF)
        if u == 0:
            own_copy(fin_send.at[0, a0, 0], fin_in, 0).start()
        each(max(u * per * R, 1), (u + 1) * per * R, lambda t: fin_copy(t).start())

    def take_queries():
        each(1, R * W, lambda t: qd_arrival(t).wait_recv())
        wide = lax.broadcasted_iota(jnp.int32, (nq, PAIR), 1)
        tall = lax.broadcasted_iota(jnp.int32, (nq, PAIR), 0)
        both = qd_in[...].astype(F32).reshape(nq, PAIR)
        mark = jnp.zeros((nq, PAIR), F32)
        for gi in range(R):
            mine = (tall >= gi * seq) & (tall < (gi + 1) * seq)
            mark = jnp.where(mine & (wide >= DH + SPLITS * gi) & (wide < DH + SPLITS * (gi + 1)), 1.0, mark)
        scaled = both * scale
        qaug[...] = jnp.where(wide < DH, scaled, mark).astype(BF)
        xraw[...] = both.astype(BF)
        qdz[:, :QC] = jnp.where(wide < DH, scaled, 0.0).astype(BF).reshape(n_chunks, QC, PAIR)
        qdz[:, QC:] = jnp.where(wide >= DH, both, 0.0).astype(BF).reshape(n_chunks, QC, PAIR)

    take_queries()
    if inline:
        each(0, n_chunks, begin)
        direct(0)
        for u in range(n_units):
            settle(u)
            forth(u, 0, 0)
            if u + 1 < n_units:
                direct(u + 1)
            each(1, n_chunks, lambda i: forth(u, i, i))
        for u in range(n_units):
            back(u, 0, 0)
            if u:
                ship_home(u - 1)
            each(1, n_chunks, lambda i: back(u, i, i))
            ship_part(u)
    else:
        for u in range(n_units):
            direct(u)
        for u in range(n_units):
            settle(u)

        def block(i):
            begin(0)
            each(0, n_units, lambda u: forth(u, i, 0))
            each(0, n_units, lambda u: back(u, i, 0))

        each(0, n_chunks, block)
        for u in range(n_units):
            ship_part(u)
        for u in range(n_units - 1):
            ship_home(u)

    def dq_copy(t):
        aa, ww = lax.rem(a0 + lax.rem(t, R), R), behind(lax.div(t, R))
        return pltpu.make_async_remote_copy(
            src_ref=dq_send.at[aa, ww], dst_ref=dq_in.at[head],
            send_sem=dq_ss.at[t], recv_sem=dq_rs.at[head],
            device_id=(aa * fs + c, ww), device_id_type=MESH)

    for i in range(n_chunks):
        dqs[i * QC:(i + 1) * QC] = jnp.concatenate([dqacc[i], jnp.zeros((DH, QC), F32)], axis=0).T
    for gi in range(R):
        for ww in range(W):
            base = gi * seq + ww * rows
            dq_send[gi, ww] = jnp.concatenate(
                [dqs[base:base + half, :DH], dqs[base + rows - half:base + rows, :DH]], axis=1).astype(BF)
    own_copy(dq_send.at[a0, w], dq_in, 1).start()
    each(1, R * W, lambda t: dq_copy(t).start())
    ship_home(n_units - 1)

    each(1, R * W, lambda t: head_arrival(t, dq_in, dq_ss, dq_rs).wait_recv())
    each(1, R * W, lambda t: head_arrival(t, fin_in, fin_ss, fin_rs).wait_recv())
    each(1, hf * W, lambda t: kv_copy(t).wait_send())
    each(0, hf * W, lambda t: pass_on(f, t).wait_send())
    each(1, R * W, lambda t: qd_copy(t).wait_send())
    own_copy(fin_send.at[0, a0, 0], fin_in, 0).wait()
    own_copy(dq_send.at[a0, w], dq_in, 1).wait()
    each(1, R * W, lambda t: dq_copy(t).wait_send())
    each(1, R * W, lambda t: fin_copy(t).wait_send())
    for u in range(n_units):
        for dc in range(1, fs):
            red_copy(u, dc).wait_send()


def tokens_again(dq_in, fin_in, dq_out, dk_out, dv_out):
    half, rows, width = dq_in.shape[1], dq_out.shape[1], dq_out.shape[2]
    for j in range(width // PAIR):
        cols = slice(j * PAIR, (j + 1) * PAIR)
        sides = []
        for h in (2 * j, 2 * j + 1):
            got = dq_in[h].astype(F32)
            sides.append(jnp.concatenate([got[:, :DH], got[2 * half - rows:, DH:]], axis=0))
        dq_out[0, :, cols] = jnp.concatenate(sides, axis=1).astype(BF)

    for j in range(width // PAIR):
        cols = slice(j * PAIR, (j + 1) * PAIR)
        one, two = fin_in[2 * j], fin_in[2 * j + 1]
        dk_out[0, :, cols] = jnp.concatenate([one[:, :DH], two[:, :DH]], axis=1)
        dv_out[0, :, cols] = jnp.concatenate([one[:, DH:], two[:, DH:]], axis=1)


def local(F, W, queries, keys_in, values_in, grad_out, partners, registers):
    _, rows, width = queries.shape
    heads = width // DH
    R = heads // W
    fs = F // R
    seq = rows * W
    nq = R * seq
    half = ((rows + 1) // 2 + 7) // 8 * 8
    inline = F * seq * nq * 8 <= 24 * 2 ** 20
    QC = next(b for b in ((576, 384, 128) if inline else (128,)) if nq % b == 0)
    held = nq // QC if inline else 1
    per = next(n for n in range(W, 0, -1) if W % n == 0 and (n == 1 or n * F * rows <= UNIT))
    units = W // per
    unit = per * F * rows
    vm = lambda *shape: pltpu.VMEM(shape, BF)
    vf = lambda *shape: pltpu.VMEM(shape, F32)
    dma = lambda n: pltpu.SemaphoreType.DMA((n,))
    out = jax.ShapeDtypeStruct((1, rows, width), BF)
    dq_heads, kv_heads = pl.pallas_call(
        functools.partial(kernel, F, W, R, QC, inline),
        out_shape=(jax.ShapeDtypeStruct((heads, half, PAIR), BF), jax.ShapeDtypeStruct((heads, rows, PAIR), BF)),
        in_specs=[pl.BlockSpec(memory_space=pltpu.SMEM)] * 2 + [pl.BlockSpec(memory_space=pltpu.VMEM)] * 4,
        out_specs=(pl.BlockSpec(memory_space=pl.ANY),) * 2,
        scratch_shapes=[
            vm(heads, rows, PAIR), vm(heads, rows, PAIR),
            vm(F, W, rows, PAIR), vm(R, W, rows, PAIR),
            vm(units, unit, PAIR), vm(units, unit, PAIR), vm(units, DH, unit),
            vm(nq, PAIR), vm(nq, PAIR), vm(nq // QC, 2 * QC, PAIR),
            vf(units, held, unit, QC), vf(units, held, unit, QC), vf(units, per, F, rows, PAIR),
            vf(nq // QC, DH, QC), vf(nq, PAIR),
            vf(units, held, 1, QC), vf(held, 1, QC), vf(held, 1, QC), vf(held, 1, QC),
            vm(units, fs - 1, R, per, rows, PAIR), vm(units, fs - 1, R, per, rows, PAIR),
            vm(units, R, per, rows, PAIR), vm(R, W, half, PAIR), dma(2),
            dma(F // 2 * W), dma(F // 2 * W), dma(F * W), dma(R * W), dma(R * W),
            dma(units * (fs - 1)), dma(units * (fs - 1)), dma(R * W), dma(heads), dma(R * W), dma(heads),
        ],
        compiler_params=pltpu.CompilerParams(
            collective_id=0, has_side_effects=True, vmem_limit_bytes=60 * 2 ** 20),
    )(partners.T, registers, queries, keys_in, values_in, grad_out)
    return pl.pallas_call(
        tokens_again,
        out_shape=(out, out, out),
        in_specs=[pl.BlockSpec(memory_space=pltpu.VMEM)] * 2,
        out_specs=(pl.BlockSpec(memory_space=pltpu.VMEM),) * 3,
    )(dq_heads, kv_heads)


def halves(F, W, part_hbm, reg_hbm, q_hbm, k_hbm, v_hbm, d_hbm, dq_in, fin_in,
           part_ref, reg_ref, q_ref, k_ref, v_ref, d_ref, kv_send, qd_send, kv_in, qd_in,
           kaug, vz, kt, qaug, xraw, qdz, sbuf, dpbuf, acc, dqacc, dqs,
           tops, top_ref, total_ref, dsum_ref, st_send, st_in, fin_send, dq_send,
           in_sem, kv_ss, kv_rs, qd_ss, qd_rs, st_ss, st_rs, dq_ss, dq_rs, fin_ss, fin_rs, below, above):
    rows, width = q_ref.shape[1], q_ref.shape[2]
    n_slots = part_ref.shape[0]
    U, per = kv_in.shape[0], kv_in.shape[1]
    L = U * per
    B = 2 * U
    heads = F * L
    group = per * F
    unit = group * rows
    QP = qaug.shape[1]
    tiles = [(c, min(c + TILE, QP)) for c in range(0, QP, TILE)]
    n_subs = tops.shape[2]
    sub = unit // n_subs
    cuts = 2 if n_subs % 2 == 0 and group % 2 == 0 else 1
    scale = DH ** -0.5
    half = dq_send.shape[1]
    f = lax.axis_index("frame")
    w = lax.axis_index("within")
    block0 = lax.div(w, per)
    d0 = lax.rem(w, per)
    part = lax.div(block0, U)
    other = 1 - part
    u0 = lax.rem(block0, U)
    l = u0 * per + d0
    head = f * L + l

    barrier = pltpu.get_barrier_semaphore()

    def around(t):
        return lax.rem(d0 + lax.div(t, F), per), lax.rem(f + lax.rem(t, F), F)

    def knock(sem, block, d, ff):
        pl.semaphore_signal(sem, inc=1, device_id=(ff, block * per + d), device_id_type=MESH)

    def greet(t):
        d, ff = around(group - t)
        knock(barrier, block0, d, ff)

    @pl.when(block0 > 0)
    def _():
        knock(barrier, block0 - 1, d0, f)

    @pl.when(block0 < B - 1)
    def _():
        knock(barrier, block0 + 1, d0, f)

    each(1, group, greet)
    loads = [pltpu.make_async_copy(src, dst, in_sem.at[n]) for n, (src, dst) in enumerate(
        ((k_hbm, k_ref), (v_hbm, v_ref), (q_hbm, q_ref), (d_hbm, d_ref), (part_hbm, part_ref), (reg_hbm, reg_ref)))]
    for load in loads:
        load.start()

    for first, second, out in ((k_ref, v_ref, kv_send), (q_ref, d_ref, qd_send)):
        for load in (loads.pop(0), loads.pop(0)):
            load.wait()
        for j in range(width // PAIR):
            cols = slice(j * PAIR, (j + 1) * PAIR)
            one = first[0, :, cols]
            two = second[0, :, cols]
            out[2 * j] = jnp.concatenate([one[:, :DH], two[:, :DH]], axis=1)
            out[2 * j + 1] = jnp.concatenate([one[:, DH:], two[:, DH:]], axis=1)

    def remote(src, dst, ss, rs, device):
        return pltpu.make_async_remote_copy(src_ref=src, dst_ref=dst, send_sem=ss, recv_sem=rs,
                                            device_id=device, device_id_type=MESH)

    def head_at(block, d, ff):
        return ff * L + lax.rem(block, U) * per + d

    def kv_copy(block, t):
        d, ff = around(t)
        return remote(kv_send.at[head_at(block, d, ff)], kv_in.at[u0, d0, f], kv_ss.at[0], kv_rs.at[u0],
                      (ff, block * per + d))

    def qd_copy(block, t):
        d, ff = around(t)
        return remote(qd_send.at[head_at(block, d, ff)], qd_in.at[block0, d0, f], qd_ss.at[0], qd_rs.at[block0],
                      (ff, block * per + d))

    def send_block(block, first):
        @pl.when(lax.div(block, U) == part)
        def _():
            each(first, group, lambda t: kv_copy(block, t).start())
        each(first, group, lambda t: qd_copy(block, t).start())

    pltpu.make_async_copy(kv_send.at[head], kv_in.at[u0, d0, f], kv_rs.at[u0]).start()
    pltpu.make_async_copy(qd_send.at[head], qd_in.at[block0, d0, f], qd_rs.at[block0]).start()
    pl.semaphore_wait(barrier, group - 1 + jnp.where(block0 > 0, 1, 0) + jnp.where(block0 < B - 1, 1, 0))

    @pl.when(block0 > 0)
    def _():
        knock(above, block0 - 1, d0, f)

    @pl.when(block0 < B - 1)
    def _():
        knock(below, block0 + 1, d0, f)

    send_block(block0, 1)
    for n in range(1, B):
        @pl.when(block0 >= n)
        def _():
            pl.semaphore_wait(below, 1)

            @pl.when(block0 < B - 1)
            def _():
                knock(below, block0 + 1, d0, f)
            send_block(block0 - n, 0)

        @pl.when(block0 + n < B)
        def _():
            pl.semaphore_wait(above, 1)

            @pl.when(block0 > 0)
            def _():
                knock(above, block0 - 1, d0, f)
            send_block(block0 + n, 0)

    acc[...] = jnp.zeros_like(acc)
    st_send[...] = jnp.zeros_like(st_send)
    if QP > unit:
        lo, hi = tiles[-1]
        for ref, first in ((qaug, unit), (xraw, unit), (qdz, lo + unit), (qdz, hi + unit)):
            ref[:, first:first + QP - unit] = jnp.zeros((B, QP - unit, PAIR), BF)
    for load in loads:
        load.wait()

    lane1 = lax.broadcasted_iota(jnp.int32, (1, PAIR), 1)
    table = [pieces_of(HIDDEN)] + [pieces_of(math.log(n)) for n in range(1, n_slots + 2)]
    marks = []
    for p in range(F):
        seen = jnp.zeros((1, PAIR), F32)
        unseen = jnp.zeros((1, PAIR), F32)
        for g in range(F):
            own = 1 if p == g else 0
            count = own
            for slot in range(n_slots):
                count = count + jnp.where(part_ref[slot, g] == p, 1, 0)
            for e in range(SPLITS):
                here = lane1 == DH + SPLITS * g + e
                unseen = jnp.where(here, table[own][e], unseen)
                for n in range(own, n_slots + 2):
                    seen = jnp.where(here & (count == n), table[n][e], seen)
        marks.append((seen, unseen))

    lane = lax.broadcasted_iota(jnp.int32, (rows, PAIR), 1)
    row = lax.broadcasted_iota(jnp.int32, (rows, PAIR), 0)
    tall = lax.broadcasted_iota(jnp.int32, (unit, PAIR), 1)
    hot = [jnp.where((lane >= DH + SPLITS * g) & (lane < DH + SPLITS * (g + 1)), 1.0, 0.0) for g in range(F)]

    def take_keys(j):
        u = lax.rem(u0 + j, U)
        here = kv_in.at[u]
        remote(here, here, kv_ss.at[0], kv_rs.at[u], (f, w)).wait_recv()
        aug, raw = [], []
        for d in range(per):
            first = ((part * U + u) * per + d) * rows
            for p in range(F):
                both = kv_in[u, d, p].astype(F32)
                extra = jnp.where(row + first >= reg_ref[p], marks[p][0], marks[p][1])
                raw.append(both)
                aug.append(jnp.where(lane < DH, both, extra))
        raw = jnp.concatenate(raw, axis=0)
        kaug[j] = jnp.concatenate(aug, axis=0).astype(BF)
        vz[j] = jnp.where(tall >= DH, raw, 0.0).astype(BF)
        kt[j] = (raw * scale).T[:DH].astype(BF)

    def take_queries(i):
        here = qd_in.at[i]
        remote(here, here, qd_ss.at[0], qd_rs.at[i], (f, w)).wait_recv()
        raw, aug = [], []
        for d in range(per):
            for g in range(F):
                both = qd_in[i, d, g].astype(F32)
                raw.append(both)
                aug.append(jnp.where(lane < DH, both * scale, hot[g]))
        raw = jnp.concatenate(raw, axis=0)
        qaug[i, :unit] = jnp.concatenate(aug, axis=0).astype(BF)
        xraw[i, :unit] = raw.astype(BF)
        for value, side in ((jnp.where(tall < DH, raw * scale, 0.0), 0), (jnp.where(tall >= DH, raw, 0.0), 1)):
            for lo, hi in tiles:
                first, n = 2 * lo + side * (hi - lo), min(hi, unit) - lo
                qdz[i, first:first + n] = value[lo:lo + n].astype(BF)

    def forth(j, i):
        for lo, hi in tiles:
            raw = rdot(kaug[j], qaug[i, lo:hi])
            dprod = rdot(vz[j], xraw[i, lo:hi])
            if j:
                top, total, dsum = top_ref[i, :, lo:hi], total_ref[i, :, lo:hi], dsum_ref[i, :, lo:hi]
            for s in range(n_subs):
                at = slice(s * sub, (s + 1) * sub)
                part_raw = raw[at].reshape(sub // 8, 8, hi - lo)
                part_dp = dprod[at].reshape(sub // 8, 8, hi - lo)
                peak = jnp.max(part_raw, axis=0)
                if j or s:
                    peak = jnp.maximum(top, peak)
                expo = jnp.exp(part_raw - peak[None])
                more, dmore = jnp.sum(expo, axis=0), jnp.sum(expo * part_dp, axis=0)
                if j or s:
                    keep = jnp.exp(top - peak)
                    more, dmore = total * keep + more, dsum * keep + dmore
                top, total, dsum = peak, more, dmore
                sbuf[j, i, at, lo:hi] = expo.reshape(sub, hi - lo)
                dpbuf[j, i, at, lo:hi] = part_dp.reshape(sub, hi - lo)
                tops[j, i, s, :, lo:hi] = peak
            top_ref[i, :, lo:hi] = top
            total_ref[i, :, lo:hi] = total
            dsum_ref[i, :, lo:hi] = dsum

    spans = [(c, c + PAIR) for c in range(0, QP, PAIR)]

    def give(i):
        peak = jnp.max(top_ref[i], axis=0, keepdims=True)
        keep = jnp.exp(top_ref[i] - peak)
        total = jnp.sum(total_ref[i] * keep, axis=0, keepdims=True)
        dsum = jnp.sum(dsum_ref[i] * keep, axis=0, keepdims=True)
        for s, value in enumerate((peak, total, dsum)):
            for n, (lo, hi) in enumerate(spans):
                at = s * len(spans) + n
                st_send[i, at:at + 1] = value[:, lo:hi]
        remote(st_send.at[i], st_in.at[i], st_ss.at[0], st_rs.at[i], (f, other * L + l)).start()

    def meet(i):
        here = st_in.at[i]
        remote(here, here, st_ss.at[0], st_rs.at[i], (f, other * L + l)).wait_recv()
        def row_of(ref, s):
            return jnp.concatenate(
                [ref[i, s * len(spans) + n:s * len(spans) + n + 1] for n in range(len(spans))], axis=1)

        mine, yours = [[row_of(ref, s) for s in range(3)] for ref in (st_send, st_in)]
        peak = jnp.maximum(mine[0], yours[0])
        a, b = jnp.exp(mine[0] - peak), jnp.exp(yours[0] - peak)
        inv = 1.0 / (mine[1] * a + yours[1] * b)
        whole = (8, QP)
        top_ref[i] = jnp.broadcast_to(peak, whole)
        total_ref[i] = jnp.broadcast_to(inv, whole)
        dsum_ref[i] = jnp.broadcast_to((mine[2] * a + yours[2] * b) * inv, whole)

    def back(j, i):
        for lo, hi in tiles:
            probs, dscores = [], []
            for s in range(n_subs):
                at = slice(s * sub, (s + 1) * sub)
                factor = jnp.exp(tops[j, i, s, :, lo:hi] - top_ref[i, :, lo:hi]) * total_ref[i, :, lo:hi]
                prob = sbuf[j, i, at, lo:hi].reshape(sub // 8, 8, hi - lo) * factor[None]
                dprod = dpbuf[j, i, at, lo:hi].reshape(sub // 8, 8, hi - lo)
                dscore = prob * (dprod - dsum_ref[i, :, lo:hi][None])
                probs.append(prob.reshape(sub, hi - lo).astype(BF))
                dscores.append(dscore.reshape(sub, hi - lo).astype(BF))
            for first in range(0, n_subs, n_subs // cuts):
                some = slice(first, first + n_subs // cuts)
                both = [jnp.concatenate(x[some], axis=0) for x in (dscores, probs)]
                added = dot(jnp.concatenate(both, axis=1), qdz[i, 2 * lo:2 * hi])
                at = slice(first * group // n_subs, (first + n_subs // cuts) * group // n_subs)
                acc[j, at] += added.reshape(group // cuts, rows, PAIR)
            more = dot(kt[j], jnp.concatenate(dscores, axis=0))
            if j < U - 1:
                more = dqacc[i, :, lo:hi] + more
            dqacc[i, :, lo:hi] = more

    def dq_copy(i, t):
        d, ff = around(t)
        return remote(dq_send.at[i * group + d * F + ff], dq_in.at[part, head], dq_ss.at[0], dq_rs.at[part], (ff, i * per + d))

    def ship_queries(i):
        dqs[...] = jnp.concatenate([dqacc[i], jnp.zeros((DH, QP), F32)], axis=0).T
        for d in range(per):
            for g in range(F):
                base = (d * F + g) * rows
                dq_send[i * group + d * F + g] = jnp.concatenate(
                    [dqs[base:base + half, :DH], dqs[base + rows - half:base + rows, :DH]], axis=1).astype(BF)

        @pl.when(i == block0)
        def _():
            pltpu.make_async_copy(dq_send.at[i * group + d0 * F + f], dq_in.at[part, head], dq_rs.at[part]).start()

        @pl.when(i != block0)
        def _():
            dq_copy(i, 0).start()
        each(1, group, lambda t: dq_copy(i, t).start())

    def fin_copy(j, t):
        d, ff = around(t)
        return remote(fin_send.at[j * group + d * F + ff], fin_in.at[head], fin_ss.at[0], fin_rs.at[0],
                      (ff, (part * U + lax.rem(u0 + j, U)) * per + d))

    def ship_keys(j):
        fin_send[j * group:(j + 1) * group] = acc[j].astype(BF)
        if j == 0:
            pltpu.make_async_copy(fin_send.at[d0 * F + f], fin_in.at[head], fin_rs.at[0]).start()
        each(0 if j else 1, group, lambda t: fin_copy(j, t).start())

    def local(n):
        return part * U + lax.rem(u0 + n, U)

    def remote_block(n):
        return other * U + n + part * (U - 1 - 2 * n)

    edge = jnp.where(part == 0, U - 1, 0) == u0
    order = [local(0)]
    for n in range(U - 1):
        order.append(jnp.where(edge, remote_block(n), local(n + 1)))
        order.append(jnp.where(edge, local(n + 1), remote_block(n)))
    order.append(remote_block(U - 1))

    for n, i in enumerate(order):
        if n:
            take_queries(i)
        for j in range(U):
            if n == 0:
                take_keys(j)
                if j == 0:
                    take_queries(i)
            forth(j, i)
        give(i)
    last = [jnp.where(edge, remote_block(U - 1 - n), remote_block(n)) for n in range(U)]
    for i in last:
        meet(i)
        for j in reversed(range(U)):
            back(j, i)
        ship_queries(i)
    mine = [local(n) for n in reversed(range(U))]
    for i in mine:
        meet(i)
    for j in reversed(range(U)):
        for i in mine:
            back(j, i)
            if j == 0:
                ship_queries(i)
        ship_keys(j)

    def sent(ref, sem):
        remote(ref, ref, sem.at[0], sem.at[0], (f, w)).wait_send()

    sent(kv_send.at[pl.ds(0, heads - 1)], kv_ss)
    sent(qd_send, qd_ss)
    sent(qd_send.at[pl.ds(0, heads - 1)], qd_ss)
    sent(st_send, st_ss)
    for side in (other, part):
        here = dq_in.at[side]
        remote(here, here, dq_ss.at[0], dq_rs.at[side], (f, w)).wait_recv()
    remote(fin_in, fin_in, fin_ss.at[0], fin_rs.at[0], (f, w)).wait_recv()
    sent(dq_send.at[pl.ds(0, B * group - 1)], dq_ss)
    sent(fin_send.at[pl.ds(0, U * group - 1)], fin_ss)


def both_halves(dq_in, fin_in, dq_out, dk_out, dv_out):
    half, rows, width = dq_in.shape[2], dq_out.shape[1], dq_out.shape[2]
    for j in range(width // PAIR):
        cols = slice(j * PAIR, (j + 1) * PAIR)
        sides = []
        for h in (2 * j, 2 * j + 1):
            got = dq_in[0, h].astype(F32) + dq_in[1, h].astype(F32)
            sides.append(jnp.concatenate([got[:, :DH], got[2 * half - rows:, DH:]], axis=0))
        dq_out[0, :, cols] = jnp.concatenate(sides, axis=1).astype(BF)
        one, two = fin_in[2 * j], fin_in[2 * j + 1]
        dk_out[0, :, cols] = jnp.concatenate([one[:, :DH], two[:, :DH]], axis=1)
        dv_out[0, :, cols] = jnp.concatenate([one[:, DH:], two[:, DH:]], axis=1)


def local_halves(F, W, queries, keys_in, values_in, grad_out, partners, registers):
    _, rows, width = queries.shape
    heads = width // DH
    L = W // 2
    half = ((rows + 1) // 2 + 7) // 8 * 8
    per = next(n for n in range(L, 0, -1) if L % n == 0 and (n == 1 or n * F * rows <= UNIT))
    U = L // per
    unit = per * F * rows
    C = 2 * U
    QP = (unit + PAIR - 1) // PAIR * PAIR
    subs = unit // next(n for n in range(SUB, 0, -8) if unit % n == 0)
    stats = (3 * (QP // PAIR) + 7) // 8 * 8
    vm = lambda *shape: pltpu.VMEM(shape, BF)
    vf = lambda *shape: pltpu.VMEM(shape, F32)
    dma = lambda n: pltpu.SemaphoreType.DMA((n,))
    out = jax.ShapeDtypeStruct((1, rows, width), BF)
    dq_heads, kv_heads = pl.pallas_call(
        functools.partial(halves, F, W),
        out_shape=(jax.ShapeDtypeStruct((2, heads, half, PAIR), BF), jax.ShapeDtypeStruct((heads, rows, PAIR), BF)),
        in_specs=[pl.BlockSpec(memory_space=pl.ANY)] * 6,
        out_specs=(pl.BlockSpec(memory_space=pl.ANY),) * 2,
        scratch_shapes=[
            pltpu.SMEM(partners.T.shape, jnp.int32), pltpu.SMEM(registers.shape, jnp.int32),
            vm(1, rows, width), vm(1, rows, width), vm(1, rows, width), vm(1, rows, width),
            vm(heads, rows, PAIR), vm(heads, rows, PAIR), vm(U, per, F, rows, PAIR), vm(C, per, F, rows, PAIR),
            vm(U, unit, PAIR), vm(U, unit, PAIR), vm(U, DH, unit),
            vm(C, QP, PAIR), vm(C, QP, PAIR), vm(C, 2 * QP, PAIR),
            vf(U, C, unit, QP), vf(U, C, unit, QP), vf(U, per * F, rows, PAIR),
            vf(C, DH, QP), vf(QP, PAIR),
            vf(U, C, subs, 8, QP), vf(C, 8, QP), vf(C, 8, QP), vf(C, 8, QP),
            vf(C, stats, PAIR), vf(C, stats, PAIR),
            vm(heads, rows, PAIR), vm(C * per * F, half, PAIR),
            dma(6), dma(1), dma(U), dma(1), dma(C), dma(1), dma(C), dma(1), dma(2), dma(1), dma(1),
            pltpu.SemaphoreType.REGULAR, pltpu.SemaphoreType.REGULAR,
        ],
        compiler_params=pltpu.CompilerParams(
            collective_id=0, has_side_effects=True, vmem_limit_bytes=60 * 2 ** 20),
    )(partners.T, registers, queries, keys_in, values_in, grad_out)
    return pl.pallas_call(
        both_halves,
        out_shape=(out, out, out),
        in_specs=[pl.BlockSpec(memory_space=pltpu.VMEM)] * 2,
        out_specs=(pl.BlockSpec(memory_space=pltpu.VMEM),) * 3,
    )(dq_heads, kv_heads)


def choose(F, W, queries, *others):
    _, rows, width = queries.shape
    heads = width // DH
    held = 2 * F * W // 2 * rows * F * W * rows * 4
    if W % 2 == 0 and F * W == 2 * heads and SPLITS * F <= DH and held <= 24 * 2 ** 20:
        return local_halves(F, W, queries, *others)
    return local(F, W, queries, *others)


def solution(mesh):
    spec = P("frame", "within", None)
    return jax.shard_map(
        functools.partial(choose, mesh.shape["frame"], mesh.shape["within"]),
        mesh=mesh,
        in_specs=(spec, spec, spec, spec, P(), P()),
        out_specs=(spec, spec, spec),
        check_vma=False,
    )
```

```python
import functools
import math

import jax
import jax.numpy as jnp
import numpy as np
from jax import lax
from jax.experimental import pallas as pl
from jax.experimental.pallas import tpu as pltpu
from jax.sharding import PartitionSpec as P

DH = 64
PAIR = 2 * DH
SPLITS = 3
UNIT = 640
TILE = 256
SUB = 96
HIDDEN = -1e30
BF = jnp.bfloat16
F32 = jnp.float32
MESH = pl.DeviceIdType.MESH


def pieces_of(value):
    left, out = float(value), []
    for _ in range(SPLITS):
        part = float(np.asarray(left, dtype=jnp.bfloat16))
        out.append(part)
        left = left - part if abs(value) < 1e20 else 0.0
    return out


def rdot(a, b):
    return lax.dot_general(a, b, (((1,), (1,)), ((), ())), preferred_element_type=F32)


def dot(a, b):
    return jnp.dot(a, b, preferred_element_type=F32)


def each(lo, hi, do):
    def step(t, carry):
        do(t)
        return carry
    lax.fori_loop(lo, hi, step, 0)


def kernel(F, W, R, QC, inline, part_ref, reg_ref, q_ref, k_ref, v_ref, d_ref, dq_in, fin_in,
           kv_send, qd_send, kv_in, qd_in, kaug, vz, kt, qaug, xraw, qdz, sbuf, dpbuf, acc, dqacc, dqs,
           tops, top_ref, total_ref, dsum_ref,
           red_send, red_in, fin_send, dq_send, own_sem,
           kv_ss, fw_ss, kv_rs, qd_ss, qd_rs, red_ss, red_rs, fin_ss, fin_rs, dq_ss, dq_rs):
    fs = F // R
    hf = F // 2
    rows = q_ref.shape[1]
    width = q_ref.shape[2]
    seq = rows * W
    n_slots = part_ref.shape[0]
    scale = DH ** -0.5
    half = dq_send.shape[2]
    nq = R * seq
    n_chunks = nq // QC
    n_units, per = acc.shape[0], acc.shape[1]
    unit = per * F * rows
    f = lax.axis_index("frame")
    w = lax.axis_index("within")
    c = lax.rem(f, fs)
    a0 = lax.div(f, fs)
    sib = f + 1 - 2 * lax.rem(f, 2)
    head = w * R + a0

    barrier = pltpu.get_barrier_semaphore()

    def ahead(dw):
        return lax.rem(w + W - dw, W)

    def behind(dw):
        return lax.rem(w + dw, W)

    def greet(t):
        pl.semaphore_signal(barrier, inc=1, device_id=(lax.rem(f + 2 * lax.rem(t, hf), F), ahead(lax.div(t, hf))),
                            device_id_type=MESH)

    each(1, hf * W, greet)
    for dc in range(1, fs, 2):
        pl.semaphore_signal(barrier, inc=1, device_id=(a0 * fs + lax.rem(c + dc, fs), w), device_id_type=MESH)

    for first, second, out in ((q_ref, d_ref, qd_send), (k_ref, v_ref, kv_send)):
        for j in range(width // PAIR):
            cols = slice(j * PAIR, (j + 1) * PAIR)
            one = first[0, :, cols]
            two = second[0, :, cols]
            out[2 * j] = jnp.concatenate([one[:, :DH], two[:, :DH]], axis=1)
            out[2 * j + 1] = jnp.concatenate([one[:, DH:], two[:, DH:]], axis=1)
    kv_in[f, w] = kv_send[head]
    qd_in[a0, w] = qd_send[head]

    pl.semaphore_wait(barrier, hf * W - 1 + fs // 2)

    def kv_copy(t):
        ff = lax.rem(f + 2 * lax.rem(t, hf), F)
        ww = ahead(lax.div(t, hf))
        return pltpu.make_async_remote_copy(
            src_ref=kv_send.at[ww * R + lax.div(ff, fs)], dst_ref=kv_in.at[f, w],
            send_sem=kv_ss.at[t], recv_sem=kv_rs.at[f * W + w],
            device_id=(ff, ww), device_id_type=MESH)

    def pass_on(origin, t):
        ff = lax.rem(origin + F - 2 * lax.rem(t, hf), F)
        ww = behind(lax.div(t, hf))
        return pltpu.make_async_remote_copy(
            src_ref=kv_in.at[ff, ww], dst_ref=kv_in.at[ff, ww],
            send_sem=fw_ss.at[t], recv_sem=kv_rs.at[ff * W + ww],
            device_id=(sib, w), device_id_type=MESH)

    def qd_copy(t):
        aa, ww = lax.rem(a0 + lax.rem(t, R), R), ahead(lax.div(t, R))
        return pltpu.make_async_remote_copy(
            src_ref=qd_send.at[ww * R + aa], dst_ref=qd_in.at[a0, w],
            send_sem=qd_ss.at[t], recv_sem=qd_rs.at[a0 * W + w],
            device_id=(aa * fs + c, ww), device_id_type=MESH)

    def arrival(t, buffer, send, recv, index, source):
        return pltpu.make_async_remote_copy(
            src_ref=buffer.at[index], dst_ref=buffer.at[index], send_sem=send.at[t], recv_sem=recv,
            device_id=source, device_id_type=MESH)

    def qd_arrival(t):
        aa, ww = lax.rem(a0 + R - lax.rem(t, R), R), behind(lax.div(t, R))
        return arrival(t, qd_in, qd_ss, qd_rs.at[aa * W + ww], (aa, ww), (aa * fs + c, ww))

    def head_arrival(t, buffer, send, recv):
        aa, ww = lax.rem(a0 + R - lax.rem(t, R), R), ahead(lax.div(t, R))
        return arrival(t, buffer, send, recv.at[ww * R + aa], (ww * R + aa,), (aa * fs + c, ww))

    each(1, R * W, lambda t: qd_copy(t).start())
    pass_on(f, 0).start()
    each(1, hf * W, lambda t: kv_copy(t).start())

    acc[...] = jnp.zeros_like(acc)
    dqacc[...] = jnp.zeros_like(dqacc)

    def relay(t):
        move = pass_on(f, t)
        move.wait_recv()
        move.start()

    lane1 = lax.broadcasted_iota(jnp.int32, (1, PAIR), 1)
    table = [pieces_of(HIDDEN)] + [pieces_of(math.log(n)) for n in range(1, n_slots + 2)]
    marks = []
    for p in range(F):
        seen = jnp.zeros((1, PAIR), F32)
        unseen = jnp.zeros((1, PAIR), F32)
        for gi in range(R):
            g = c + fs * gi
            own = jnp.where(p == g, 1, 0)
            count = own
            for slot in range(n_slots):
                count = count + jnp.where(part_ref[slot, g] == p, 1, 0)
            for e in range(SPLITS):
                here = lane1 == DH + SPLITS * gi + e
                for n in range(n_slots + 2):
                    if n < 2:
                        unseen = jnp.where(here & (own == n), table[n][e], unseen)
                    seen = jnp.where(here & (count == n), table[n][e], seen)
        marks.append((seen, unseen))

    lane = lax.broadcasted_iota(jnp.int32, (rows, PAIR), 1)
    row = lax.broadcasted_iota(jnp.int32, (rows, PAIR), 0)

    def prepare(u):
        aug, raw = [], []
        for d in range(per):
            ww = behind(u * per + d)
            for p in range(F):
                both = kv_in[p, ww].astype(F32)
                extra = jnp.where(row + ww * rows >= reg_ref[p], marks[p][0], marks[p][1])
                raw.append(both)
                aug.append(jnp.where(lane < DH, both, extra))
        raw = jnp.concatenate(raw, axis=0)
        keep = lax.broadcasted_iota(jnp.int32, (unit, PAIR), 1) >= DH
        kaug[u] = jnp.concatenate(aug, axis=0).astype(BF)
        vz[u] = jnp.where(keep, raw, 0.0).astype(BF)
        kt[u] = (raw * scale).T[:DH].astype(BF)

    def direct(u):
        each(max(u * per * hf, 1), (u + 1) * per * hf, relay)

    def settle(u):
        each(u * per * hf, (u + 1) * per * hf, lambda t: pass_on(sib, t).wait_recv())
        prepare(u)

    def rows_of(i):
        return pl.ds(pl.multiple_of(i * QC, QC), QC)

    def begin(b):
        top_ref[b] = jnp.full_like(top_ref[b], -3e38)
        total_ref[b] = jnp.zeros_like(total_ref[b])
        dsum_ref[b] = jnp.zeros_like(dsum_ref[b])

    def forth(u, i, b):
        at = rows_of(i)
        raw = rdot(kaug[u], qaug[at])
        old = top_ref[b]
        top = jnp.maximum(old, jnp.max(raw, axis=0, keepdims=True))
        keep = jnp.exp(old - top)
        expo = jnp.exp(raw - top)
        dprod = rdot(vz[u], xraw[at])
        sbuf[u, b] = expo
        dpbuf[u, b] = dprod
        tops[u, b] = top
        top_ref[b] = top
        total_ref[b] = total_ref[b] * keep + jnp.sum(expo, axis=0, keepdims=True)
        dsum_ref[b] = dsum_ref[b] * keep + jnp.sum(expo * dprod, axis=0, keepdims=True)

    def back(u, i, b):
        inv = 1.0 / total_ref[b]
        factor = jnp.exp(tops[u, b] - top_ref[b]) * inv
        prob = sbuf[u, b] * factor
        dscore = (prob * (dpbuf[u, b] - dsum_ref[b] * inv)).astype(BF)
        added = dot(jnp.concatenate([dscore, prob.astype(BF)], axis=1), qdz[i])
        acc[u] += added.reshape(per, F, rows, PAIR)
        dqacc[i] += dot(kt[u], dscore)

    def own_copy(block, buffer, n):
        return pltpu.make_async_copy(block, buffer.at[head], own_sem.at[n])

    def red_copy(u, dc):
        return pltpu.make_async_remote_copy(
            src_ref=red_send.at[u, dc - 1], dst_ref=red_in.at[u, dc - 1],
            send_sem=red_ss.at[u * (fs - 1) + dc - 1], recv_sem=red_rs.at[u * (fs - 1) + dc - 1],
            device_id=(a0 * fs + lax.rem(c + dc, fs), w), device_id_type=MESH)

    def ship_part(u):
        for dc in range(1, fs):
            for gi in range(R):
                red_send[u, dc - 1, gi] = acc[u, :, lax.rem(c + dc, fs) + fs * gi].astype(BF)
            red_copy(u, dc).start()

    def fin_copy(t):
        dw = lax.div(t, R)
        aa, ww = lax.rem(a0 + lax.rem(t, R), R), behind(dw)
        return pltpu.make_async_remote_copy(
            src_ref=fin_send.at[lax.div(dw, per), aa, lax.rem(dw, per)], dst_ref=fin_in.at[head],
            send_sem=fin_ss.at[t], recv_sem=fin_rs.at[head],
            device_id=(aa * fs + c, ww), device_id_type=MESH)

    def ship_home(u):
        for dc in range(1, fs):
            red_copy(u, dc).wait_recv()
        for gi in range(R):
            whole = acc[u, :, c + fs * gi]
            for dc in range(1, fs):
                whole = whole + red_in[u, dc - 1, gi].astype(F32)
            fin_send[u, gi] = whole.astype(BF)
        if u == 0:
            own_copy(fin_send.at[0, a0, 0], fin_in, 0).start()
        each(max(u * per * R, 1), (u + 1) * per * R, lambda t: fin_copy(t).start())

    def take_queries():
        each(1, R * W, lambda t: qd_arrival(t).wait_recv())
        wide = lax.broadcasted_iota(jnp.int32, (nq, PAIR), 1)
        tall = lax.broadcasted_iota(jnp.int32, (nq, PAIR), 0)
        both = qd_in[...].astype(F32).reshape(nq, PAIR)
        mark = jnp.zeros((nq, PAIR), F32)
        for gi in range(R):
            mine = (tall >= gi * seq) & (tall < (gi + 1) * seq)
            mark = jnp.where(mine & (wide >= DH + SPLITS * gi) & (wide < DH + SPLITS * (gi + 1)), 1.0, mark)
        scaled = both * scale
        qaug[...] = jnp.where(wide < DH, scaled, mark).astype(BF)
        xraw[...] = both.astype(BF)
        qdz[:, :QC] = jnp.where(wide < DH, scaled, 0.0).astype(BF).reshape(n_chunks, QC, PAIR)
        qdz[:, QC:] = jnp.where(wide >= DH, both, 0.0).astype(BF).reshape(n_chunks, QC, PAIR)

    take_queries()
    if inline:
        each(0, n_chunks, begin)
        direct(0)
        for u in range(n_units):
            settle(u)
            forth(u, 0, 0)
            if u + 1 < n_units:
                direct(u + 1)
            each(1, n_chunks, lambda i: forth(u, i, i))
        for u in range(n_units):
            back(u, 0, 0)
            if u:
                ship_home(u - 1)
            each(1, n_chunks, lambda i: back(u, i, i))
            ship_part(u)
    else:
        for u in range(n_units):
            direct(u)
        for u in range(n_units):
            settle(u)

        def block(i):
            begin(0)
            each(0, n_units, lambda u: forth(u, i, 0))
            each(0, n_units, lambda u: back(u, i, 0))

        each(0, n_chunks, block)
        for u in range(n_units):
            ship_part(u)
        for u in range(n_units - 1):
            ship_home(u)

    def dq_copy(t):
        aa, ww = lax.rem(a0 + lax.rem(t, R), R), behind(lax.div(t, R))
        return pltpu.make_async_remote_copy(
            src_ref=dq_send.at[aa, ww], dst_ref=dq_in.at[head],
            send_sem=dq_ss.at[t], recv_sem=dq_rs.at[head],
            device_id=(aa * fs + c, ww), device_id_type=MESH)

    for i in range(n_chunks):
        dqs[i * QC:(i + 1) * QC] = jnp.concatenate([dqacc[i], jnp.zeros((DH, QC), F32)], axis=0).T
    for gi in range(R):
        for ww in range(W):
            base = gi * seq + ww * rows
            dq_send[gi, ww] = jnp.concatenate(
                [dqs[base:base + half, :DH], dqs[base + rows - half:base + rows, :DH]], axis=1).astype(BF)
    own_copy(dq_send.at[a0, w], dq_in, 1).start()
    each(1, R * W, lambda t: dq_copy(t).start())
    ship_home(n_units - 1)

    each(1, R * W, lambda t: head_arrival(t, dq_in, dq_ss, dq_rs).wait_recv())
    each(1, R * W, lambda t: head_arrival(t, fin_in, fin_ss, fin_rs).wait_recv())
    each(1, hf * W, lambda t: kv_copy(t).wait_send())
    each(0, hf * W, lambda t: pass_on(f, t).wait_send())
    each(1, R * W, lambda t: qd_copy(t).wait_send())
    own_copy(fin_send.at[0, a0, 0], fin_in, 0).wait()
    own_copy(dq_send.at[a0, w], dq_in, 1).wait()
    each(1, R * W, lambda t: dq_copy(t).wait_send())
    each(1, R * W, lambda t: fin_copy(t).wait_send())
    for u in range(n_units):
        for dc in range(1, fs):
            red_copy(u, dc).wait_send()


def tokens_again(dq_in, fin_in, dq_out, dk_out, dv_out):
    half, rows, width = dq_in.shape[1], dq_out.shape[1], dq_out.shape[2]
    for j in range(width // PAIR):
        cols = slice(j * PAIR, (j + 1) * PAIR)
        sides = []
        for h in (2 * j, 2 * j + 1):
            got = dq_in[h].astype(F32)
            sides.append(jnp.concatenate([got[:, :DH], got[2 * half - rows:, DH:]], axis=0))
        dq_out[0, :, cols] = jnp.concatenate(sides, axis=1).astype(BF)

    for j in range(width // PAIR):
        cols = slice(j * PAIR, (j + 1) * PAIR)
        one, two = fin_in[2 * j], fin_in[2 * j + 1]
        dk_out[0, :, cols] = jnp.concatenate([one[:, :DH], two[:, :DH]], axis=1)
        dv_out[0, :, cols] = jnp.concatenate([one[:, DH:], two[:, DH:]], axis=1)


def local(F, W, queries, keys_in, values_in, grad_out, partners, registers):
    _, rows, width = queries.shape
    heads = width // DH
    R = heads // W
    fs = F // R
    seq = rows * W
    nq = R * seq
    half = ((rows + 1) // 2 + 7) // 8 * 8
    inline = F * seq * nq * 8 <= 24 * 2 ** 20
    QC = next(b for b in ((576, 384, 128) if inline else (128,)) if nq % b == 0)
    held = nq // QC if inline else 1
    per = next(n for n in range(W, 0, -1) if W % n == 0 and (n == 1 or n * F * rows <= UNIT))
    units = W // per
    unit = per * F * rows
    vm = lambda *shape: pltpu.VMEM(shape, BF)
    vf = lambda *shape: pltpu.VMEM(shape, F32)
    dma = lambda n: pltpu.SemaphoreType.DMA((n,))
    out = jax.ShapeDtypeStruct((1, rows, width), BF)
    dq_heads, kv_heads = pl.pallas_call(
        functools.partial(kernel, F, W, R, QC, inline),
        out_shape=(jax.ShapeDtypeStruct((heads, half, PAIR), BF), jax.ShapeDtypeStruct((heads, rows, PAIR), BF)),
        in_specs=[pl.BlockSpec(memory_space=pltpu.SMEM)] * 2 + [pl.BlockSpec(memory_space=pltpu.VMEM)] * 4,
        out_specs=(pl.BlockSpec(memory_space=pl.ANY),) * 2,
        scratch_shapes=[
            vm(heads, rows, PAIR), vm(heads, rows, PAIR),
            vm(F, W, rows, PAIR), vm(R, W, rows, PAIR),
            vm(units, unit, PAIR), vm(units, unit, PAIR), vm(units, DH, unit),
            vm(nq, PAIR), vm(nq, PAIR), vm(nq // QC, 2 * QC, PAIR),
            vf(units, held, unit, QC), vf(units, held, unit, QC), vf(units, per, F, rows, PAIR),
            vf(nq // QC, DH, QC), vf(nq, PAIR),
            vf(units, held, 1, QC), vf(held, 1, QC), vf(held, 1, QC), vf(held, 1, QC),
            vm(units, fs - 1, R, per, rows, PAIR), vm(units, fs - 1, R, per, rows, PAIR),
            vm(units, R, per, rows, PAIR), vm(R, W, half, PAIR), dma(2),
            dma(F // 2 * W), dma(F // 2 * W), dma(F * W), dma(R * W), dma(R * W),
            dma(units * (fs - 1)), dma(units * (fs - 1)), dma(R * W), dma(heads), dma(R * W), dma(heads),
        ],
        compiler_params=pltpu.CompilerParams(
            collective_id=0, has_side_effects=True, vmem_limit_bytes=60 * 2 ** 20),
    )(partners.T, registers, queries, keys_in, values_in, grad_out)
    return pl.pallas_call(
        tokens_again,
        out_shape=(out, out, out),
        in_specs=[pl.BlockSpec(memory_space=pltpu.VMEM)] * 2,
        out_specs=(pl.BlockSpec(memory_space=pltpu.VMEM),) * 3,
    )(dq_heads, kv_heads)


def halves(F, W, part_hbm, reg_hbm, q_hbm, k_hbm, v_hbm, d_hbm, dq_in, fin_in,
           part_ref, reg_ref, q_ref, k_ref, v_ref, d_ref, kv_send, qd_send, kv_in, qd_in,
           kaug, vz, kt, qaug, xraw, qdz, sbuf, dpbuf, acc, dqacc, dqs,
           tops, top_ref, total_ref, dsum_ref, st_send, st_in, fin_send, dq_send,
           in_sem, kv_ss, kv_rs, qd_ss, qd_rs, st_ss, st_rs, dq_ss, dq_rs, fin_ss, fin_rs, below, above):
    rows, width = q_ref.shape[1], q_ref.shape[2]
    n_slots = part_ref.shape[0]
    U, per = kv_in.shape[0], kv_in.shape[1]
    L = U * per
    B = 2 * U
    heads = F * L
    group = per * F
    unit = group * rows
    QP = qaug.shape[1]
    tiles = [(c, min(c + TILE, QP)) for c in range(0, QP, TILE)]
    n_subs = tops.shape[2]
    sub = unit // n_subs
    cuts = 2 if n_subs % 2 == 0 and group % 2 == 0 else 1
    scale = DH ** -0.5
    half = dq_send.shape[1]
    f = lax.axis_index("frame")
    w = lax.axis_index("within")
    block0 = lax.div(w, per)
    d0 = lax.rem(w, per)
    part = lax.div(block0, U)
    other = 1 - part
    u0 = lax.rem(block0, U)
    l = u0 * per + d0
    head = f * L + l

    barrier = pltpu.get_barrier_semaphore()

    def around(t):
        return lax.rem(d0 + lax.div(t, F), per), lax.rem(f + lax.rem(t, F), F)

    def knock(sem, block, d, ff):
        pl.semaphore_signal(sem, inc=1, device_id=(ff, block * per + d), device_id_type=MESH)

    def greet(t):
        d, ff = around(group - t)
        knock(barrier, block0, d, ff)

    @pl.when(block0 > 0)
    def _():
        knock(barrier, block0 - 1, d0, f)

    @pl.when(block0 < B - 1)
    def _():
        knock(barrier, block0 + 1, d0, f)

    each(1, group, greet)
    loads = [pltpu.make_async_copy(src, dst, in_sem.at[n]) for n, (src, dst) in enumerate(
        ((k_hbm, k_ref), (v_hbm, v_ref), (q_hbm, q_ref), (d_hbm, d_ref), (part_hbm, part_ref), (reg_hbm, reg_ref)))]
    for load in loads:
        load.start()

    for first, second, out in ((k_ref, v_ref, kv_send), (q_ref, d_ref, qd_send)):
        for load in (loads.pop(0), loads.pop(0)):
            load.wait()
        for j in range(width // PAIR):
            cols = slice(j * PAIR, (j + 1) * PAIR)
            one = first[0, :, cols]
            two = second[0, :, cols]
            out[2 * j] = jnp.concatenate([one[:, :DH], two[:, :DH]], axis=1)
            out[2 * j + 1] = jnp.concatenate([one[:, DH:], two[:, DH:]], axis=1)

    def remote(src, dst, ss, rs, device):
        return pltpu.make_async_remote_copy(src_ref=src, dst_ref=dst, send_sem=ss, recv_sem=rs,
                                            device_id=device, device_id_type=MESH)

    def head_at(block, d, ff):
        return ff * L + lax.rem(block, U) * per + d

    def kv_copy(block, t):
        d, ff = around(t)
        return remote(kv_send.at[head_at(block, d, ff)], kv_in.at[u0, d0, f], kv_ss.at[0], kv_rs.at[u0],
                      (ff, block * per + d))

    def qd_copy(block, t):
        d, ff = around(t)
        return remote(qd_send.at[head_at(block, d, ff)], qd_in.at[block0, d0, f], qd_ss.at[0], qd_rs.at[block0],
                      (ff, block * per + d))

    def send_block(block, first):
        @pl.when(lax.div(block, U) == part)
        def _():
            each(first, group, lambda t: kv_copy(block, t).start())
        each(first, group, lambda t: qd_copy(block, t).start())

    pltpu.make_async_copy(kv_send.at[head], kv_in.at[u0, d0, f], kv_rs.at[u0]).start()
    pltpu.make_async_copy(qd_send.at[head], qd_in.at[block0, d0, f], qd_rs.at[block0]).start()
    pl.semaphore_wait(barrier, group - 1 + jnp.where(block0 > 0, 1, 0) + jnp.where(block0 < B - 1, 1, 0))

    @pl.when(block0 > 0)
    def _():
        knock(above, block0 - 1, d0, f)

    @pl.when(block0 < B - 1)
    def _():
        knock(below, block0 + 1, d0, f)

    for copy in (kv_copy, qd_copy):
        for t in range(1, group):
            copy(block0, t).start()
    for n in range(1, B):
        @pl.when(block0 >= n)
        def _():
            pl.semaphore_wait(below, 1)

            @pl.when(block0 < B - 1)
            def _():
                knock(below, block0 + 1, d0, f)
            send_block(block0 - n, 0)

        @pl.when(block0 + n < B)
        def _():
            pl.semaphore_wait(above, 1)

            @pl.when(block0 > 0)
            def _():
                knock(above, block0 - 1, d0, f)
            send_block(block0 + n, 0)

    acc[...] = jnp.zeros_like(acc)
    st_send[...] = jnp.zeros_like(st_send)
    if QP > unit:
        lo, hi = tiles[-1]
        for ref, first in ((qaug, unit), (xraw, unit), (qdz, lo + unit), (qdz, hi + unit)):
            ref[:, first:first + QP - unit] = jnp.zeros((B, QP - unit, PAIR), BF)
    for load in loads:
        load.wait()

    lane1 = lax.broadcasted_iota(jnp.int32, (1, PAIR), 1)
    table = [pieces_of(HIDDEN)] + [pieces_of(math.log(n)) for n in range(1, n_slots + 2)]
    marks = []
    for p in range(F):
        seen = jnp.zeros((1, PAIR), F32)
        unseen = jnp.zeros((1, PAIR), F32)
        for g in range(F):
            own = 1 if p == g else 0
            count = own
            for slot in range(n_slots):
                count = count + jnp.where(part_ref[slot, g] == p, 1, 0)
            for e in range(SPLITS):
                here = lane1 == DH + SPLITS * g + e
                unseen = jnp.where(here, table[own][e], unseen)
                for n in range(own, n_slots + 2):
                    seen = jnp.where(here & (count == n), table[n][e], seen)
        marks.append((seen, unseen))

    lane = lax.broadcasted_iota(jnp.int32, (rows, PAIR), 1)
    row = lax.broadcasted_iota(jnp.int32, (rows, PAIR), 0)
    tall = lax.broadcasted_iota(jnp.int32, (unit, PAIR), 1)
    hot = [jnp.where((lane >= DH + SPLITS * g) & (lane < DH + SPLITS * (g + 1)), 1.0, 0.0) for g in range(F)]

    def take_keys(j):
        u = lax.rem(u0 + j, U)
        here = kv_in.at[u]
        remote(here, here, kv_ss.at[0], kv_rs.at[u], (f, w)).wait_recv()
        aug, raw = [], []
        for d in range(per):
            first = ((part * U + u) * per + d) * rows
            for p in range(F):
                both = kv_in[u, d, p].astype(F32)
                extra = jnp.where(row + first >= reg_ref[p], marks[p][0], marks[p][1])
                raw.append(both)
                aug.append(jnp.where(lane < DH, both, extra))
        raw = jnp.concatenate(raw, axis=0)
        kaug[j] = jnp.concatenate(aug, axis=0).astype(BF)
        vz[j] = jnp.where(tall >= DH, raw, 0.0).astype(BF)
        kt[j] = (raw * scale).T[:DH].astype(BF)

    def take_queries(i):
        here = qd_in.at[i]
        remote(here, here, qd_ss.at[0], qd_rs.at[i], (f, w)).wait_recv()
        raw, aug = [], []
        for d in range(per):
            for g in range(F):
                both = qd_in[i, d, g].astype(F32)
                raw.append(both)
                aug.append(jnp.where(lane < DH, both * scale, hot[g]))
        raw = jnp.concatenate(raw, axis=0)
        qaug[i, :unit] = jnp.concatenate(aug, axis=0).astype(BF)
        xraw[i, :unit] = raw.astype(BF)
        for value, side in ((jnp.where(tall < DH, raw * scale, 0.0), 0), (jnp.where(tall >= DH, raw, 0.0), 1)):
            for lo, hi in tiles:
                first, n = 2 * lo + side * (hi - lo), min(hi, unit) - lo
                qdz[i, first:first + n] = value[lo:lo + n].astype(BF)

    def forth(j, i):
        for lo, hi in tiles:
            raw = rdot(kaug[j], qaug[i, lo:hi])
            dprod = rdot(vz[j], xraw[i, lo:hi])
            if j:
                top, total, dsum = top_ref[i, :, lo:hi], total_ref[i, :, lo:hi], dsum_ref[i, :, lo:hi]
            for s in range(n_subs):
                at = slice(s * sub, (s + 1) * sub)
                part_raw = raw[at].reshape(sub // 8, 8, hi - lo)
                part_dp = dprod[at].reshape(sub // 8, 8, hi - lo)
                peak = jnp.max(part_raw, axis=0)
                if j or s:
                    peak = jnp.maximum(top, peak)
                expo = jnp.exp(part_raw - peak[None])
                more, dmore = jnp.sum(expo, axis=0), jnp.sum(expo * part_dp, axis=0)
                if j or s:
                    keep = jnp.exp(top - peak)
                    more, dmore = total * keep + more, dsum * keep + dmore
                top, total, dsum = peak, more, dmore
                sbuf[j, i, at, lo:hi] = expo.reshape(sub, hi - lo)
                dpbuf[j, i, at, lo:hi] = part_dp.reshape(sub, hi - lo)
                tops[j, i, s, :, lo:hi] = peak
            top_ref[i, :, lo:hi] = top
            total_ref[i, :, lo:hi] = total
            dsum_ref[i, :, lo:hi] = dsum

    spans = [(c, c + PAIR) for c in range(0, QP, PAIR)]

    def give(i):
        peak = jnp.max(top_ref[i], axis=0, keepdims=True)
        keep = jnp.exp(top_ref[i] - peak)
        total = jnp.sum(total_ref[i] * keep, axis=0, keepdims=True)
        dsum = jnp.sum(dsum_ref[i] * keep, axis=0, keepdims=True)
        for s, value in enumerate((peak, total, dsum)):
            for n, (lo, hi) in enumerate(spans):
                at = s * len(spans) + n
                st_send[i, at:at + 1] = value[:, lo:hi]
        remote(st_send.at[i], st_in.at[i], st_ss.at[0], st_rs.at[i], (f, other * L + l)).start()

    def meet(i):
        here = st_in.at[i]
        remote(here, here, st_ss.at[0], st_rs.at[i], (f, other * L + l)).wait_recv()
        def row_of(ref, s):
            return jnp.concatenate(
                [ref[i, s * len(spans) + n:s * len(spans) + n + 1] for n in range(len(spans))], axis=1)

        mine, yours = [[row_of(ref, s) for s in range(3)] for ref in (st_send, st_in)]
        peak = jnp.maximum(mine[0], yours[0])
        a, b = jnp.exp(mine[0] - peak), jnp.exp(yours[0] - peak)
        inv = 1.0 / (mine[1] * a + yours[1] * b)
        whole = (8, QP)
        top_ref[i] = jnp.broadcast_to(peak, whole)
        total_ref[i] = jnp.broadcast_to(inv, whole)
        dsum_ref[i] = jnp.broadcast_to((mine[2] * a + yours[2] * b) * inv, whole)

    def back(j, i):
        for lo, hi in tiles:
            probs, dscores = [], []
            for s in range(n_subs):
                at = slice(s * sub, (s + 1) * sub)
                factor = jnp.exp(tops[j, i, s, :, lo:hi] - top_ref[i, :, lo:hi]) * total_ref[i, :, lo:hi]
                prob = sbuf[j, i, at, lo:hi].reshape(sub // 8, 8, hi - lo) * factor[None]
                dprod = dpbuf[j, i, at, lo:hi].reshape(sub // 8, 8, hi - lo)
                dscore = prob * (dprod - dsum_ref[i, :, lo:hi][None])
                probs.append(prob.reshape(sub, hi - lo).astype(BF))
                dscores.append(dscore.reshape(sub, hi - lo).astype(BF))
            for first in range(0, n_subs, n_subs // cuts):
                some = slice(first, first + n_subs // cuts)
                both = [jnp.concatenate(x[some], axis=0) for x in (dscores, probs)]
                added = dot(jnp.concatenate(both, axis=1), qdz[i, 2 * lo:2 * hi])
                at = slice(first * group // n_subs, (first + n_subs // cuts) * group // n_subs)
                acc[j, at] += added.reshape(group // cuts, rows, PAIR)
            more = dot(kt[j], jnp.concatenate(dscores, axis=0))
            if j < U - 1:
                more = dqacc[i, :, lo:hi] + more
            dqacc[i, :, lo:hi] = more

    def dq_copy(i, t):
        d, ff = around(t)
        return remote(dq_send.at[i * group + d * F + ff], dq_in.at[part, head], dq_ss.at[0], dq_rs.at[part], (ff, i * per + d))

    def ship_queries(i, own):
        dqs[...] = jnp.concatenate([dqacc[i], jnp.zeros((DH, QP), F32)], axis=0).T
        for d in range(per):
            for g in range(F):
                base = (d * F + g) * rows
                dq_send[i * group + d * F + g] = jnp.concatenate(
                    [dqs[base:base + half, :DH], dqs[base + rows - half:base + rows, :DH]], axis=1).astype(BF)

        if own:
            pltpu.make_async_copy(dq_send.at[i * group + d0 * F + f], dq_in.at[part, head], dq_rs.at[part]).start()
        for t in range(1 if own else 0, group):
            dq_copy(i, t).start()

    def fin_copy(j, t):
        d, ff = around(t)
        return remote(fin_send.at[j * group + d * F + ff], fin_in.at[head], fin_ss.at[0], fin_rs.at[0],
                      (ff, (part * U + lax.rem(u0 + j, U)) * per + d))

    def ship_keys(j):
        fin_send[j * group:(j + 1) * group] = acc[j].astype(BF)
        if j == 0:
            pltpu.make_async_copy(fin_send.at[d0 * F + f], fin_in.at[head], fin_rs.at[0]).start()
        for t in range(0 if j else 1, group):
            fin_copy(j, t).start()

    def local(n):
        return part * U + lax.rem(u0 + n, U)

    def remote_block(n):
        return other * U + n + part * (U - 1 - 2 * n)

    edge = jnp.where(part == 0, U - 1, 0) == u0
    order = [local(0)]
    for n in range(U - 1):
        order.append(jnp.where(edge, remote_block(n), local(n + 1)))
        order.append(jnp.where(edge, local(n + 1), remote_block(n)))
    order.append(remote_block(U - 1))

    for n, i in enumerate(order):
        if n:
            take_queries(i)
        for j in range(U):
            if n == 0:
                take_keys(j)
                if j == 0:
                    take_queries(i)
            forth(j, i)
        give(i)
    last = [remote_block(U - 1 - n) for n in range(U)]
    for i in last:
        meet(i)
        for j in reversed(range(U)):
            back(j, i)
        ship_queries(i, False)
    mine = [local(n) for n in reversed(range(U))]
    for i in mine:
        meet(i)
    for j in reversed(range(U)):
        for n, i in enumerate(mine):
            back(j, i)
            if j == 0:
                ship_queries(i, n == U - 1)
        ship_keys(j)

    def sent(ref, sem):
        remote(ref, ref, sem.at[0], sem.at[0], (f, w)).wait_send()

    sent(kv_send.at[pl.ds(0, heads - 1)], kv_ss)
    sent(qd_send, qd_ss)
    sent(qd_send.at[pl.ds(0, heads - 1)], qd_ss)
    sent(st_send, st_ss)
    for side in (other, part):
        here = dq_in.at[side]
        remote(here, here, dq_ss.at[0], dq_rs.at[side], (f, w)).wait_recv()
    remote(fin_in, fin_in, fin_ss.at[0], fin_rs.at[0], (f, w)).wait_recv()
    sent(dq_send.at[pl.ds(0, B * group - 1)], dq_ss)
    sent(fin_send.at[pl.ds(0, U * group - 1)], fin_ss)


def both_halves(dq_in, fin_in, dq_out, dk_out, dv_out):
    half, rows, width = dq_in.shape[2], dq_out.shape[1], dq_out.shape[2]
    for j in range(width // PAIR):
        cols = slice(j * PAIR, (j + 1) * PAIR)
        sides = []
        for h in (2 * j, 2 * j + 1):
            got = dq_in[0, h].astype(F32) + dq_in[1, h].astype(F32)
            sides.append(jnp.concatenate([got[:, :DH], got[2 * half - rows:, DH:]], axis=0))
        dq_out[0, :, cols] = jnp.concatenate(sides, axis=1).astype(BF)
        one, two = fin_in[2 * j], fin_in[2 * j + 1]
        dk_out[0, :, cols] = jnp.concatenate([one[:, :DH], two[:, :DH]], axis=1)
        dv_out[0, :, cols] = jnp.concatenate([one[:, DH:], two[:, DH:]], axis=1)


def local_halves(F, W, queries, keys_in, values_in, grad_out, partners, registers):
    _, rows, width = queries.shape
    heads = width // DH
    L = W // 2
    half = ((rows + 1) // 2 + 7) // 8 * 8
    per = next(n for n in range(L, 0, -1) if L % n == 0 and (n == 1 or n * F * rows <= UNIT))
    U = L // per
    unit = per * F * rows
    C = 2 * U
    QP = (unit + PAIR - 1) // PAIR * PAIR
    subs = unit // next(n for n in range(SUB, 0, -8) if unit % n == 0)
    stats = (3 * (QP // PAIR) + 7) // 8 * 8
    vm = lambda *shape: pltpu.VMEM(shape, BF)
    vf = lambda *shape: pltpu.VMEM(shape, F32)
    dma = lambda n: pltpu.SemaphoreType.DMA((n,))
    out = jax.ShapeDtypeStruct((1, rows, width), BF)
    dq_heads, kv_heads = pl.pallas_call(
        functools.partial(halves, F, W),
        out_shape=(jax.ShapeDtypeStruct((2, heads, half, PAIR), BF), jax.ShapeDtypeStruct((heads, rows, PAIR), BF)),
        in_specs=[pl.BlockSpec(memory_space=pl.ANY)] * 6,
        out_specs=(pl.BlockSpec(memory_space=pl.ANY),) * 2,
        scratch_shapes=[
            pltpu.SMEM(partners.T.shape, jnp.int32), pltpu.SMEM(registers.shape, jnp.int32),
            vm(1, rows, width), vm(1, rows, width), vm(1, rows, width), vm(1, rows, width),
            vm(heads, rows, PAIR), vm(heads, rows, PAIR), vm(U, per, F, rows, PAIR), vm(C, per, F, rows, PAIR),
            vm(U, unit, PAIR), vm(U, unit, PAIR), vm(U, DH, unit),
            vm(C, QP, PAIR), vm(C, QP, PAIR), vm(C, 2 * QP, PAIR),
            vf(U, C, unit, QP), vf(U, C, unit, QP), vf(U, per * F, rows, PAIR),
            vf(C, DH, QP), vf(QP, PAIR),
            vf(U, C, subs, 8, QP), vf(C, 8, QP), vf(C, 8, QP), vf(C, 8, QP),
            vf(C, stats, PAIR), vf(C, stats, PAIR),
            vm(heads, rows, PAIR), vm(C * per * F, half, PAIR),
            dma(6), dma(1), dma(U), dma(1), dma(C), dma(1), dma(C), dma(1), dma(2), dma(1), dma(1),
            pltpu.SemaphoreType.REGULAR, pltpu.SemaphoreType.REGULAR,
        ],
        compiler_params=pltpu.CompilerParams(
            collective_id=0, has_side_effects=True, vmem_limit_bytes=40 * 2 ** 20),
    )(*[pltpu.with_memory_space_constraint(x, pltpu.HBM) for x in (
        partners.T, registers, queries, keys_in, values_in, grad_out)])
    return pl.pallas_call(
        both_halves,
        out_shape=(out, out, out),
        in_specs=[pl.BlockSpec(memory_space=pltpu.VMEM)] * 2,
        out_specs=(pl.BlockSpec(memory_space=pltpu.VMEM),) * 3,
        compiler_params=pltpu.CompilerParams(vmem_limit_bytes=8 * 2 ** 20),
    )(dq_heads, kv_heads)


def choose(F, W, queries, *others):
    _, rows, width = queries.shape
    heads = width // DH
    held = 2 * F * W // 2 * rows * F * W * rows * 4
    if W % 2 == 0 and F * W == 2 * heads and SPLITS * F <= DH and held <= 24 * 2 ** 20:
        return local_halves(F, W, queries, *others)
    return local(F, W, queries, *others)


def solution(mesh):
    spec = P("frame", "within", None)
    return jax.shard_map(
        functools.partial(choose, mesh.shape["frame"], mesh.shape["within"]),
        mesh=mesh,
        in_specs=(spec, spec, spec, spec, P(), P()),
        out_specs=(spec, spec, spec),
        check_vma=False,
    )
```

```python
import functools
import math

import jax
import jax.numpy as jnp
import numpy as np
from jax import lax
from jax.experimental import pallas as pl
from jax.experimental.pallas import tpu as pltpu
from jax.sharding import PartitionSpec as P

DH = 64
PAIR = 2 * DH
SPLITS = 3
UNIT = 640
TILE = 256
SUB = 144
HIDDEN = -1e30
BF = jnp.bfloat16
F32 = jnp.float32
MESH = pl.DeviceIdType.MESH


def pieces_of(value):
    left, out = float(value), []
    for _ in range(SPLITS):
        part = float(np.asarray(left, dtype=jnp.bfloat16))
        out.append(part)
        left = left - part if abs(value) < 1e20 else 0.0
    return out


def rdot(a, b):
    return lax.dot_general(a, b, (((1,), (1,)), ((), ())), preferred_element_type=F32)


def dot(a, b):
    return jnp.dot(a, b, preferred_element_type=F32)


def each(lo, hi, do):
    def step(t, carry):
        do(t)
        return carry
    lax.fori_loop(lo, hi, step, 0)


def kernel(F, W, R, QC, inline, part_ref, reg_ref, q_ref, k_ref, v_ref, d_ref, dq_in, fin_in,
           kv_send, qd_send, kv_in, qd_in, kaug, vz, kt, qaug, xraw, qdz, sbuf, dpbuf, acc, dqacc, dqs,
           tops, top_ref, total_ref, dsum_ref,
           red_send, red_in, fin_send, dq_send, own_sem,
           kv_ss, fw_ss, kv_rs, qd_ss, qd_rs, red_ss, red_rs, fin_ss, fin_rs, dq_ss, dq_rs):
    fs = F // R
    hf = F // 2
    rows = q_ref.shape[1]
    width = q_ref.shape[2]
    seq = rows * W
    n_slots = part_ref.shape[0]
    scale = DH ** -0.5
    half = dq_send.shape[2]
    nq = R * seq
    n_chunks = nq // QC
    n_units, per = acc.shape[0], acc.shape[1]
    unit = per * F * rows
    f = lax.axis_index("frame")
    w = lax.axis_index("within")
    c = lax.rem(f, fs)
    a0 = lax.div(f, fs)
    sib = f + 1 - 2 * lax.rem(f, 2)
    head = w * R + a0

    barrier = pltpu.get_barrier_semaphore()

    def ahead(dw):
        return lax.rem(w + W - dw, W)

    def behind(dw):
        return lax.rem(w + dw, W)

    def greet(t):
        pl.semaphore_signal(barrier, inc=1, device_id=(lax.rem(f + 2 * lax.rem(t, hf), F), ahead(lax.div(t, hf))),
                            device_id_type=MESH)

    each(1, hf * W, greet)
    for dc in range(1, fs, 2):
        pl.semaphore_signal(barrier, inc=1, device_id=(a0 * fs + lax.rem(c + dc, fs), w), device_id_type=MESH)

    for first, second, out in ((q_ref, d_ref, qd_send), (k_ref, v_ref, kv_send)):
        for j in range(width // PAIR):
            cols = slice(j * PAIR, (j + 1) * PAIR)
            one = first[0, :, cols]
            two = second[0, :, cols]
            out[2 * j] = jnp.concatenate([one[:, :DH], two[:, :DH]], axis=1)
            out[2 * j + 1] = jnp.concatenate([one[:, DH:], two[:, DH:]], axis=1)
    kv_in[f, w] = kv_send[head]
    qd_in[a0, w] = qd_send[head]

    pl.semaphore_wait(barrier, hf * W - 1 + fs // 2)

    def kv_copy(t):
        ff = lax.rem(f + 2 * lax.rem(t, hf), F)
        ww = ahead(lax.div(t, hf))
        return pltpu.make_async_remote_copy(
            src_ref=kv_send.at[ww * R + lax.div(ff, fs)], dst_ref=kv_in.at[f, w],
            send_sem=kv_ss.at[t], recv_sem=kv_rs.at[f * W + w],
            device_id=(ff, ww), device_id_type=MESH)

    def pass_on(origin, t):
        ff = lax.rem(origin + F - 2 * lax.rem(t, hf), F)
        ww = behind(lax.div(t, hf))
        return pltpu.make_async_remote_copy(
            src_ref=kv_in.at[ff, ww], dst_ref=kv_in.at[ff, ww],
            send_sem=fw_ss.at[t], recv_sem=kv_rs.at[ff * W + ww],
            device_id=(sib, w), device_id_type=MESH)

    def qd_copy(t):
        aa, ww = lax.rem(a0 + lax.rem(t, R), R), ahead(lax.div(t, R))
        return pltpu.make_async_remote_copy(
            src_ref=qd_send.at[ww * R + aa], dst_ref=qd_in.at[a0, w],
            send_sem=qd_ss.at[t], recv_sem=qd_rs.at[a0 * W + w],
            device_id=(aa * fs + c, ww), device_id_type=MESH)

    def arrival(t, buffer, send, recv, index, source):
        return pltpu.make_async_remote_copy(
            src_ref=buffer.at[index], dst_ref=buffer.at[index], send_sem=send.at[t], recv_sem=recv,
            device_id=source, device_id_type=MESH)

    def qd_arrival(t):
        aa, ww = lax.rem(a0 + R - lax.rem(t, R), R), behind(lax.div(t, R))
        return arrival(t, qd_in, qd_ss, qd_rs.at[aa * W + ww], (aa, ww), (aa * fs + c, ww))

    def head_arrival(t, buffer, send, recv):
        aa, ww = lax.rem(a0 + R - lax.rem(t, R), R), ahead(lax.div(t, R))
        return arrival(t, buffer, send, recv.at[ww * R + aa], (ww * R + aa,), (aa * fs + c, ww))

    each(1, R * W, lambda t: qd_copy(t).start())
    pass_on(f, 0).start()
    each(1, hf * W, lambda t: kv_copy(t).start())

    acc[...] = jnp.zeros_like(acc)
    dqacc[...] = jnp.zeros_like(dqacc)

    def relay(t):
        move = pass_on(f, t)
        move.wait_recv()
        move.start()

    lane1 = lax.broadcasted_iota(jnp.int32, (1, PAIR), 1)
    table = [pieces_of(HIDDEN)] + [pieces_of(math.log(n)) for n in range(1, n_slots + 2)]
    marks = []
    for p in range(F):
        seen = jnp.zeros((1, PAIR), F32)
        unseen = jnp.zeros((1, PAIR), F32)
        for gi in range(R):
            g = c + fs * gi
            own = jnp.where(p == g, 1, 0)
            count = own
            for slot in range(n_slots):
                count = count + jnp.where(part_ref[slot, g] == p, 1, 0)
            for e in range(SPLITS):
                here = lane1 == DH + SPLITS * gi + e
                for n in range(n_slots + 2):
                    if n < 2:
                        unseen = jnp.where(here & (own == n), table[n][e], unseen)
                    seen = jnp.where(here & (count == n), table[n][e], seen)
        marks.append((seen, unseen))

    lane = lax.broadcasted_iota(jnp.int32, (rows, PAIR), 1)
    row = lax.broadcasted_iota(jnp.int32, (rows, PAIR), 0)

    def prepare(u):
        aug, raw = [], []
        for d in range(per):
            ww = behind(u * per + d)
            for p in range(F):
                both = kv_in[p, ww].astype(F32)
                extra = jnp.where(row + ww * rows >= reg_ref[p], marks[p][0], marks[p][1])
                raw.append(both)
                aug.append(jnp.where(lane < DH, both, extra))
        raw = jnp.concatenate(raw, axis=0)
        keep = lax.broadcasted_iota(jnp.int32, (unit, PAIR), 1) >= DH
        kaug[u] = jnp.concatenate(aug, axis=0).astype(BF)
        vz[u] = jnp.where(keep, raw, 0.0).astype(BF)
        kt[u] = (raw * scale).T[:DH].astype(BF)

    def direct(u):
        each(max(u * per * hf, 1), (u + 1) * per * hf, relay)

    def settle(u):
        each(u * per * hf, (u + 1) * per * hf, lambda t: pass_on(sib, t).wait_recv())
        prepare(u)

    def rows_of(i):
        return pl.ds(pl.multiple_of(i * QC, QC), QC)

    def begin(b):
        top_ref[b] = jnp.full_like(top_ref[b], -3e38)
        total_ref[b] = jnp.zeros_like(total_ref[b])
        dsum_ref[b] = jnp.zeros_like(dsum_ref[b])

    def forth(u, i, b):
        at = rows_of(i)
        raw = rdot(kaug[u], qaug[at])
        old = top_ref[b]
        top = jnp.maximum(old, jnp.max(raw, axis=0, keepdims=True))
        keep = jnp.exp(old - top)
        expo = jnp.exp(raw - top)
        dprod = rdot(vz[u], xraw[at])
        sbuf[u, b] = expo
        dpbuf[u, b] = dprod
        tops[u, b] = top
        top_ref[b] = top
        total_ref[b] = total_ref[b] * keep + jnp.sum(expo, axis=0, keepdims=True)
        dsum_ref[b] = dsum_ref[b] * keep + jnp.sum(expo * dprod, axis=0, keepdims=True)

    def back(u, i, b):
        inv = 1.0 / total_ref[b]
        factor = jnp.exp(tops[u, b] - top_ref[b]) * inv
        prob = sbuf[u, b] * factor
        dscore = (prob * (dpbuf[u, b] - dsum_ref[b] * inv)).astype(BF)
        added = dot(jnp.concatenate([dscore, prob.astype(BF)], axis=1), qdz[i])
        acc[u] += added.reshape(per, F, rows, PAIR)
        dqacc[i] += dot(kt[u], dscore)

    def own_copy(block, buffer, n):
        return pltpu.make_async_copy(block, buffer.at[head], own_sem.at[n])

    def red_copy(u, dc):
        return pltpu.make_async_remote_copy(
            src_ref=red_send.at[u, dc - 1], dst_ref=red_in.at[u, dc - 1],
            send_sem=red_ss.at[u * (fs - 1) + dc - 1], recv_sem=red_rs.at[u * (fs - 1) + dc - 1],
            device_id=(a0 * fs + lax.rem(c + dc, fs), w), device_id_type=MESH)

    def ship_part(u):
        for dc in range(1, fs):
            for gi in range(R):
                red_send[u, dc - 1, gi] = acc[u, :, lax.rem(c + dc, fs) + fs * gi].astype(BF)
            red_copy(u, dc).start()

    def fin_copy(t):
        dw = lax.div(t, R)
        aa, ww = lax.rem(a0 + lax.rem(t, R), R), behind(dw)
        return pltpu.make_async_remote_copy(
            src_ref=fin_send.at[lax.div(dw, per), aa, lax.rem(dw, per)], dst_ref=fin_in.at[head],
            send_sem=fin_ss.at[t], recv_sem=fin_rs.at[head],
            device_id=(aa * fs + c, ww), device_id_type=MESH)

    def ship_home(u):
        for dc in range(1, fs):
            red_copy(u, dc).wait_recv()
        for gi in range(R):
            whole = acc[u, :, c + fs * gi]
            for dc in range(1, fs):
                whole = whole + red_in[u, dc - 1, gi].astype(F32)
            fin_send[u, gi] = whole.astype(BF)
        if u == 0:
            own_copy(fin_send.at[0, a0, 0], fin_in, 0).start()
        each(max(u * per * R, 1), (u + 1) * per * R, lambda t: fin_copy(t).start())

    def take_queries():
        each(1, R * W, lambda t: qd_arrival(t).wait_recv())
        wide = lax.broadcasted_iota(jnp.int32, (nq, PAIR), 1)
        tall = lax.broadcasted_iota(jnp.int32, (nq, PAIR), 0)
        both = qd_in[...].astype(F32).reshape(nq, PAIR)
        mark = jnp.zeros((nq, PAIR), F32)
        for gi in range(R):
            mine = (tall >= gi * seq) & (tall < (gi + 1) * seq)
            mark = jnp.where(mine & (wide >= DH + SPLITS * gi) & (wide < DH + SPLITS * (gi + 1)), 1.0, mark)
        scaled = both * scale
        qaug[...] = jnp.where(wide < DH, scaled, mark).astype(BF)
        xraw[...] = both.astype(BF)
        qdz[:, :QC] = jnp.where(wide < DH, scaled, 0.0).astype(BF).reshape(n_chunks, QC, PAIR)
        qdz[:, QC:] = jnp.where(wide >= DH, both, 0.0).astype(BF).reshape(n_chunks, QC, PAIR)

    take_queries()
    if inline:
        each(0, n_chunks, begin)
        direct(0)
        for u in range(n_units):
            settle(u)
            forth(u, 0, 0)
            if u + 1 < n_units:
                direct(u + 1)
            each(1, n_chunks, lambda i: forth(u, i, i))
        for u in range(n_units):
            back(u, 0, 0)
            if u:
                ship_home(u - 1)
            each(1, n_chunks, lambda i: back(u, i, i))
            ship_part(u)
    else:
        for u in range(n_units):
            direct(u)
        for u in range(n_units):
            settle(u)

        def block(i):
            begin(0)
            each(0, n_units, lambda u: forth(u, i, 0))
            each(0, n_units, lambda u: back(u, i, 0))

        each(0, n_chunks, block)
        for u in range(n_units):
            ship_part(u)
        for u in range(n_units - 1):
            ship_home(u)

    def dq_copy(t):
        aa, ww = lax.rem(a0 + lax.rem(t, R), R), behind(lax.div(t, R))
        return pltpu.make_async_remote_copy(
            src_ref=dq_send.at[aa, ww], dst_ref=dq_in.at[head],
            send_sem=dq_ss.at[t], recv_sem=dq_rs.at[head],
            device_id=(aa * fs + c, ww), device_id_type=MESH)

    for i in range(n_chunks):
        dqs[i * QC:(i + 1) * QC] = jnp.concatenate([dqacc[i], jnp.zeros((DH, QC), F32)], axis=0).T
    for gi in range(R):
        for ww in range(W):
            base = gi * seq + ww * rows
            dq_send[gi, ww] = jnp.concatenate(
                [dqs[base:base + half, :DH], dqs[base + rows - half:base + rows, :DH]], axis=1).astype(BF)
    own_copy(dq_send.at[a0, w], dq_in, 1).start()
    each(1, R * W, lambda t: dq_copy(t).start())
    ship_home(n_units - 1)

    each(1, R * W, lambda t: head_arrival(t, dq_in, dq_ss, dq_rs).wait_recv())
    each(1, R * W, lambda t: head_arrival(t, fin_in, fin_ss, fin_rs).wait_recv())
    each(1, hf * W, lambda t: kv_copy(t).wait_send())
    each(0, hf * W, lambda t: pass_on(f, t).wait_send())
    each(1, R * W, lambda t: qd_copy(t).wait_send())
    own_copy(fin_send.at[0, a0, 0], fin_in, 0).wait()
    own_copy(dq_send.at[a0, w], dq_in, 1).wait()
    each(1, R * W, lambda t: dq_copy(t).wait_send())
    each(1, R * W, lambda t: fin_copy(t).wait_send())
    for u in range(n_units):
        for dc in range(1, fs):
            red_copy(u, dc).wait_send()


def tokens_again(dq_in, fin_in, dq_out, dk_out, dv_out):
    half, rows, width = dq_in.shape[1], dq_out.shape[1], dq_out.shape[2]
    for j in range(width // PAIR):
        cols = slice(j * PAIR, (j + 1) * PAIR)
        sides = []
        for h in (2 * j, 2 * j + 1):
            got = dq_in[h].astype(F32)
            sides.append(jnp.concatenate([got[:, :DH], got[2 * half - rows:, DH:]], axis=0))
        dq_out[0, :, cols] = jnp.concatenate(sides, axis=1).astype(BF)

    for j in range(width // PAIR):
        cols = slice(j * PAIR, (j + 1) * PAIR)
        one, two = fin_in[2 * j], fin_in[2 * j + 1]
        dk_out[0, :, cols] = jnp.concatenate([one[:, :DH], two[:, :DH]], axis=1)
        dv_out[0, :, cols] = jnp.concatenate([one[:, DH:], two[:, DH:]], axis=1)


def local(F, W, queries, keys_in, values_in, grad_out, partners, registers):
    _, rows, width = queries.shape
    heads = width // DH
    R = heads // W
    fs = F // R
    seq = rows * W
    nq = R * seq
    half = ((rows + 1) // 2 + 7) // 8 * 8
    inline = F * seq * nq * 8 <= 24 * 2 ** 20
    QC = next(b for b in ((576, 384, 128) if inline else (128,)) if nq % b == 0)
    held = nq // QC if inline else 1
    per = next(n for n in range(W, 0, -1) if W % n == 0 and (n == 1 or n * F * rows <= UNIT))
    units = W // per
    unit = per * F * rows
    vm = lambda *shape: pltpu.VMEM(shape, BF)
    vf = lambda *shape: pltpu.VMEM(shape, F32)
    dma = lambda n: pltpu.SemaphoreType.DMA((n,))
    out = jax.ShapeDtypeStruct((1, rows, width), BF)
    dq_heads, kv_heads = pl.pallas_call(
        functools.partial(kernel, F, W, R, QC, inline),
        out_shape=(jax.ShapeDtypeStruct((heads, half, PAIR), BF), jax.ShapeDtypeStruct((heads, rows, PAIR), BF)),
        in_specs=[pl.BlockSpec(memory_space=pltpu.SMEM)] * 2 + [pl.BlockSpec(memory_space=pltpu.VMEM)] * 4,
        out_specs=(pl.BlockSpec(memory_space=pl.ANY),) * 2,
        scratch_shapes=[
            vm(heads, rows, PAIR), vm(heads, rows, PAIR),
            vm(F, W, rows, PAIR), vm(R, W, rows, PAIR),
            vm(units, unit, PAIR), vm(units, unit, PAIR), vm(units, DH, unit),
            vm(nq, PAIR), vm(nq, PAIR), vm(nq // QC, 2 * QC, PAIR),
            vf(units, held, unit, QC), vf(units, held, unit, QC), vf(units, per, F, rows, PAIR),
            vf(nq // QC, DH, QC), vf(nq, PAIR),
            vf(units, held, 1, QC), vf(held, 1, QC), vf(held, 1, QC), vf(held, 1, QC),
            vm(units, fs - 1, R, per, rows, PAIR), vm(units, fs - 1, R, per, rows, PAIR),
            vm(units, R, per, rows, PAIR), vm(R, W, half, PAIR), dma(2),
            dma(F // 2 * W), dma(F // 2 * W), dma(F * W), dma(R * W), dma(R * W),
            dma(units * (fs - 1)), dma(units * (fs - 1)), dma(R * W), dma(heads), dma(R * W), dma(heads),
        ],
        compiler_params=pltpu.CompilerParams(
            collective_id=0, has_side_effects=True, vmem_limit_bytes=60 * 2 ** 20),
    )(partners.T, registers, queries, keys_in, values_in, grad_out)
    return pl.pallas_call(
        tokens_again,
        out_shape=(out, out, out),
        in_specs=[pl.BlockSpec(memory_space=pltpu.VMEM)] * 2,
        out_specs=(pl.BlockSpec(memory_space=pltpu.VMEM),) * 3,
    )(dq_heads, kv_heads)


def halves(F, W, part_hbm, reg_hbm, q_hbm, k_hbm, v_hbm, d_hbm, dq_in, fin_in,
           part_ref, reg_ref, q_ref, k_ref, v_ref, d_ref, kv_send, qd_send, kv_in, qd_in,
           kaug, vz, kt, qaug, xraw, qdz, sbuf, dpbuf, acc, dqacc, dqs,
           tops, top_ref, total_ref, dsum_ref, st_send, st_in, fin_send, dq_send,
           in_sem, kv_ss, kv_rs, qd_ss, qd_rs, st_ss, st_rs, dq_ss, dq_rs, fin_ss, fin_rs, below, above):
    rows, width = q_ref.shape[1], q_ref.shape[2]
    n_slots = part_ref.shape[0]
    U, per = kv_in.shape[0], kv_in.shape[1]
    L = U * per
    B = 2 * U
    heads = F * L
    group = per * F
    unit = group * rows
    QP = qaug.shape[1]
    tiles = [(c, min(c + TILE, QP)) for c in range(0, QP, TILE)]
    n_subs = tops.shape[2]
    sub = unit // n_subs
    cuts = 2 if n_subs % 2 == 0 and group % 2 == 0 else 1
    scale = DH ** -0.5
    half = dq_send.shape[1]
    f = lax.axis_index("frame")
    w = lax.axis_index("within")
    block0 = lax.div(w, per)
    d0 = lax.rem(w, per)
    part = lax.div(block0, U)
    other = 1 - part
    u0 = lax.rem(block0, U)
    l = u0 * per + d0
    head = f * L + l

    barrier = pltpu.get_barrier_semaphore()

    def around(t):
        return lax.rem(d0 + lax.div(t, F), per), lax.rem(f + lax.rem(t, F), F)

    def knock(sem, block, d, ff):
        pl.semaphore_signal(sem, inc=1, device_id=(ff, block * per + d), device_id_type=MESH)

    def greet(t):
        d, ff = around(group - t)
        knock(barrier, block0, d, ff)

    loads = [pltpu.make_async_copy(src, dst, in_sem.at[n]) for n, (src, dst) in enumerate(
        ((k_hbm, k_ref), (v_hbm, v_ref), (q_hbm, q_ref), (d_hbm, d_ref), (part_hbm, part_ref), (reg_hbm, reg_ref)))]
    for load in loads:
        load.start()

    @pl.when(block0 > 0)
    def _():
        knock(barrier, block0 - 1, d0, f)

    @pl.when(block0 < B - 1)
    def _():
        knock(barrier, block0 + 1, d0, f)

    each(1, group, greet)
    def pack(first, second, out):
        for load in (loads.pop(0), loads.pop(0)):
            load.wait()
        for j in range(width // PAIR):
            cols = slice(j * PAIR, (j + 1) * PAIR)
            one = first[0, :, cols]
            two = second[0, :, cols]
            out[2 * j] = jnp.concatenate([one[:, :DH], two[:, :DH]], axis=1)
            out[2 * j + 1] = jnp.concatenate([one[:, DH:], two[:, DH:]], axis=1)

    pack(k_ref, v_ref, kv_send)
    pl.semaphore_wait(barrier, group - 1 + jnp.where(block0 > 0, 1, 0) + jnp.where(block0 < B - 1, 1, 0))

    @pl.when(block0 > 0)
    def _():
        knock(above, block0 - 1, d0, f)

    @pl.when(block0 < B - 1)
    def _():
        knock(below, block0 + 1, d0, f)

    pack(q_ref, d_ref, qd_send)

    def remote(src, dst, ss, rs, device):
        return pltpu.make_async_remote_copy(src_ref=src, dst_ref=dst, send_sem=ss, recv_sem=rs,
                                            device_id=device, device_id_type=MESH)

    def head_at(block, d, ff):
        return ff * L + lax.rem(block, U) * per + d

    def kv_copy(block, t):
        d, ff = around(t)
        return remote(kv_send.at[head_at(block, d, ff)], kv_in.at[u0, d0, f], kv_ss.at[0], kv_rs.at[u0],
                      (ff, block * per + d))

    def qd_copy(block, t):
        d, ff = around(t)
        return remote(qd_send.at[head_at(block, d, ff)], qd_in.at[block0, d0, f], qd_ss.at[0], qd_rs.at[block0],
                      (ff, block * per + d))

    def send_block(block, first):
        @pl.when(lax.div(block, U) == part)
        def _():
            each(first, group, lambda t: kv_copy(block, t).start())
        each(first, group, lambda t: qd_copy(block, t).start())

    pltpu.make_async_copy(kv_send.at[head], kv_in.at[u0, d0, f], kv_rs.at[u0]).start()
    pltpu.make_async_copy(qd_send.at[head], qd_in.at[block0, d0, f], qd_rs.at[block0]).start()
    for copy in (kv_copy, qd_copy):
        for t in range(1, group):
            copy(block0, t).start()
    for n in range(1, B):
        @pl.when(block0 >= n)
        def _():
            pl.semaphore_wait(below, 1)

            @pl.when(block0 < B - 1)
            def _():
                knock(below, block0 + 1, d0, f)
            send_block(block0 - n, 0)

        @pl.when(block0 + n < B)
        def _():
            pl.semaphore_wait(above, 1)

            @pl.when(block0 > 0)
            def _():
                knock(above, block0 - 1, d0, f)
            send_block(block0 + n, 0)

    acc[...] = jnp.zeros_like(acc)
    st_send[...] = jnp.zeros_like(st_send)
    if QP > unit:
        lo, hi = tiles[-1]
        for ref, first in ((qaug, unit), (xraw, unit), (qdz, lo + unit), (qdz, hi + unit)):
            ref[:, first:first + QP - unit] = jnp.zeros((B, QP - unit, PAIR), BF)
    for load in loads:
        load.wait()

    lane1 = lax.broadcasted_iota(jnp.int32, (1, PAIR), 1)
    table = [pieces_of(HIDDEN)] + [pieces_of(math.log(n)) for n in range(1, n_slots + 2)]
    marks = []
    for p in range(F):
        seen = jnp.zeros((1, PAIR), F32)
        unseen = jnp.zeros((1, PAIR), F32)
        for g in range(F):
            own = 1 if p == g else 0
            count = own
            for slot in range(n_slots):
                count = count + jnp.where(part_ref[slot, g] == p, 1, 0)
            for e in range(SPLITS):
                here = lane1 == DH + SPLITS * g + e
                unseen = jnp.where(here, table[own][e], unseen)
                for n in range(own, n_slots + 2):
                    seen = jnp.where(here & (count == n), table[n][e], seen)
        marks.append((seen, unseen))

    lane = lax.broadcasted_iota(jnp.int32, (rows, PAIR), 1)
    row = lax.broadcasted_iota(jnp.int32, (rows, PAIR), 0)
    tall = lax.broadcasted_iota(jnp.int32, (unit, PAIR), 1)
    hot = [jnp.where((lane >= DH + SPLITS * g) & (lane < DH + SPLITS * (g + 1)), 1.0, 0.0) for g in range(F)]

    def take_keys(j):
        u = lax.rem(u0 + j, U)
        here = kv_in.at[u]
        remote(here, here, kv_ss.at[0], kv_rs.at[u], (f, w)).wait_recv()
        aug, raw = [], []
        for d in range(per):
            first = ((part * U + u) * per + d) * rows
            for p in range(F):
                both = kv_in[u, d, p].astype(F32)
                extra = jnp.where(row + first >= reg_ref[p], marks[p][0], marks[p][1])
                raw.append(both)
                aug.append(jnp.where(lane < DH, both, extra))
        raw = jnp.concatenate(raw, axis=0)
        kaug[j] = jnp.concatenate(aug, axis=0).astype(BF)
        vz[j] = jnp.where(tall >= DH, raw, 0.0).astype(BF)
        kt[j] = (raw * scale).T[:DH].astype(BF)

    def take_queries(i):
        here = qd_in.at[i]
        remote(here, here, qd_ss.at[0], qd_rs.at[i], (f, w)).wait_recv()
        raw, aug = [], []
        for d in range(per):
            for g in range(F):
                both = qd_in[i, d, g].astype(F32)
                raw.append(both)
                aug.append(jnp.where(lane < DH, both * scale, hot[g]))
        raw = jnp.concatenate(raw, axis=0)
        qaug[i, :unit] = jnp.concatenate(aug, axis=0).astype(BF)
        xraw[i, :unit] = raw.astype(BF)
        for value, side in ((jnp.where(tall < DH, raw * scale, 0.0), 0), (jnp.where(tall >= DH, raw, 0.0), 1)):
            for lo, hi in tiles:
                first, n = 2 * lo + side * (hi - lo), min(hi, unit) - lo
                qdz[i, first:first + n] = value[lo:lo + n].astype(BF)

    def forth(j, i):
        for lo, hi in tiles:
            raw = rdot(kaug[j], qaug[i, lo:hi])
            dprod = rdot(vz[j], xraw[i, lo:hi])
            if j:
                top, total, dsum = top_ref[i, :, lo:hi], total_ref[i, :, lo:hi], dsum_ref[i, :, lo:hi]
            for s in range(n_subs):
                at = slice(s * sub, (s + 1) * sub)
                part_raw = raw[at].reshape(sub // 8, 8, hi - lo)
                part_dp = dprod[at].reshape(sub // 8, 8, hi - lo)
                peak = jnp.max(part_raw, axis=0)
                if j or s:
                    peak = jnp.maximum(top, peak)
                expo = jnp.exp(part_raw - peak[None])
                more, dmore = jnp.sum(expo, axis=0), jnp.sum(expo * part_dp, axis=0)
                if j or s:
                    keep = jnp.exp(top - peak)
                    more, dmore = total * keep + more, dsum * keep + dmore
                top, total, dsum = peak, more, dmore
                sbuf[j, i, at, lo:hi] = expo.reshape(sub, hi - lo)
                dpbuf[j, i, at, lo:hi] = part_dp.reshape(sub, hi - lo)
                tops[j, i, s, :, lo:hi] = peak
            top_ref[i, :, lo:hi] = top
            total_ref[i, :, lo:hi] = total
            dsum_ref[i, :, lo:hi] = dsum

    spans = [(c, c + PAIR) for c in range(0, QP, PAIR)]

    def give(i):
        peak = jnp.max(top_ref[i], axis=0, keepdims=True)
        keep = jnp.exp(top_ref[i] - peak)
        total = jnp.sum(total_ref[i] * keep, axis=0, keepdims=True)
        dsum = jnp.sum(dsum_ref[i] * keep, axis=0, keepdims=True)
        for s, value in enumerate((peak, total, dsum)):
            for n, (lo, hi) in enumerate(spans):
                at = s * len(spans) + n
                st_send[i, at:at + 1] = value[:, lo:hi]
        remote(st_send.at[i], st_in.at[i], st_ss.at[0], st_rs.at[i], (f, other * L + l)).start()

    def meet(i):
        here = st_in.at[i]
        remote(here, here, st_ss.at[0], st_rs.at[i], (f, other * L + l)).wait_recv()
        def row_of(ref, s):
            return jnp.concatenate(
                [ref[i, s * len(spans) + n:s * len(spans) + n + 1] for n in range(len(spans))], axis=1)

        mine, yours = [[row_of(ref, s) for s in range(3)] for ref in (st_send, st_in)]
        peak = jnp.maximum(mine[0], yours[0])
        a, b = jnp.exp(mine[0] - peak), jnp.exp(yours[0] - peak)
        inv = 1.0 / (mine[1] * a + yours[1] * b)
        whole = (8, QP)
        top_ref[i] = jnp.broadcast_to(peak, whole)
        total_ref[i] = jnp.broadcast_to(inv, whole)
        dsum_ref[i] = jnp.broadcast_to((mine[2] * a + yours[2] * b) * inv, whole)

    def back(j, i):
        for lo, hi in tiles:
            probs, dscores = [], []
            for s in range(n_subs):
                at = slice(s * sub, (s + 1) * sub)
                factor = jnp.exp(tops[j, i, s, :, lo:hi] - top_ref[i, :, lo:hi]) * total_ref[i, :, lo:hi]
                prob = sbuf[j, i, at, lo:hi].reshape(sub // 8, 8, hi - lo) * factor[None]
                dprod = dpbuf[j, i, at, lo:hi].reshape(sub // 8, 8, hi - lo)
                dscore = prob * (dprod - dsum_ref[i, :, lo:hi][None])
                probs.append(prob.reshape(sub, hi - lo).astype(BF))
                dscores.append(dscore.reshape(sub, hi - lo).astype(BF))
            for first in range(0, n_subs, n_subs // cuts):
                some = slice(first, first + n_subs // cuts)
                both = [jnp.concatenate(x[some], axis=0) for x in (dscores, probs)]
                added = dot(jnp.concatenate(both, axis=1), qdz[i, 2 * lo:2 * hi])
                at = slice(first * group // n_subs, (first + n_subs // cuts) * group // n_subs)
                acc[j, at] += added.reshape(group // cuts, rows, PAIR)
            more = dot(kt[j], jnp.concatenate(dscores, axis=0))
            if j < U - 1:
                more = dqacc[i, :, lo:hi] + more
            dqacc[i, :, lo:hi] = more

    def dq_copy(i, t):
        d, ff = around(t)
        return remote(dq_send.at[i * group + d * F + ff], dq_in.at[part, head], dq_ss.at[0], dq_rs.at[part], (ff, i * per + d))

    def ship_queries(i, own):
        dqs[...] = jnp.concatenate([dqacc[i], jnp.zeros((DH, QP), F32)], axis=0).T
        for d in range(per):
            for g in range(F):
                base = (d * F + g) * rows
                dq_send[i * group + d * F + g] = jnp.concatenate(
                    [dqs[base:base + half, :DH], dqs[base + rows - half:base + rows, :DH]], axis=1).astype(BF)

        if own:
            pltpu.make_async_copy(dq_send.at[i * group + d0 * F + f], dq_in.at[part, head], dq_rs.at[part]).start()
        for t in range(1 if own else 0, group):
            dq_copy(i, t).start()

    def fin_copy(j, t):
        d, ff = around(t)
        return remote(fin_send.at[j * group + d * F + ff], fin_in.at[head], fin_ss.at[0], fin_rs.at[0],
                      (ff, (part * U + lax.rem(u0 + j, U)) * per + d))

    def ship_keys(j):
        fin_send[j * group:(j + 1) * group] = acc[j].astype(BF)
        if j == 0:
            pltpu.make_async_copy(fin_send.at[d0 * F + f], fin_in.at[head], fin_rs.at[0]).start()
        for t in range(0 if j else 1, group):
            fin_copy(j, t).start()

    def local(n):
        return part * U + lax.rem(u0 + n, U)

    def remote_block(n):
        return other * U + n + part * (U - 1 - 2 * n)

    edge = jnp.where(part == 0, U - 1, 0) == u0
    order = [local(0)]
    for n in range(U - 1):
        order.append(jnp.where(edge, remote_block(n), local(n + 1)))
        order.append(jnp.where(edge, local(n + 1), remote_block(n)))
    order.append(remote_block(U - 1))

    for n, i in enumerate(order):
        if n:
            take_queries(i)
        for j in range(U):
            if n == 0:
                take_keys(j)
                if j == 0:
                    take_queries(i)
            forth(j, i)
        give(i)
    last = [remote_block(U - 1 - n) for n in range(U)]
    for i in last:
        meet(i)
        for j in reversed(range(U)):
            back(j, i)
        ship_queries(i, False)
    mine = [local(n) for n in reversed(range(U))]
    for i in mine:
        meet(i)
    for j in reversed(range(U)):
        for n, i in enumerate(mine):
            back(j, i)
            if j == 0:
                ship_queries(i, n == U - 1)
        ship_keys(j)

    def sent(ref, sem):
        remote(ref, ref, sem.at[0], sem.at[0], (f, w)).wait_send()

    sent(kv_send.at[pl.ds(0, heads - 1)], kv_ss)
    sent(qd_send, qd_ss)
    sent(qd_send.at[pl.ds(0, heads - 1)], qd_ss)
    sent(st_send, st_ss)
    for side in (other, part):
        here = dq_in.at[side]
        remote(here, here, dq_ss.at[0], dq_rs.at[side], (f, w)).wait_recv()
    remote(fin_in, fin_in, fin_ss.at[0], fin_rs.at[0], (f, w)).wait_recv()
    sent(dq_send.at[pl.ds(0, B * group - 1)], dq_ss)
    sent(fin_send.at[pl.ds(0, U * group - 1)], fin_ss)


def both_halves(dq_in, fin_in, dq_out, dk_out, dv_out):
    half, rows, width = dq_in.shape[2], dq_out.shape[1], dq_out.shape[2]
    for j in range(width // PAIR):
        cols = slice(j * PAIR, (j + 1) * PAIR)
        sides = []
        for h in (2 * j, 2 * j + 1):
            got = dq_in[0, h].astype(F32) + dq_in[1, h].astype(F32)
            sides.append(jnp.concatenate([got[:, :DH], got[2 * half - rows:, DH:]], axis=0))
        dq_out[0, :, cols] = jnp.concatenate(sides, axis=1).astype(BF)
        one, two = fin_in[2 * j], fin_in[2 * j + 1]
        dk_out[0, :, cols] = jnp.concatenate([one[:, :DH], two[:, :DH]], axis=1)
        dv_out[0, :, cols] = jnp.concatenate([one[:, DH:], two[:, DH:]], axis=1)


def local_halves(F, W, queries, keys_in, values_in, grad_out, partners, registers):
    _, rows, width = queries.shape
    heads = width // DH
    L = W // 2
    half = ((rows + 1) // 2 + 7) // 8 * 8
    per = next(n for n in range(L, 0, -1) if L % n == 0 and (n == 1 or n * F * rows <= UNIT))
    U = L // per
    unit = per * F * rows
    C = 2 * U
    QP = (unit + PAIR - 1) // PAIR * PAIR
    subs = unit // next(n for n in range(SUB, 0, -8) if unit % n == 0)
    stats = (3 * (QP // PAIR) + 7) // 8 * 8
    vm = lambda *shape: pltpu.VMEM(shape, BF)
    vf = lambda *shape: pltpu.VMEM(shape, F32)
    dma = lambda n: pltpu.SemaphoreType.DMA((n,))
    out = jax.ShapeDtypeStruct((1, rows, width), BF)
    dq_heads, kv_heads = pl.pallas_call(
        functools.partial(halves, F, W),
        out_shape=(jax.ShapeDtypeStruct((2, heads, half, PAIR), BF), jax.ShapeDtypeStruct((heads, rows, PAIR), BF)),
        in_specs=[pl.BlockSpec(memory_space=pl.ANY)] * 6,
        out_specs=(pl.BlockSpec(memory_space=pl.ANY),) * 2,
        scratch_shapes=[
            pltpu.SMEM(partners.T.shape, jnp.int32), pltpu.SMEM(registers.shape, jnp.int32),
            vm(1, rows, width), vm(1, rows, width), vm(1, rows, width), vm(1, rows, width),
            vm(heads, rows, PAIR), vm(heads, rows, PAIR), vm(U, per, F, rows, PAIR), vm(C, per, F, rows, PAIR),
            vm(U, unit, PAIR), vm(U, unit, PAIR), vm(U, DH, unit),
            vm(C, QP, PAIR), vm(C, QP, PAIR), vm(C, 2 * QP, PAIR),
            vf(U, C, unit, QP), vf(U, C, unit, QP), vf(U, per * F, rows, PAIR),
            vf(C, DH, QP), vf(QP, PAIR),
            vf(U, C, subs, 8, QP), vf(C, 8, QP), vf(C, 8, QP), vf(C, 8, QP),
            vf(C, stats, PAIR), vf(C, stats, PAIR),
            vm(heads, rows, PAIR), vm(C * per * F, half, PAIR),
            dma(6), dma(1), dma(U), dma(1), dma(C), dma(1), dma(C), dma(1), dma(2), dma(1), dma(1),
            pltpu.SemaphoreType.REGULAR, pltpu.SemaphoreType.REGULAR,
        ],
        compiler_params=pltpu.CompilerParams(
            collective_id=0, has_side_effects=True, vmem_limit_bytes=40 * 2 ** 20),
    )(*[pltpu.with_memory_space_constraint(x, pltpu.HBM) for x in (
        partners.T, registers, queries, keys_in, values_in, grad_out)])
    return pl.pallas_call(
        both_halves,
        out_shape=(out, out, out),
        in_specs=[pl.BlockSpec(memory_space=pltpu.VMEM)] * 2,
        out_specs=(pl.BlockSpec(memory_space=pltpu.VMEM),) * 3,
        compiler_params=pltpu.CompilerParams(vmem_limit_bytes=8 * 2 ** 20),
    )(dq_heads, kv_heads)


def choose(F, W, queries, *others):
    _, rows, width = queries.shape
    heads = width // DH
    held = 2 * F * W // 2 * rows * F * W * rows * 4
    if W % 2 == 0 and F * W == 2 * heads and SPLITS * F <= DH and held <= 24 * 2 ** 20:
        return local_halves(F, W, queries, *others)
    return local(F, W, queries, *others)


def solution(mesh):
    spec = P("frame", "within", None)
    return jax.shard_map(
        functools.partial(choose, mesh.shape["frame"], mesh.shape["within"]),
        mesh=mesh,
        in_specs=(spec, spec, spec, spec, P(), P()),
        out_specs=(spec, spec, spec),
        check_vma=False,
    )
```

```python
import functools
import math

import jax
import jax.numpy as jnp
import numpy as np
from jax import lax
from jax.experimental import pallas as pl
from jax.experimental.pallas import tpu as pltpu
from jax.sharding import PartitionSpec as P

DH = 64
PAIR = 2 * DH
SPLITS = 3
UNIT = 640
TILE = 256
SUB = 144
HIDDEN = -1e30
BF = jnp.bfloat16
F32 = jnp.float32
MESH = pl.DeviceIdType.MESH


def pieces_of(value):
    left, out = float(value), []
    for _ in range(SPLITS):
        part = float(np.asarray(left, dtype=jnp.bfloat16))
        out.append(part)
        left = left - part if abs(value) < 1e20 else 0.0
    return out


def rdot(a, b):
    return lax.dot_general(a, b, (((1,), (1,)), ((), ())), preferred_element_type=F32)


def dot(a, b):
    return jnp.dot(a, b, preferred_element_type=F32)


def each(lo, hi, do):
    def step(t, carry):
        do(t)
        return carry
    lax.fori_loop(lo, hi, step, 0)


def kernel(F, W, R, QC, inline, part_ref, reg_ref, q_ref, k_ref, v_ref, d_ref, dq_in, fin_in,
           kv_send, qd_send, kv_in, qd_in, kaug, vz, kt, qaug, xraw, qdz, sbuf, dpbuf, acc, dqacc, dqs,
           tops, top_ref, total_ref, dsum_ref,
           red_send, red_in, fin_send, dq_send, own_sem,
           kv_ss, fw_ss, kv_rs, qd_ss, qd_rs, red_ss, red_rs, fin_ss, fin_rs, dq_ss, dq_rs):
    fs = F // R
    hf = F // 2
    rows = q_ref.shape[1]
    width = q_ref.shape[2]
    seq = rows * W
    n_slots = part_ref.shape[0]
    scale = DH ** -0.5
    half = dq_send.shape[2]
    nq = R * seq
    n_chunks = nq // QC
    n_units, per = acc.shape[0], acc.shape[1]
    unit = per * F * rows
    f = lax.axis_index("frame")
    w = lax.axis_index("within")
    c = lax.rem(f, fs)
    a0 = lax.div(f, fs)
    sib = f + 1 - 2 * lax.rem(f, 2)
    head = w * R + a0

    barrier = pltpu.get_barrier_semaphore()

    def ahead(dw):
        return lax.rem(w + W - dw, W)

    def behind(dw):
        return lax.rem(w + dw, W)

    def greet(t):
        pl.semaphore_signal(barrier, inc=1, device_id=(lax.rem(f + 2 * lax.rem(t, hf), F), ahead(lax.div(t, hf))),
                            device_id_type=MESH)

    each(1, hf * W, greet)
    for dc in range(1, fs, 2):
        pl.semaphore_signal(barrier, inc=1, device_id=(a0 * fs + lax.rem(c + dc, fs), w), device_id_type=MESH)

    for first, second, out in ((q_ref, d_ref, qd_send), (k_ref, v_ref, kv_send)):
        for j in range(width // PAIR):
            cols = slice(j * PAIR, (j + 1) * PAIR)
            one = first[0, :, cols]
            two = second[0, :, cols]
            out[2 * j] = jnp.concatenate([one[:, :DH], two[:, :DH]], axis=1)
            out[2 * j + 1] = jnp.concatenate([one[:, DH:], two[:, DH:]], axis=1)
    kv_in[f, w] = kv_send[head]
    qd_in[a0, w] = qd_send[head]

    pl.semaphore_wait(barrier, hf * W - 1 + fs // 2)

    def kv_copy(t):
        ff = lax.rem(f + 2 * lax.rem(t, hf), F)
        ww = ahead(lax.div(t, hf))
        return pltpu.make_async_remote_copy(
            src_ref=kv_send.at[ww * R + lax.div(ff, fs)], dst_ref=kv_in.at[f, w],
            send_sem=kv_ss.at[t], recv_sem=kv_rs.at[f * W + w],
            device_id=(ff, ww), device_id_type=MESH)

    def pass_on(origin, t):
        ff = lax.rem(origin + F - 2 * lax.rem(t, hf), F)
        ww = behind(lax.div(t, hf))
        return pltpu.make_async_remote_copy(
            src_ref=kv_in.at[ff, ww], dst_ref=kv_in.at[ff, ww],
            send_sem=fw_ss.at[t], recv_sem=kv_rs.at[ff * W + ww],
            device_id=(sib, w), device_id_type=MESH)

    def qd_copy(t):
        aa, ww = lax.rem(a0 + lax.rem(t, R), R), ahead(lax.div(t, R))
        return pltpu.make_async_remote_copy(
            src_ref=qd_send.at[ww * R + aa], dst_ref=qd_in.at[a0, w],
            send_sem=qd_ss.at[t], recv_sem=qd_rs.at[a0 * W + w],
            device_id=(aa * fs + c, ww), device_id_type=MESH)

    def arrival(t, buffer, send, recv, index, source):
        return pltpu.make_async_remote_copy(
            src_ref=buffer.at[index], dst_ref=buffer.at[index], send_sem=send.at[t], recv_sem=recv,
            device_id=source, device_id_type=MESH)

    def qd_arrival(t):
        aa, ww = lax.rem(a0 + R - lax.rem(t, R), R), behind(lax.div(t, R))
        return arrival(t, qd_in, qd_ss, qd_rs.at[aa * W + ww], (aa, ww), (aa * fs + c, ww))

    def head_arrival(t, buffer, send, recv):
        aa, ww = lax.rem(a0 + R - lax.rem(t, R), R), ahead(lax.div(t, R))
        return arrival(t, buffer, send, recv.at[ww * R + aa], (ww * R + aa,), (aa * fs + c, ww))

    each(1, R * W, lambda t: qd_copy(t).start())
    pass_on(f, 0).start()
    each(1, hf * W, lambda t: kv_copy(t).start())

    acc[...] = jnp.zeros_like(acc)
    dqacc[...] = jnp.zeros_like(dqacc)

    def relay(t):
        move = pass_on(f, t)
        move.wait_recv()
        move.start()

    lane1 = lax.broadcasted_iota(jnp.int32, (1, PAIR), 1)
    table = [pieces_of(HIDDEN)] + [pieces_of(math.log(n)) for n in range(1, n_slots + 2)]
    marks = []
    for p in range(F):
        seen = jnp.zeros((1, PAIR), F32)
        unseen = jnp.zeros((1, PAIR), F32)
        for gi in range(R):
            g = c + fs * gi
            own = jnp.where(p == g, 1, 0)
            count = own
            for slot in range(n_slots):
                count = count + jnp.where(part_ref[slot, g] == p, 1, 0)
            for e in range(SPLITS):
                here = lane1 == DH + SPLITS * gi + e
                for n in range(n_slots + 2):
                    if n < 2:
                        unseen = jnp.where(here & (own == n), table[n][e], unseen)
                    seen = jnp.where(here & (count == n), table[n][e], seen)
        marks.append((seen, unseen))

    lane = lax.broadcasted_iota(jnp.int32, (rows, PAIR), 1)
    row = lax.broadcasted_iota(jnp.int32, (rows, PAIR), 0)

    def prepare(u):
        aug, raw = [], []
        for d in range(per):
            ww = behind(u * per + d)
            for p in range(F):
                both = kv_in[p, ww].astype(F32)
                extra = jnp.where(row + ww * rows >= reg_ref[p], marks[p][0], marks[p][1])
                raw.append(both)
                aug.append(jnp.where(lane < DH, both, extra))
        raw = jnp.concatenate(raw, axis=0)
        keep = lax.broadcasted_iota(jnp.int32, (unit, PAIR), 1) >= DH
        kaug[u] = jnp.concatenate(aug, axis=0).astype(BF)
        vz[u] = jnp.where(keep, raw, 0.0).astype(BF)
        kt[u] = (raw * scale).T[:DH].astype(BF)

    def direct(u):
        each(max(u * per * hf, 1), (u + 1) * per * hf, relay)

    def settle(u):
        each(u * per * hf, (u + 1) * per * hf, lambda t: pass_on(sib, t).wait_recv())
        prepare(u)

    def rows_of(i):
        return pl.ds(pl.multiple_of(i * QC, QC), QC)

    def begin(b):
        top_ref[b] = jnp.full_like(top_ref[b], -3e38)
        total_ref[b] = jnp.zeros_like(total_ref[b])
        dsum_ref[b] = jnp.zeros_like(dsum_ref[b])

    def forth(u, i, b):
        at = rows_of(i)
        raw = rdot(kaug[u], qaug[at])
        old = top_ref[b]
        top = jnp.maximum(old, jnp.max(raw, axis=0, keepdims=True))
        keep = jnp.exp(old - top)
        expo = jnp.exp(raw - top)
        dprod = rdot(vz[u], xraw[at])
        sbuf[u, b] = expo
        dpbuf[u, b] = dprod
        tops[u, b] = top
        top_ref[b] = top
        total_ref[b] = total_ref[b] * keep + jnp.sum(expo, axis=0, keepdims=True)
        dsum_ref[b] = dsum_ref[b] * keep + jnp.sum(expo * dprod, axis=0, keepdims=True)

    def back(u, i, b):
        inv = 1.0 / total_ref[b]
        factor = jnp.exp(tops[u, b] - top_ref[b]) * inv
        prob = sbuf[u, b] * factor
        dscore = (prob * (dpbuf[u, b] - dsum_ref[b] * inv)).astype(BF)
        added = dot(jnp.concatenate([dscore, prob.astype(BF)], axis=1), qdz[i])
        acc[u] += added.reshape(per, F, rows, PAIR)
        dqacc[i] += dot(kt[u], dscore)

    def own_copy(block, buffer, n):
        return pltpu.make_async_copy(block, buffer.at[head], own_sem.at[n])

    def red_copy(u, dc):
        return pltpu.make_async_remote_copy(
            src_ref=red_send.at[u, dc - 1], dst_ref=red_in.at[u, dc - 1],
            send_sem=red_ss.at[u * (fs - 1) + dc - 1], recv_sem=red_rs.at[u * (fs - 1) + dc - 1],
            device_id=(a0 * fs + lax.rem(c + dc, fs), w), device_id_type=MESH)

    def ship_part(u):
        for dc in range(1, fs):
            for gi in range(R):
                red_send[u, dc - 1, gi] = acc[u, :, lax.rem(c + dc, fs) + fs * gi].astype(BF)
            red_copy(u, dc).start()

    def fin_copy(t):
        dw = lax.div(t, R)
        aa, ww = lax.rem(a0 + lax.rem(t, R), R), behind(dw)
        return pltpu.make_async_remote_copy(
            src_ref=fin_send.at[lax.div(dw, per), aa, lax.rem(dw, per)], dst_ref=fin_in.at[head],
            send_sem=fin_ss.at[t], recv_sem=fin_rs.at[head],
            device_id=(aa * fs + c, ww), device_id_type=MESH)

    def ship_home(u):
        for dc in range(1, fs):
            red_copy(u, dc).wait_recv()
        for gi in range(R):
            whole = acc[u, :, c + fs * gi]
            for dc in range(1, fs):
                whole = whole + red_in[u, dc - 1, gi].astype(F32)
            fin_send[u, gi] = whole.astype(BF)
        if u == 0:
            own_copy(fin_send.at[0, a0, 0], fin_in, 0).start()
        each(max(u * per * R, 1), (u + 1) * per * R, lambda t: fin_copy(t).start())

    def take_queries():
        each(1, R * W, lambda t: qd_arrival(t).wait_recv())
        wide = lax.broadcasted_iota(jnp.int32, (nq, PAIR), 1)
        tall = lax.broadcasted_iota(jnp.int32, (nq, PAIR), 0)
        both = qd_in[...].astype(F32).reshape(nq, PAIR)
        mark = jnp.zeros((nq, PAIR), F32)
        for gi in range(R):
            mine = (tall >= gi * seq) & (tall < (gi + 1) * seq)
            mark = jnp.where(mine & (wide >= DH + SPLITS * gi) & (wide < DH + SPLITS * (gi + 1)), 1.0, mark)
        scaled = both * scale
        qaug[...] = jnp.where(wide < DH, scaled, mark).astype(BF)
        xraw[...] = both.astype(BF)
        qdz[:, :QC] = jnp.where(wide < DH, scaled, 0.0).astype(BF).reshape(n_chunks, QC, PAIR)
        qdz[:, QC:] = jnp.where(wide >= DH, both, 0.0).astype(BF).reshape(n_chunks, QC, PAIR)

    take_queries()
    if inline:
        each(0, n_chunks, begin)
        direct(0)
        for u in range(n_units):
            settle(u)
            forth(u, 0, 0)
            if u + 1 < n_units:
                direct(u + 1)
            each(1, n_chunks, lambda i: forth(u, i, i))
        for u in range(n_units):
            back(u, 0, 0)
            if u:
                ship_home(u - 1)
            each(1, n_chunks, lambda i: back(u, i, i))
            ship_part(u)
    else:
        for u in range(n_units):
            direct(u)
        for u in range(n_units):
            settle(u)

        def block(i):
            begin(0)
            each(0, n_units, lambda u: forth(u, i, 0))
            each(0, n_units, lambda u: back(u, i, 0))

        each(0, n_chunks, block)
        for u in range(n_units):
            ship_part(u)
        for u in range(n_units - 1):
            ship_home(u)

    def dq_copy(t):
        aa, ww = lax.rem(a0 + lax.rem(t, R), R), behind(lax.div(t, R))
        return pltpu.make_async_remote_copy(
            src_ref=dq_send.at[aa, ww], dst_ref=dq_in.at[head],
            send_sem=dq_ss.at[t], recv_sem=dq_rs.at[head],
            device_id=(aa * fs + c, ww), device_id_type=MESH)

    for i in range(n_chunks):
        dqs[i * QC:(i + 1) * QC] = jnp.concatenate([dqacc[i], jnp.zeros((DH, QC), F32)], axis=0).T
    for gi in range(R):
        for ww in range(W):
            base = gi * seq + ww * rows
            dq_send[gi, ww] = jnp.concatenate(
                [dqs[base:base + half, :DH], dqs[base + rows - half:base + rows, :DH]], axis=1).astype(BF)
    own_copy(dq_send.at[a0, w], dq_in, 1).start()
    each(1, R * W, lambda t: dq_copy(t).start())
    ship_home(n_units - 1)

    each(1, R * W, lambda t: head_arrival(t, dq_in, dq_ss, dq_rs).wait_recv())
    each(1, R * W, lambda t: head_arrival(t, fin_in, fin_ss, fin_rs).wait_recv())
    each(1, hf * W, lambda t: kv_copy(t).wait_send())
    each(0, hf * W, lambda t: pass_on(f, t).wait_send())
    each(1, R * W, lambda t: qd_copy(t).wait_send())
    own_copy(fin_send.at[0, a0, 0], fin_in, 0).wait()
    own_copy(dq_send.at[a0, w], dq_in, 1).wait()
    each(1, R * W, lambda t: dq_copy(t).wait_send())
    each(1, R * W, lambda t: fin_copy(t).wait_send())
    for u in range(n_units):
        for dc in range(1, fs):
            red_copy(u, dc).wait_send()


def tokens_again(dq_in, fin_in, dq_out, dk_out, dv_out):
    half, rows, width = dq_in.shape[1], dq_out.shape[1], dq_out.shape[2]
    for j in range(width // PAIR):
        cols = slice(j * PAIR, (j + 1) * PAIR)
        sides = []
        for h in (2 * j, 2 * j + 1):
            got = dq_in[h].astype(F32)
            sides.append(jnp.concatenate([got[:, :DH], got[2 * half - rows:, DH:]], axis=0))
        dq_out[0, :, cols] = jnp.concatenate(sides, axis=1).astype(BF)

    for j in range(width // PAIR):
        cols = slice(j * PAIR, (j + 1) * PAIR)
        one, two = fin_in[2 * j], fin_in[2 * j + 1]
        dk_out[0, :, cols] = jnp.concatenate([one[:, :DH], two[:, :DH]], axis=1)
        dv_out[0, :, cols] = jnp.concatenate([one[:, DH:], two[:, DH:]], axis=1)


def local(F, W, queries, keys_in, values_in, grad_out, partners, registers):
    _, rows, width = queries.shape
    heads = width // DH
    R = heads // W
    fs = F // R
    seq = rows * W
    nq = R * seq
    half = ((rows + 1) // 2 + 7) // 8 * 8
    inline = F * seq * nq * 8 <= 24 * 2 ** 20
    QC = next(b for b in ((576, 384, 128) if inline else (128,)) if nq % b == 0)
    held = nq // QC if inline else 1
    per = next(n for n in range(W, 0, -1) if W % n == 0 and (n == 1 or n * F * rows <= UNIT))
    units = W // per
    unit = per * F * rows
    vm = lambda *shape: pltpu.VMEM(shape, BF)
    vf = lambda *shape: pltpu.VMEM(shape, F32)
    dma = lambda n: pltpu.SemaphoreType.DMA((n,))
    out = jax.ShapeDtypeStruct((1, rows, width), BF)
    dq_heads, kv_heads = pl.pallas_call(
        functools.partial(kernel, F, W, R, QC, inline),
        out_shape=(jax.ShapeDtypeStruct((heads, half, PAIR), BF), jax.ShapeDtypeStruct((heads, rows, PAIR), BF)),
        in_specs=[pl.BlockSpec(memory_space=pltpu.SMEM)] * 2 + [pl.BlockSpec(memory_space=pltpu.VMEM)] * 4,
        out_specs=(pl.BlockSpec(memory_space=pl.ANY),) * 2,
        scratch_shapes=[
            vm(heads, rows, PAIR), vm(heads, rows, PAIR),
            vm(F, W, rows, PAIR), vm(R, W, rows, PAIR),
            vm(units, unit, PAIR), vm(units, unit, PAIR), vm(units, DH, unit),
            vm(nq, PAIR), vm(nq, PAIR), vm(nq // QC, 2 * QC, PAIR),
            vf(units, held, unit, QC), vf(units, held, unit, QC), vf(units, per, F, rows, PAIR),
            vf(nq // QC, DH, QC), vf(nq, PAIR),
            vf(units, held, 1, QC), vf(held, 1, QC), vf(held, 1, QC), vf(held, 1, QC),
            vm(units, fs - 1, R, per, rows, PAIR), vm(units, fs - 1, R, per, rows, PAIR),
            vm(units, R, per, rows, PAIR), vm(R, W, half, PAIR), dma(2),
            dma(F // 2 * W), dma(F // 2 * W), dma(F * W), dma(R * W), dma(R * W),
            dma(units * (fs - 1)), dma(units * (fs - 1)), dma(R * W), dma(heads), dma(R * W), dma(heads),
        ],
        compiler_params=pltpu.CompilerParams(
            collective_id=0, has_side_effects=True, vmem_limit_bytes=60 * 2 ** 20),
    )(partners.T, registers, queries, keys_in, values_in, grad_out)
    return pl.pallas_call(
        tokens_again,
        out_shape=(out, out, out),
        in_specs=[pl.BlockSpec(memory_space=pltpu.VMEM)] * 2,
        out_specs=(pl.BlockSpec(memory_space=pltpu.VMEM),) * 3,
    )(dq_heads, kv_heads)


def halves(F, W, part_hbm, reg_hbm, q_hbm, k_hbm, v_hbm, d_hbm, dq_in, fin_in,
           part_ref, reg_ref, q_ref, k_ref, v_ref, d_ref, kv_send, qd_send, kv_in, qd_in,
           kaug, vz, kt, qaug, xraw, qdz, sbuf, dpbuf, acc, dqacc, dqs,
           tops, top_ref, total_ref, dsum_ref, st_send, st_in, fin_send, dq_send,
           in_sem, kv_ss, kv_rs, qd_ss, qd_rs, st_ss, st_rs, dq_ss, dq_rs, fin_ss, fin_rs, below, above):
    rows, width = q_ref.shape[1], q_ref.shape[2]
    n_slots = part_ref.shape[0]
    U, per = kv_in.shape[0], kv_in.shape[1]
    L = U * per
    B = 2 * U
    heads = F * L
    group = per * F
    unit = group * rows
    QP = qaug.shape[1]
    tiles = [(c, min(c + TILE, QP)) for c in range(0, QP, TILE)]
    n_subs = tops.shape[2]
    sub = unit // n_subs
    cuts = 2 if n_subs % 2 == 0 and group % 2 == 0 else 1
    scale = DH ** -0.5
    half = dq_send.shape[1]
    f = lax.axis_index("frame")
    w = lax.axis_index("within")
    block0 = lax.div(w, per)
    d0 = lax.rem(w, per)
    part = lax.div(block0, U)
    other = 1 - part
    u0 = lax.rem(block0, U)
    l = u0 * per + d0
    head = f * L + l

    barrier = pltpu.get_barrier_semaphore()

    def around(t):
        return lax.rem(d0 + lax.div(t, F), per), lax.rem(f + lax.rem(t, F), F)

    def knock(sem, block, d, ff):
        pl.semaphore_signal(sem, inc=1, device_id=(ff, block * per + d), device_id_type=MESH)

    def greet(t):
        d, ff = around(group - t)
        knock(barrier, block0, d, ff)

    loads = [pltpu.make_async_copy(src, dst, in_sem.at[n]) for n, (src, dst) in enumerate(
        ((k_hbm, k_ref), (v_hbm, v_ref), (q_hbm, q_ref), (d_hbm, d_ref), (part_hbm, part_ref), (reg_hbm, reg_ref)))]
    for load in loads:
        load.start()

    @pl.when(block0 > 0)
    def _():
        knock(barrier, block0 - 1, d0, f)

    @pl.when(block0 < B - 1)
    def _():
        knock(barrier, block0 + 1, d0, f)

    each(1, group, greet)
    def pack(first, second, out):
        for load in (loads.pop(0), loads.pop(0)):
            load.wait()
        for j in range(width // PAIR):
            cols = slice(j * PAIR, (j + 1) * PAIR)
            one = first[0, :, cols]
            two = second[0, :, cols]
            out[2 * j] = jnp.concatenate([one[:, :DH], two[:, :DH]], axis=1)
            out[2 * j + 1] = jnp.concatenate([one[:, DH:], two[:, DH:]], axis=1)

    pack(k_ref, v_ref, kv_send)
    pl.semaphore_wait(barrier, group - 1 + jnp.where(block0 > 0, 1, 0) + jnp.where(block0 < B - 1, 1, 0))

    @pl.when(block0 > 0)
    def _():
        knock(above, block0 - 1, d0, f)

    @pl.when(block0 < B - 1)
    def _():
        knock(below, block0 + 1, d0, f)

    pack(q_ref, d_ref, qd_send)

    def remote(src, dst, ss, rs, device):
        return pltpu.make_async_remote_copy(src_ref=src, dst_ref=dst, send_sem=ss, recv_sem=rs,
                                            device_id=device, device_id_type=MESH)

    def head_at(block, d, ff):
        return ff * L + lax.rem(block, U) * per + d

    def kv_copy(block, t):
        d, ff = around(t)
        return remote(kv_send.at[head_at(block, d, ff)], kv_in.at[u0, d0, f], kv_ss.at[0], kv_rs.at[u0],
                      (ff, block * per + d))

    def qd_copy(block, t):
        d, ff = around(t)
        return remote(qd_send.at[head_at(block, d, ff)], qd_in.at[block0, d0, f], qd_ss.at[0], qd_rs.at[block0],
                      (ff, block * per + d))

    def send_block(block, first):
        @pl.when(lax.div(block, U) == part)
        def _():
            each(first, group, lambda t: kv_copy(block, t).start())
        each(first, group, lambda t: qd_copy(block, t).start())

    pltpu.make_async_copy(kv_send.at[head], kv_in.at[u0, d0, f], kv_rs.at[u0]).start()
    pltpu.make_async_copy(qd_send.at[head], qd_in.at[block0, d0, f], qd_rs.at[block0]).start()
    for copy in (kv_copy, qd_copy):
        for t in range(1, group):
            copy(block0, t).start()
    for n in range(1, B):
        @pl.when(block0 >= n)
        def _():
            pl.semaphore_wait(below, 1)

            @pl.when(block0 < B - 1)
            def _():
                knock(below, block0 + 1, d0, f)
            send_block(block0 - n, 0)

        @pl.when(block0 + n < B)
        def _():
            pl.semaphore_wait(above, 1)

            @pl.when(block0 > 0)
            def _():
                knock(above, block0 - 1, d0, f)
            send_block(block0 + n, 0)

    acc[...] = jnp.zeros_like(acc)
    st_send[...] = jnp.zeros_like(st_send)
    if QP > unit:
        lo, hi = tiles[-1]
        for ref, first in ((qaug, unit), (xraw, unit), (qdz, lo + unit), (qdz, hi + unit)):
            ref[:, first:first + QP - unit] = jnp.zeros((B, QP - unit, PAIR), BF)
    for load in loads:
        load.wait()

    lane1 = lax.broadcasted_iota(jnp.int32, (1, PAIR), 1)
    table = [pieces_of(HIDDEN)] + [pieces_of(math.log(n)) for n in range(1, n_slots + 2)]
    marks = []
    for p in range(F):
        seen = jnp.zeros((1, PAIR), F32)
        unseen = jnp.zeros((1, PAIR), F32)
        for g in range(F):
            own = 1 if p == g else 0
            count = own
            for slot in range(n_slots):
                count = count + jnp.where(part_ref[slot, g] == p, 1, 0)
            for e in range(SPLITS):
                here = lane1 == DH + SPLITS * g + e
                unseen = jnp.where(here, table[own][e], unseen)
                for n in range(own, n_slots + 2):
                    seen = jnp.where(here & (count == n), table[n][e], seen)
        marks.append((seen, unseen))

    lane = lax.broadcasted_iota(jnp.int32, (rows, PAIR), 1)
    row = lax.broadcasted_iota(jnp.int32, (rows, PAIR), 0)
    tall = lax.broadcasted_iota(jnp.int32, (unit, PAIR), 1)
    hot = [jnp.where((lane >= DH + SPLITS * g) & (lane < DH + SPLITS * (g + 1)), 1.0, 0.0) for g in range(F)]

    def take_keys(j):
        u = lax.rem(u0 + j, U)
        here = kv_in.at[u]
        remote(here, here, kv_ss.at[0], kv_rs.at[u], (f, w)).wait_recv()
        aug, raw = [], []
        for d in range(per):
            first = ((part * U + u) * per + d) * rows
            for p in range(F):
                both = kv_in[u, d, p].astype(F32)
                extra = jnp.where(row + first >= reg_ref[p], marks[p][0], marks[p][1])
                raw.append(both)
                aug.append(jnp.where(lane < DH, both, extra))
        raw = jnp.concatenate(raw, axis=0)
        kaug[j] = jnp.concatenate(aug, axis=0).astype(BF)
        vz[j] = jnp.where(tall >= DH, raw, 0.0).astype(BF)
        kt[j] = (raw * scale).T[:DH].astype(BF)

    def take_queries(i):
        here = qd_in.at[i]
        remote(here, here, qd_ss.at[0], qd_rs.at[i], (f, w)).wait_recv()
        raw, aug = [], []
        for d in range(per):
            for g in range(F):
                both = qd_in[i, d, g].astype(F32)
                raw.append(both)
                aug.append(jnp.where(lane < DH, both * scale, hot[g]))
        raw = jnp.concatenate(raw, axis=0)
        qaug[i, :unit] = jnp.concatenate(aug, axis=0).astype(BF)
        xraw[i, :unit] = raw.astype(BF)
        for value, side in ((jnp.where(tall < DH, raw * scale, 0.0), 0), (jnp.where(tall >= DH, raw, 0.0), 1)):
            for lo, hi in tiles:
                first, n = 2 * lo + side * (hi - lo), min(hi, unit) - lo
                qdz[i, first:first + n] = value[lo:lo + n].astype(BF)

    def forth(j, i):
        for lo, hi in tiles:
            raw = rdot(kaug[j], qaug[i, lo:hi])
            dprod = rdot(vz[j], xraw[i, lo:hi])
            if j:
                top, total, dsum = top_ref[i, :, lo:hi], total_ref[i, :, lo:hi], dsum_ref[i, :, lo:hi]
            for s in range(n_subs):
                at = slice(s * sub, (s + 1) * sub)
                part_raw = raw[at].reshape(sub // 8, 8, hi - lo)
                part_dp = dprod[at].reshape(sub // 8, 8, hi - lo)
                peak = jnp.max(part_raw, axis=0)
                if j or s:
                    peak = jnp.maximum(top, peak)
                expo = jnp.exp(part_raw - peak[None])
                more, dmore = jnp.sum(expo, axis=0), jnp.sum(expo * part_dp, axis=0)
                if j or s:
                    keep = jnp.exp(top - peak)
                    more, dmore = total * keep + more, dsum * keep + dmore
                top, total, dsum = peak, more, dmore
                sbuf[j, i, at, lo:hi] = expo.reshape(sub, hi - lo)
                dpbuf[j, i, at, lo:hi] = part_dp.reshape(sub, hi - lo)
                tops[j, i, s, :, lo:hi] = peak
            top_ref[i, :, lo:hi] = top
            total_ref[i, :, lo:hi] = total
            dsum_ref[i, :, lo:hi] = dsum

    spans = [(c, c + PAIR) for c in range(0, QP, PAIR)]

    def give(i):
        peak = jnp.max(top_ref[i], axis=0, keepdims=True)
        keep = jnp.exp(top_ref[i] - peak)
        total = jnp.sum(total_ref[i] * keep, axis=0, keepdims=True)
        dsum = jnp.sum(dsum_ref[i] * keep, axis=0, keepdims=True)
        for s, value in enumerate((peak, total, dsum)):
            for n, (lo, hi) in enumerate(spans):
                at = s * len(spans) + n
                st_send[i, at:at + 1] = value[:, lo:hi]
        remote(st_send.at[i], st_in.at[i], st_ss.at[0], st_rs.at[i], (f, other * L + l)).start()

    def meet(i):
        here = st_in.at[i]
        remote(here, here, st_ss.at[0], st_rs.at[i], (f, other * L + l)).wait_recv()
        def row_of(ref, s):
            return jnp.concatenate(
                [ref[i, s * len(spans) + n:s * len(spans) + n + 1] for n in range(len(spans))], axis=1)

        mine, yours = [[row_of(ref, s) for s in range(3)] for ref in (st_send, st_in)]
        peak = jnp.maximum(mine[0], yours[0])
        a, b = jnp.exp(mine[0] - peak), jnp.exp(yours[0] - peak)
        inv = 1.0 / (mine[1] * a + yours[1] * b)
        whole = (8, QP)
        top_ref[i] = jnp.broadcast_to(peak, whole)
        total_ref[i] = jnp.broadcast_to(inv, whole)
        dsum_ref[i] = jnp.broadcast_to((mine[2] * a + yours[2] * b) * inv, whole)

    def back(j, i):
        for lo, hi in tiles:
            probs, dscores = [], []
            for s in range(n_subs):
                at = slice(s * sub, (s + 1) * sub)
                factor = jnp.exp(tops[j, i, s, :, lo:hi] - top_ref[i, :, lo:hi]) * total_ref[i, :, lo:hi]
                prob = sbuf[j, i, at, lo:hi].reshape(sub // 8, 8, hi - lo) * factor[None]
                dprod = dpbuf[j, i, at, lo:hi].reshape(sub // 8, 8, hi - lo)
                dscore = prob * (dprod - dsum_ref[i, :, lo:hi][None])
                probs.append(prob.reshape(sub, hi - lo).astype(BF))
                dscores.append(dscore.reshape(sub, hi - lo).astype(BF))
            for first in range(0, n_subs, n_subs // cuts):
                some = slice(first, first + n_subs // cuts)
                both = [jnp.concatenate(x[some], axis=0) for x in (dscores, probs)]
                added = dot(jnp.concatenate(both, axis=1), qdz[i, 2 * lo:2 * hi])
                at = slice(first * group // n_subs, (first + n_subs // cuts) * group // n_subs)
                acc[j, at] += added.reshape(group // cuts, rows, PAIR)
            more = dot(kt[j], jnp.concatenate(dscores, axis=0))
            if j < U - 1:
                more = dqacc[i, :, lo:hi] + more
            dqacc[i, :, lo:hi] = more

    def dq_copy(i, t):
        d, ff = around(t)
        return remote(dq_send.at[i * group + d * F + ff], dq_in.at[part, head], dq_ss.at[0], dq_rs.at[part], (ff, i * per + d))

    def ship_queries(i, own):
        dqs[...] = jnp.concatenate([dqacc[i], jnp.zeros((DH, QP), F32)], axis=0).T
        for d in range(per):
            for g in range(F):
                base = (d * F + g) * rows
                dq_send[i * group + d * F + g] = jnp.concatenate(
                    [dqs[base:base + half, :DH], dqs[base + rows - half:base + rows, :DH]], axis=1).astype(BF)

        if own:
            pltpu.make_async_copy(dq_send.at[i * group + d0 * F + f], dq_in.at[part, head], dq_rs.at[part]).start()
        for t in range(1 if own else 0, group):
            dq_copy(i, t).start()

    def fin_copy(j, t):
        d, ff = around(t)
        return remote(fin_send.at[j * group + d * F + ff], fin_in.at[head], fin_ss.at[0], fin_rs.at[0],
                      (ff, (part * U + lax.rem(u0 + j, U)) * per + d))

    def ship_keys(j):
        fin_send[j * group:(j + 1) * group] = acc[j].astype(BF)
        if j == 0:
            pltpu.make_async_copy(fin_send.at[d0 * F + f], fin_in.at[head], fin_rs.at[0]).start()
        for t in range(0 if j else 1, group):
            fin_copy(j, t).start()

    def local(n):
        return part * U + lax.rem(u0 + n, U)

    def remote_block(n):
        return other * U + n + part * (U - 1 - 2 * n)

    edge = jnp.where(part == 0, U - 1, 0) == u0
    order = [local(0)]
    for n in range(U - 1):
        order.append(jnp.where(edge, remote_block(n), local(n + 1)))
        order.append(jnp.where(edge, local(n + 1), remote_block(n)))
    order.append(remote_block(U - 1))

    for n, i in enumerate(order):
        if n:
            take_queries(i)
        for j in range(U):
            if n == 0:
                take_keys(j)
                if j == 0:
                    take_queries(i)
            forth(j, i)
        give(i)
    last = [remote_block(U - 1 - n) for n in range(U)]
    i = last[0]
    meet(i)
    for j in reversed(range(U)):
        back(j, i)
    ship_queries(i, False)
    rest = last[1:] + [local(n) for n in reversed(range(U))]
    for j in reversed(range(U)):
        for n, i in enumerate(rest):
            if j == U - 1:
                meet(i)
            back(j, i)
            if j == 0:
                ship_queries(i, n == len(rest) - 1)
        ship_keys(j)

    def sent(ref, sem):
        remote(ref, ref, sem.at[0], sem.at[0], (f, w)).wait_send()

    sent(kv_send.at[pl.ds(0, heads - 1)], kv_ss)
    sent(qd_send, qd_ss)
    sent(qd_send.at[pl.ds(0, heads - 1)], qd_ss)
    sent(st_send, st_ss)
    for side in (other, part):
        here = dq_in.at[side]
        remote(here, here, dq_ss.at[0], dq_rs.at[side], (f, w)).wait_recv()
    remote(fin_in, fin_in, fin_ss.at[0], fin_rs.at[0], (f, w)).wait_recv()
    sent(dq_send.at[pl.ds(0, B * group - 1)], dq_ss)
    sent(fin_send.at[pl.ds(0, U * group - 1)], fin_ss)


def both_halves(dq_in, fin_in, dq_out, dk_out, dv_out):
    half, rows, width = dq_in.shape[2], dq_out.shape[1], dq_out.shape[2]
    for j in range(width // PAIR):
        cols = slice(j * PAIR, (j + 1) * PAIR)
        sides = []
        for h in (2 * j, 2 * j + 1):
            got = dq_in[0, h].astype(F32) + dq_in[1, h].astype(F32)
            sides.append(jnp.concatenate([got[:, :DH], got[2 * half - rows:, DH:]], axis=0))
        dq_out[0, :, cols] = jnp.concatenate(sides, axis=1).astype(BF)
        one, two = fin_in[2 * j], fin_in[2 * j + 1]
        dk_out[0, :, cols] = jnp.concatenate([one[:, :DH], two[:, :DH]], axis=1)
        dv_out[0, :, cols] = jnp.concatenate([one[:, DH:], two[:, DH:]], axis=1)


def local_halves(F, W, queries, keys_in, values_in, grad_out, partners, registers):
    _, rows, width = queries.shape
    heads = width // DH
    L = W // 2
    half = ((rows + 1) // 2 + 7) // 8 * 8
    per = next(n for n in range(L, 0, -1) if L % n == 0 and (n == 1 or n * F * rows <= UNIT))
    U = L // per
    unit = per * F * rows
    C = 2 * U
    QP = (unit + PAIR - 1) // PAIR * PAIR
    subs = unit // next(n for n in range(SUB, 0, -8) if unit % n == 0)
    stats = (3 * (QP // PAIR) + 7) // 8 * 8
    vm = lambda *shape: pltpu.VMEM(shape, BF)
    vf = lambda *shape: pltpu.VMEM(shape, F32)
    dma = lambda n: pltpu.SemaphoreType.DMA((n,))
    out = jax.ShapeDtypeStruct((1, rows, width), BF)
    dq_heads, kv_heads = pl.pallas_call(
        functools.partial(halves, F, W),
        out_shape=(jax.ShapeDtypeStruct((2, heads, half, PAIR), BF), jax.ShapeDtypeStruct((heads, rows, PAIR), BF)),
        in_specs=[pl.BlockSpec(memory_space=pl.ANY)] * 6,
        out_specs=(pl.BlockSpec(memory_space=pl.ANY),) * 2,
        scratch_shapes=[
            pltpu.SMEM(partners.T.shape, jnp.int32), pltpu.SMEM(registers.shape, jnp.int32),
            vm(1, rows, width), vm(1, rows, width), vm(1, rows, width), vm(1, rows, width),
            vm(heads, rows, PAIR), vm(heads, rows, PAIR), vm(U, per, F, rows, PAIR), vm(C, per, F, rows, PAIR),
            vm(U, unit, PAIR), vm(U, unit, PAIR), vm(U, DH, unit),
            vm(C, QP, PAIR), vm(C, QP, PAIR), vm(C, 2 * QP, PAIR),
            vf(U, C, unit, QP), vf(U, C, unit, QP), vf(U, per * F, rows, PAIR),
            vf(C, DH, QP), vf(QP, PAIR),
            vf(U, C, subs, 8, QP), vf(C, 8, QP), vf(C, 8, QP), vf(C, 8, QP),
            vf(C, stats, PAIR), vf(C, stats, PAIR),
            vm(heads, rows, PAIR), vm(C * per * F, half, PAIR),
            dma(6), dma(1), dma(U), dma(1), dma(C), dma(1), dma(C), dma(1), dma(2), dma(1), dma(1),
            pltpu.SemaphoreType.REGULAR, pltpu.SemaphoreType.REGULAR,
        ],
        compiler_params=pltpu.CompilerParams(
            collective_id=0, has_side_effects=True, vmem_limit_bytes=40 * 2 ** 20),
    )(*[pltpu.with_memory_space_constraint(x, pltpu.HBM) for x in (
        partners.T, registers, queries, keys_in, values_in, grad_out)])
    return pl.pallas_call(
        both_halves,
        out_shape=(out, out, out),
        in_specs=[pl.BlockSpec(memory_space=pltpu.VMEM)] * 2,
        out_specs=(pl.BlockSpec(memory_space=pltpu.VMEM),) * 3,
        compiler_params=pltpu.CompilerParams(vmem_limit_bytes=8 * 2 ** 20),
    )(dq_heads, kv_heads)


def choose(F, W, queries, *others):
    _, rows, width = queries.shape
    heads = width // DH
    held = 2 * F * W // 2 * rows * F * W * rows * 4
    if W % 2 == 0 and F * W == 2 * heads and SPLITS * F <= DH and held <= 24 * 2 ** 20:
        return local_halves(F, W, queries, *others)
    return local(F, W, queries, *others)


def solution(mesh):
    spec = P("frame", "within", None)
    return jax.shard_map(
        functools.partial(choose, mesh.shape["frame"], mesh.shape["within"]),
        mesh=mesh,
        in_specs=(spec, spec, spec, spec, P(), P()),
        out_specs=(spec, spec, spec),
        check_vma=False,
    )
```
